32 devices in a mesh: dp: 4 (over y, core), fsdp: 8 (over z, x).
Axes of the slice: x: 2, y: 2, z: 4, core: 2. Of those that a mesh axis runs over, the one named last changes fastest.
Arguments:
- tokens: bfloat16 [65536, 512], P(('dp', 'fsdp')), may hold values from -6 to 6
- lengths: int32 [256], replicated, may hold values from 0 to 2048, as said below
- assignment: int32 [256], replicated, may hold values from 0 to 31, as said below
- weights: bfloat16 [2097152], P(('dp', 'fsdp')), may hold values from -1.5 to 1.5
- vectors: bfloat16 [5120], P(('dp', 'fsdp')), may hold values from -1.6 to 1.8
- cotangent: bfloat16 [65536, 512], P(('dp', 'fsdp')), may hold values from -6 to 6
Outputs:
- layer_output: bfloat16 [65536, 512], P(('dp', 'fsdp'))
- grad_tokens: float32 [65536, 512], P(('dp', 'fsdp'))
- grad_weights: float32 [2097152], P(('dp', 'fsdp'))
- grad_vectors: float32 [5120], P(('dp', 'fsdp'))
The draws below stay inside these ranges and needn't reach their ends.
Inputs may be any that keep to these rules, and one draw needn't show every extreme that they name: The datasets that assignment gives one device have lengths adding up to exactly 2048; some dataset has 2048 samples. `assignment`: every device holds exactly 8 datasets.
All inputs are finite; a program needn't handle non-finite values.
Results may differ from the reference program's by a relative error of at most 0.012.
The reference program's roundings to bfloat16 on the way count: a program that leaves them out, or rounds other values in their place, can miss the bound.
Values may be sent and summed in bfloat16 or wider, within the bound.
No kernel may reach another device: no remote copies, remote signals or barrier semaphores. Data moves between devices by JAX's collectives and lax.ppermute only.
A program may use at most 256 MiB of HBM per device.

```python
import math
import jax
import jax.numpy as jnp
from jax import lax

D = 512
HEADS = 4
HEAD_DIM = 128
FF = 1024
TOK_DEV = 2048
SETS_DEV = 8
TOKENS = 65536
SETS = 256
WEIGHT_COUNT = 2097152
VECTOR_COUNT = 5120
N_DP = 4
N_FSDP = 8


def dataset_layout(key):
    base = jax.random.fold_in(key, 7)
    device_count = SETS // SETS_DEV
    shift_key, cut_key, big_key, order_key = jax.random.split(base, 4)
    shifts = jax.random.randint(shift_key, (device_count,), 0, 4)
    windows = jnp.right_shift(jnp.full((device_count,), TOK_DEV, jnp.int32), shifts)
    chosen = jax.random.randint(big_key, (), 0, device_count)
    windows = jnp.where(jnp.arange(device_count) == chosen, 0, windows)
    raw_cuts = jax.random.randint(cut_key, (device_count, SETS_DEV - 1), 0, TOK_DEV + 1)
    cuts = TOK_DEV - windows[:, None] + raw_cuts % (windows[:, None] + 1)
    cuts = jnp.sort(cuts, axis=1)
    bounds = jnp.concatenate([jnp.zeros((device_count, 1), jnp.int32), cuts.astype(jnp.int32), jnp.full((device_count, 1), TOK_DEV, jnp.int32)], axis=1)
    slot_lengths = (bounds[:, 1:] - bounds[:, :-1]).reshape(-1)
    order = jax.random.permutation(order_key, SETS)
    set_lengths = jnp.zeros((SETS,), jnp.int32).at[order].set(slot_lengths)
    owners = jnp.zeros((SETS,), jnp.int32).at[order].set(jnp.arange(SETS, dtype=jnp.int32) // SETS_DEV)
    return (set_lengths, owners)


def draw_lengths(key, part):
    return dataset_layout(key)[0]


def draw_assignment(key, part):
    return dataset_layout(key)[1]


def draw_weights(key, part):
    device_count = SETS // SETS_DEV
    square = D * D // device_count
    rect = D * FF // device_count
    block_width = WEIGHT_COUNT // device_count
    column = jnp.arange(WEIGHT_COUNT) % block_width
    spread = jnp.where(column < 3 * square, 1.0 / math.sqrt(D), jnp.where(column < 4 * square, 1.0 / math.sqrt(8.0), jnp.where(column < 4 * square + rect, 1.0 / math.sqrt(D), 1.0 / math.sqrt(FF))))
    noise = jax.random.truncated_normal(key, -4.0, 4.0, (WEIGHT_COUNT,), jnp.float32)
    return (noise * spread.astype(jnp.float32)).astype(jnp.bfloat16)


def draw_vectors(key, part):
    index = jnp.arange(VECTOR_COUNT)
    group = jnp.minimum(index // D, 8)
    spreads = jnp.array([0.1, 0.1, 0.3, 0.3, 0.25, 0.3, 0.25, 0.3, 0.5], jnp.float32)
    centers = jnp.array([0.0, 0.0, 0.0, 0.0, 1.0, 0.0, 1.0, 0.0, 0.0], jnp.float32)
    noise = jax.random.truncated_normal(key, -3.0, 3.0, (VECTOR_COUNT,), jnp.float32)
    return (centers[group] + noise * spreads[group]).astype(jnp.bfloat16)


def block_levels(own_key, extent, cuts, smallest, top_value):
    gain = 1.0
    for dim, blocks in cuts:
        draws = jax.random.uniform(jax.random.fold_in(jax.random.fold_in(own_key, 6), dim), (blocks,), jnp.float32, smallest / len(cuts), top_value / len(cuts))
        gain = gain * jnp.repeat(jnp.exp(draws), extent[dim] // blocks).reshape((-1,) + (1,) * (len(extent) - 1 - dim))
    return gain


def gaussian(own_key, extent, deviation, most, cuts=(), kind=jnp.bfloat16):
    values = deviation * jax.random.normal(own_key, extent, jnp.float32)
    if cuts:
        values = values * block_levels(own_key, extent, cuts, -0.22, 0.18)
    return jnp.clip(values, -most, most).astype(kind)


def setup_inputs(seed: int = 0) -> dict:
    keys = jax.random.split(jax.random.key(seed), 7)
    return {
        "tokens": gaussian(keys[0], (TOKENS, D), 1.0, 6.0, ((0, 32),)),
        "lengths": draw_lengths(jax.random.fold_in(keys[6], 71), 0),
        "assignment": draw_assignment(jax.random.fold_in(keys[6], 71), 0),
        "weights": draw_weights(jax.random.fold_in(keys[6], 71), 0),
        "vectors": draw_vectors(jax.random.fold_in(keys[6], 71), 0),
        "cotangent": gaussian(keys[5], (TOKENS, D), 1.0, 6.0, ((0, 32),)),
    }


@jax.custom_vjp
def low(v):
    return lax.optimization_barrier(v.astype(jnp.bfloat16)).astype(jnp.float32)

@jax.custom_vjp
def low_back(v):
    return v

def low_keep(v):
    return (low(v), None)

def low_pass(kept, grad):
    return (grad,)

def back_keep(v):
    return (v, None)

def back_low(kept, grad):
    return (low(grad),)
low.defvjp(low_keep, low_pass)
low_back.defvjp(back_keep, back_low)
norm_eps = 1e-05
highest = lax.Precision.HIGHEST

def dataset_labels(lengths, assignment, owner, row_count):
    owned = assignment == owner
    dataset_ends = jnp.cumsum(jnp.where(owned, lengths, 0), dtype=jnp.int32)
    places = jnp.arange(row_count, dtype=jnp.int32)
    passed = owned[None, :] & (dataset_ends[None, :] <= places[:, None])
    return lax.optimization_barrier(jnp.sum(passed.astype(jnp.int32), axis=1, dtype=jnp.int32))

def unpack_params(flat_weights, flat_vectors, model_width, hidden_width, device_count):
    square = model_width * model_width
    rect = model_width * hidden_width
    widths = [3 * square // device_count, square // device_count, rect // device_count, rect // device_count]
    blocks = flat_weights.reshape(device_count, -1)
    starts = [0, widths[0], widths[0] + widths[1], widths[0] + widths[1] + widths[2]]
    pieces = [blocks[:, starts[k]:starts[k] + widths[k]].reshape(-1) for k in range(4)]
    qkv_weight = pieces[0].reshape(3, model_width, model_width)
    attn_weight = pieces[1].reshape(model_width, model_width)
    in_weight = pieces[2].reshape(model_width, hidden_width)
    out_weight = pieces[3].reshape(hidden_width, model_width)
    bias_rows = flat_vectors[:8 * model_width].reshape(8, model_width)
    hidden_bias = flat_vectors[8 * model_width:]
    return (qkv_weight, attn_weight, in_weight, out_weight, bias_rows, hidden_bias)

def layer_norm(summed):
    row_mean = lax.optimization_barrier(jnp.mean(summed, axis=-1, keepdims=True))
    centered = summed - row_mean
    variance = lax.optimization_barrier(jnp.mean(centered * centered, axis=-1, keepdims=True))
    return centered * lax.rsqrt(variance + norm_eps)

def attend_block(pieces):
    queries, key_heads, values, labels = pieces
    scores = low_back(jnp.einsum('qhd,khd->hqk', queries, key_heads, precision=highest))
    allowed = labels[:, None] == labels[None, :]
    scores = jnp.where(allowed[None], scores, -1e+30)
    attn_probs = low(jax.nn.softmax(scores, axis=-1))
    return jnp.einsum('hqk,khd->qhd', attn_probs, values, precision=highest)

def forward(inputs, flat_weights, flat_vectors, labels):
    device_count = N_DP * N_FSDP
    qkv_weight, attn_weight, in_weight, out_weight, bias_rows, hidden_bias = unpack_params(flat_weights, flat_vectors, D, FF, device_count)
    score_scale = 1.0 / math.sqrt(HEAD_DIM)
    projected = jnp.einsum('td,cde->cte', inputs, qkv_weight, precision=highest)
    queries = low(low_back((projected[0] + bias_rows[0]) * score_scale))
    key_heads = low(low_back(projected[1]))
    values = low(low_back(projected[2] + bias_rows[1]))

    def by_device(array):
        return array.reshape(device_count, TOK_DEV, HEADS, HEAD_DIM)
    attended = lax.map(jax.checkpoint(attend_block), (by_device(queries), by_device(key_heads), by_device(values), labels))
    attended = low(low_back(attended.reshape(device_count * TOK_DEV, D)))
    branch = low_back(jnp.dot(attended, attn_weight, precision=highest) + bias_rows[2])
    hidden = layer_norm(inputs + branch) * bias_rows[4] + bias_rows[5]
    pre_act = low_back(jnp.dot(low(hidden), in_weight, precision=highest) + hidden_bias)
    activated = low(jax.nn.gelu(pre_act, approximate=False))
    ffn_result = low_back(jnp.dot(activated, out_weight, precision=highest) + bias_rows[3])
    return layer_norm(hidden + ffn_result) * bias_rows[6] + bias_rows[7]

def reference(tokens, lengths, assignment, weights, vectors, cotangent):
    device_count = N_DP * N_FSDP

    def labels_of(owner):
        return dataset_labels(lengths, assignment, owner, TOK_DEV)
    labels = lax.map(labels_of, jnp.arange(device_count, dtype=jnp.int32))

    def whole(inputs, flat_weights, flat_vectors):
        return forward(inputs, flat_weights, flat_vectors, labels)
    result, pullback = jax.vjp(whole, tokens.astype(jnp.float32), weights.astype(jnp.float32), vectors.astype(jnp.float32))
    grad_inputs, grad_flat_weights, grad_flat_vectors = pullback(cotangent.astype(jnp.float32))
    return (result.astype(jnp.bfloat16), grad_inputs, grad_flat_weights, grad_flat_vectors)
```

```python
import functools
import math

import jax
import jax.numpy as jnp
from jax import lax
from jax.experimental import pallas as pl
from jax.experimental.pallas import tpu as pltpu
from jax.sharding import PartitionSpec as P

HEADS = 4
HEAD_DIM = 128
FF = 1024
AXES = ("dp", "fsdp")
NORM_EPS = 1e-05
BLOCKS = 32
QKV_ROWS = 48
Q_ROWS = 4 * QKV_ROWS + 16
R_ROWS = 320
FAR = -1e30
f32 = jnp.float32
bf16 = jnp.bfloat16
NT = (((1,), (1,)), ((), ()))
NN = (((1,), (0,)), ((), ()))
TN = (((0,), (0,)), ((), ()))
TT = (((0,), (1,)), ((), ()))
VMEM_BYTES = 60 << 20


def dot(a, b, dims):
    return lax.dot_general(a, b, dims, preferred_element_type=f32)


def params():
    return pltpu.CompilerParams(vmem_limit_bytes=VMEM_BYTES)


def whole(shape):
    return pl.BlockSpec(shape, lambda *_: (0,) * len(shape))


def scalar_spec():
    return pl.BlockSpec(memory_space=pltpu.SMEM)


def owner_of(place, me, order):
    mask = 0
    for bit, step in enumerate(order):
        mask = mask + ((place >> bit) & 1) * step
    return jnp.bitwise_xor(me, mask)


def split3(value):
    high = value.astype(bf16)
    rest = value - high.astype(f32)
    middle = rest.astype(bf16)
    low = (rest - middle.astype(f32)).astype(bf16)
    return high, middle, low


PANELS = ((0, 48, 4), (192, 16, 4), (256, 16, 8), (384, 32, 4))


def pack_kernel(flat, vec, q_out, r_out, wide):
    wide[...] = flat[...].astype(f32)
    parts = []
    for start, rows, count in PANELS:
        for j in range(count):
            parts.append(wide[pl.ds(start + j, rows, stride=count), :].astype(bf16))
    q_out[0:192, :] = jnp.concatenate(parts[:4], axis=0)
    q_out[192:208, :] = vec[...]
    r_out[...] = jnp.concatenate(parts[4:], axis=0)


def pack(flat, vec):
    return pl.pallas_call(
        pack_kernel,
        out_shape=[
            jax.ShapeDtypeStruct((Q_ROWS, 128), bf16),
            jax.ShapeDtypeStruct((R_ROWS, 128), bf16),
        ],
        scratch_shapes=[pltpu.VMEM((512, 128), f32)],
        name="pack",
    )(flat, vec)


def project_kernel(
    order, vec_width, vec_count, me_ref, ends, tokens, first, second, qkv, keys_extra, query_extra, vec_out, weight, vec
):
    step = pl.program_id(0)
    rows = tokens.shape[0]
    me = me_ref[0]

    @pl.when(step == 0)
    def _():
        half = BLOCKS // 2
        for base, ref in ((0, first), (half, second)):

            def place(i, _, base=base, ref=ref):
                d = owner_of(base + i, me, order)
                for j in range(4):
                    weight[pl.ds(pl.multiple_of(d * QKV_ROWS, 16), QKV_ROWS), 128 * j : 128 * (j + 1)] = ref[
                        pl.ds(pl.multiple_of(i * Q_ROWS + QKV_ROWS * j, 16), QKV_ROWS), :
                    ]
                return 0

            lax.fori_loop(0, half, place, 0)
        vec[...] = jnp.zeros_like(vec)
        for base, ref in ((0, first), (half, second)):

            def add(i, _, base=base, ref=ref):
                d = owner_of(base + i, me, order)
                row = (d * vec_width) // 128
                piece = ref[pl.ds(pl.multiple_of(i * Q_ROWS + 4 * QKV_ROWS, 16), 16), :].astype(f32)
                vec[pl.ds(row, 2), :] = vec[pl.ds(row, 2), :] + piece[0:2, :]
                return 0

            lax.fori_loop(0, half, add, 0)
        vec_out[...] = vec[...]

    x = tokens[...]
    scale = 1.0 / math.sqrt(HEAD_DIM)
    query_bias = jnp.concatenate([vec[j : j + 1, :] for j in range(4)], axis=1)
    value_bias = jnp.concatenate([vec[4 + j : 5 + j, :] for j in range(4)], axis=1)
    queries = ((dot(x, weight[0:512, :], NN) + query_bias) * scale).astype(bf16)
    key_heads = dot(x, weight[512:1024, :], NN).astype(bf16)
    values = (dot(x, weight[1024:1536, :], NN) + value_bias).astype(bf16)
    qkv[:, 0:512] = queries
    qkv[:, 512:1024] = key_heads
    qkv[:, 1024:1536] = values
    places = step * rows + lax.broadcasted_iota(jnp.int32, (rows, ends.shape[1]), 0)
    label = jnp.sum((ends[...] <= places).astype(f32), axis=1, keepdims=True)
    lane = lax.broadcasted_iota(jnp.int32, (rows, 128), 1)
    same = lane.astype(f32) == label
    keys_extra[...] = jnp.where(lane < 8, jnp.where(same, 1.0, 0.0), jnp.where(lane < 12, 1.0, 0.0)).astype(bf16)
    apart = jnp.where((lane < 8) & jnp.logical_not(same), FAR, 0.0)
    product = queries.astype(f32) * key_heads.astype(f32)
    for h in range(HEADS):
        own = jnp.sum(product[:, 128 * h : 128 * (h + 1)], axis=1, keepdims=True)
        query_extra[h] = jnp.where(lane == 8, -own, apart).astype(bf16)


def project(me, ends, tokens, first, second, order, vec_width, vec_count, rows=512):
    count = tokens.shape[0]
    sets = ends.shape[1]
    return pl.pallas_call(
        functools.partial(project_kernel, order, vec_width, vec_count),
        grid=(count // rows,),
        in_specs=[
            scalar_spec(),
            whole((1, sets)),
            pl.BlockSpec((rows, 512), lambda i: (i, 0)),
            whole(first.shape),
            whole(second.shape),
        ],
        out_specs=[
            pl.BlockSpec((rows, 1536), lambda i: (i, 0)),
            pl.BlockSpec((rows, 128), lambda i: (i, 0)),
            pl.BlockSpec((HEADS, rows, 128), lambda i: (0, i, 0)),
            whole((48, 128)),
        ],
        out_shape=[
            jax.ShapeDtypeStruct((count, 1536), bf16),
            jax.ShapeDtypeStruct((count, 128), bf16),
            jax.ShapeDtypeStruct((HEADS, count, 128), bf16),
            jax.ShapeDtypeStruct((48, 128), f32),
        ],
        scratch_shapes=[pltpu.VMEM((1536, 512), bf16), pltpu.VMEM((48, 128), f32)],
        compiler_params=params(),
        name="project",
    )(me, ends, tokens, first, second)


def attend_kernel(q, k, v, query_extra, keys_extra, attended, query_extra_out, total, mixed, peak):
    rows = q.shape[0]
    left = jnp.concatenate([k[...], keys_extra[...]], axis=1)
    right = jnp.concatenate([q[...], query_extra[0]], axis=1)
    scores = dot(left, right, NT)
    weights = jnp.exp(scores)
    total[...] = jnp.sum(weights, axis=0, keepdims=True)
    mixed[...] = dot(v[...], weights.astype(bf16), TN)
    peak[...] = jnp.zeros_like(peak)
    good = jnp.where((total[...] > 1e-20) & (total[...] < 1e30), 0.0, 1.0)

    @pl.when(jnp.sum(good) > 0.0)
    def _():
        again = dot(left, right, NT)
        top = jnp.max(again, axis=0, keepdims=True)
        safe = jnp.exp(again - top)
        total[...] = jnp.sum(safe, axis=0, keepdims=True)
        mixed[...] = dot(v[...], safe.astype(bf16), TN)
        peak[...] = top

    attended[...] = (mixed[...] * (1.0 / total[...])).T.astype(bf16)
    offset = jnp.broadcast_to(peak[...] + jnp.log(total[...]), (128, rows)).T
    high, middle, low = split3(-offset)
    lane = lax.broadcasted_iota(jnp.int32, (rows, 128), 1)
    extra = query_extra[0].astype(f32)
    extra = jnp.where(lane == 9, high.astype(f32), extra)
    extra = jnp.where(lane == 10, middle.astype(f32), extra)
    extra = jnp.where(lane == 11, low.astype(f32), extra)
    query_extra_out[0] = extra.astype(bf16)


def attend(qkv, query_extra, keys_extra, rows=1024):
    count = qkv.shape[0]
    return pl.pallas_call(
        attend_kernel,
        grid=(HEADS, count // rows),
        in_specs=[
            pl.BlockSpec((rows, 128), lambda h, i: (i, h)),
            pl.BlockSpec((count, 128), lambda h, i: (0, HEADS + h)),
            pl.BlockSpec((count, 128), lambda h, i: (0, 2 * HEADS + h)),
            pl.BlockSpec((1, rows, 128), lambda h, i: (h, i, 0)),
            pl.BlockSpec((count, 128), lambda h, i: (0, 0)),
        ],
        out_specs=[
            pl.BlockSpec((rows, 128), lambda h, i: (i, h)),
            pl.BlockSpec((1, rows, 128), lambda h, i: (h, i, 0)),
        ],
        out_shape=[
            jax.ShapeDtypeStruct((count, 512), bf16),
            jax.ShapeDtypeStruct((HEADS, count, 128), bf16),
        ],
        scratch_shapes=[pltpu.VMEM((1, rows), f32), pltpu.VMEM((128, rows), f32), pltpu.VMEM((1, rows), f32)],
        compiler_params=params(),
        name="attend",
    )(qkv, qkv, qkv, query_extra, keys_extra)


def mean_row(value):
    return jnp.sum(value, axis=1, keepdims=True) * (1.0 / value.shape[1])


def norm_rows(summed):
    centered = summed - mean_row(summed)
    inverse = lax.rsqrt(mean_row(centered * centered) + NORM_EPS)
    return centered * inverse, inverse


def norm_back(grad, normed, inverse):
    return inverse * (grad - mean_row(grad) - normed * mean_row(grad * normed))


def fold8(value):
    return jnp.sum(value.reshape(value.shape[0] // 8, 8, value.shape[1]), axis=0)


def middle_kernel(
    order_in,
    order_out,
    sub,
    me_ref,
    tokens,
    attended,
    cotangent,
    vec,
    first,
    second,
    layer_output,
    grad_first_out,
    grad_attended_out,
    grad_extra,
    keep,
    send,
    vec_out,
    attn_weight,
    in_weight,
    out_weight,
    grad_attn,
    grad_in,
    grad_out,
    sums,
    hidden_sum,
):
    step = pl.program_id(0)
    me = me_ref[0]
    half = BLOCKS // 2

    @pl.when(step == 0)
    def _():
        for base, ref in ((0, first), (half, second)):

            def place(i, _, base=base, ref=ref):
                d = owner_of(base + i, me, order_in)
                start = i * R_ROWS
                a_row = pl.multiple_of(d * 16, 16)
                o_row = pl.multiple_of(d * 32, 16)
                for j in range(4):
                    attn_weight[pl.ds(a_row, 16), 128 * j : 128 * (j + 1)] = ref[
                        pl.ds(pl.multiple_of(start + 16 * j, 16), 16), :
                    ]
                for j in range(8):
                    in_weight[pl.ds(a_row, 16), 128 * j : 128 * (j + 1)] = ref[
                        pl.ds(pl.multiple_of(start + 64 + 16 * j, 16), 16), :
                    ]
                for j in range(4):
                    out_weight[pl.ds(o_row, 32), 128 * j : 128 * (j + 1)] = ref[
                        pl.ds(pl.multiple_of(start + 192 + 32 * j, 16), 32), :
                    ]
                return 0

            lax.fori_loop(0, half, place, 0)
        grad_attn[...] = jnp.zeros_like(grad_attn)
        grad_in[...] = jnp.zeros_like(grad_in)
        grad_out[...] = jnp.zeros_like(grad_out)
        sums[...] = jnp.zeros_like(sums)
        hidden_sum[...] = jnp.zeros_like(hidden_sum)

    def row_of(index):
        return jnp.concatenate([vec[4 * index + j : 4 * index + j + 1, :] for j in range(4)], axis=1)

    attn_bias, ffn_bias, gain_one, shift_one, gain_two, shift_two = [row_of(i) for i in range(2, 8)]
    hidden_bias = jnp.concatenate([vec[32 + j : 33 + j, :] for j in range(8)], axis=1)

    def chain(s):
        sl = slice(s * sub, (s + 1) * sub)
        att = attended[sl, :]
        branch = dot(att, attn_weight[...], NN) + attn_bias
        yield
        normed_one, inverse_one = norm_rows(tokens[sl, :].astype(f32) + branch)
        hidden = normed_one * gain_one + shift_one
        hidden_low = hidden.astype(bf16)
        yield
        pre_act = dot(hidden_low, in_weight[...], NN) + hidden_bias
        yield
        cdf = 0.5 * (1.0 + lax.erf(pre_act * 0.7071067811865476))
        density = jnp.exp(-0.5 * pre_act * pre_act) * 0.3989422804014327
        activated = (pre_act * cdf).astype(bf16)
        slope = cdf + pre_act * density
        yield
        ffn_result = dot(activated, out_weight[...], NN) + ffn_bias
        yield
        normed_two, inverse_two = norm_rows(hidden + ffn_result)
        layer_output[sl, :] = (normed_two * gain_two + shift_two).astype(bf16)
        grad_result = cotangent[sl, :].astype(f32)
        sums[4] += fold8(grad_result * normed_two)
        sums[5] += fold8(grad_result)
        grad_second = norm_back(grad_result * gain_two, normed_two, inverse_two)
        grad_ffn = grad_second.astype(bf16)
        sums[1] += fold8(grad_ffn.astype(f32))
        yield
        grad_activated = dot(grad_ffn, out_weight[...], NT)
        grad_out[...] += dot(activated, grad_ffn, TN)
        yield
        grad_pre = (grad_activated * slope).astype(bf16)
        hidden_sum[...] += fold8(grad_pre.astype(f32))
        yield
        grad_hidden = grad_second + dot(grad_pre, in_weight[...], NT)
        grad_in[...] += dot(hidden_low, grad_pre, TN)
        yield
        sums[2] += fold8(grad_hidden * normed_one)
        sums[3] += fold8(grad_hidden)
        grad_first = norm_back(grad_hidden * gain_one, normed_one, inverse_one)
        grad_first_out[sl, :] = grad_first
        grad_branch = grad_first.astype(bf16)
        sums[0] += fold8(grad_branch.astype(f32))
        yield
        grad_attended = dot(grad_branch, attn_weight[...], NT).astype(bf16)
        grad_attn[...] += dot(att, grad_branch, TN)
        yield
        grad_attended_out[sl, :] = grad_attended
        product = grad_attended.astype(f32) * att.astype(f32)
        lane = lax.broadcasted_iota(jnp.int32, (sub, 128), 1)
        for h in range(HEADS):
            centre = jnp.sum(product[:, 128 * h : 128 * (h + 1)], axis=1, keepdims=True)
            high, middle, low = split3(-centre)
            extra = jnp.where(lane == 0, high.astype(f32), 0.0)
            extra = jnp.where(lane == 1, middle.astype(f32), extra)
            extra = jnp.where(lane == 2, low.astype(f32), extra)
            grad_extra[h, sl, :] = extra.astype(bf16)
        yield

    chains = [chain(s) for s in range(tokens.shape[0] // sub)]
    started = 0
    live = []
    while started < len(chains) or live:
        if started < len(chains):
            live.append(chains[started])
            started += 1
        remaining = []
        for c in live:
            try:
                next(c)
                remaining.append(c)
            except StopIteration:
                pass
        live = remaining

    @pl.when(step == pl.num_programs(0) - 1)
    def _():
        for base, ref in ((0, keep), (half, send)):

            def place(i, _, base=base, ref=ref):
                d = owner_of(base + i, me, order_out)
                start = i * R_ROWS
                a_row = pl.multiple_of(d * 16, 16)
                o_row = pl.multiple_of(d * 32, 16)
                for j in range(4):
                    ref[pl.ds(pl.multiple_of(start + 16 * j, 16), 16), :] = grad_attn[
                        pl.ds(a_row, 16), 128 * j : 128 * (j + 1)
                    ].astype(bf16)
                for j in range(8):
                    ref[pl.ds(pl.multiple_of(start + 64 + 16 * j, 16), 16), :] = grad_in[
                        pl.ds(a_row, 16), 128 * j : 128 * (j + 1)
                    ].astype(bf16)
                for j in range(4):
                    ref[pl.ds(pl.multiple_of(start + 192 + 32 * j, 16), 32), :] = grad_out[
                        pl.ds(o_row, 32), 128 * j : 128 * (j + 1)
                    ].astype(bf16)
                return 0

            lax.fori_loop(0, half, place, 0)
        vec_out[...] = jnp.zeros_like(vec_out)
        for i in range(6):
            row = jnp.sum(sums[i], axis=0, keepdims=True)
            for j in range(4):
                vec_out[8 + 4 * i + j : 9 + 4 * i + j, :] = row[:, 128 * j : 128 * (j + 1)]
        row = jnp.sum(hidden_sum[...], axis=0, keepdims=True)
        for j in range(8):
            vec_out[32 + j : 33 + j, :] = row[:, 128 * j : 128 * (j + 1)]


def middle(me, tokens, attended, cotangent, vec, first, second, order_in, order_out, rows=512, sub=256):
    count = tokens.shape[0]
    by_row = pl.BlockSpec((rows, 512), lambda i: (i, 0))
    half_rows = BLOCKS // 2 * R_ROWS
    return pl.pallas_call(
        functools.partial(middle_kernel, order_in, order_out, sub),
        grid=(count // rows,),
        in_specs=[
            scalar_spec(),
            by_row,
            by_row,
            by_row,
            whole((48, 128)),
            whole(first.shape),
            whole(second.shape),
        ],
        out_specs=[
            by_row,
            by_row,
            by_row,
            pl.BlockSpec((HEADS, rows, 128), lambda i: (0, i, 0)),
            whole((half_rows, 128)),
            whole((half_rows, 128)),
            whole((48, 128)),
        ],
        out_shape=[
            jax.ShapeDtypeStruct((count, 512), bf16),
            jax.ShapeDtypeStruct((count, 512), f32),
            jax.ShapeDtypeStruct((count, 512), bf16),
            jax.ShapeDtypeStruct((HEADS, count, 128), bf16),
            jax.ShapeDtypeStruct((half_rows, 128), bf16),
            jax.ShapeDtypeStruct((half_rows, 128), bf16),
            jax.ShapeDtypeStruct((48, 128), f32),
        ],
        scratch_shapes=[
            pltpu.VMEM((512, 512), bf16),
            pltpu.VMEM((512, FF), bf16),
            pltpu.VMEM((FF, 512), bf16),
            pltpu.VMEM((512, 512), f32),
            pltpu.VMEM((512, FF), f32),
            pltpu.VMEM((FF, 512), f32),
            pltpu.VMEM((6, 8, 512), f32),
            pltpu.VMEM((8, FF), f32),
        ],
        compiler_params=params(),
        name="middle",
    )(me, tokens, attended, cotangent, vec, first, second)


def attend_back_kernel(
    q, k, v, grad, query_extra, keys_extra, grad_extra, grad_query, grad_keys, grad_values, acc
):
    step = pl.program_id(1)
    width = k.shape[0]
    lane = lax.broadcasted_iota(jnp.int32, (width, 128), 1)
    ones = jnp.where(lane < 3, 1.0, 0.0).astype(bf16)
    scores = dot(
        jnp.concatenate([q[...], query_extra[0]], axis=1),
        jnp.concatenate([k[...], keys_extra[...]], axis=1),
        NT,
    )
    centred = dot(
        jnp.concatenate([grad[...], grad_extra[0]], axis=1), jnp.concatenate([v[...], ones], axis=1), NT
    )
    probs = jnp.exp(scores)
    probs_low = probs.astype(bf16)
    grad_scores = (probs * centred).astype(bf16)
    grad_values[...] = dot(grad[...], probs_low, TN).astype(bf16)
    grad_keys[...] = dot(q[...], grad_scores, TN).astype(bf16)
    part = dot(grad_scores, k[...], NN)

    @pl.when(step == 0)
    def _():
        acc[...] = part

    @pl.when(step > 0)
    def _():
        acc[...] += part

    @pl.when(step == pl.num_programs(1) - 1)
    def _():
        grad_query[...] = acc[...].astype(bf16)


def attend_back(qkv, grad_attended, query_extra, keys_extra, grad_extra, width=512):
    count = qkv.shape[0]
    return pl.pallas_call(
        attend_back_kernel,
        grid=(HEADS, count // width),
        in_specs=[
            pl.BlockSpec((count, 128), lambda h, i: (0, h)),
            pl.BlockSpec((width, 128), lambda h, i: (i, HEADS + h)),
            pl.BlockSpec((width, 128), lambda h, i: (i, 2 * HEADS + h)),
            pl.BlockSpec((count, 128), lambda h, i: (0, h)),
            pl.BlockSpec((1, count, 128), lambda h, i: (h, 0, 0)),
            pl.BlockSpec((width, 128), lambda h, i: (i, 0)),
            pl.BlockSpec((1, count, 128), lambda h, i: (h, 0, 0)),
        ],
        out_specs=[
            pl.BlockSpec((count, 128), lambda h, i: (0, h)),
            pl.BlockSpec((128, width), lambda h, i: (h, i)),
            pl.BlockSpec((128, width), lambda h, i: (h, i)),
        ],
        out_shape=[
            jax.ShapeDtypeStruct((count, 512), bf16),
            jax.ShapeDtypeStruct((512, count), bf16),
            jax.ShapeDtypeStruct((512, count), bf16),
        ],
        scratch_shapes=[pltpu.VMEM((count, 128), f32)],
        compiler_params=params(),
        name="attend_back",
    )(qkv, qkv, qkv, grad_attended, query_extra, keys_extra, grad_extra)


def weight_grad_kernel(
    order, vec_width, me_ref, tokens, grad_query, grad_keys, grad_values, vec_in, keep, send, vec, grad_weight
):
    me = me_ref[0]
    half = BLOCKS // 2
    scale = 1.0 / math.sqrt(HEAD_DIM)
    x = tokens[...]
    ones = jnp.ones((8, x.shape[0]), bf16)
    vec[...] = vec_in[...]
    for h in range(HEADS):
        cols = slice(128 * h, 128 * (h + 1))
        gq = grad_query[:, cols]
        gk = grad_keys[cols, :]
        gv = grad_values[cols, :]
        grad_weight[0:512, cols] = dot(gq, x, TN).T * scale
        grad_weight[512:1024, cols] = dot(gk, x, NN).T
        grad_weight[1024:1536, cols] = dot(gv, x, NN).T
        vec[h : h + 1, :] = dot(ones, gq, NN)[0:1] * scale
        vec[4 + h : 5 + h, :] = dot(ones, gv, NT)[0:1]
    for base, ref in ((0, keep), (half, send)):

        def place(i, _, base=base, ref=ref):
            d = owner_of(base + i, me, order)
            start = i * Q_ROWS
            row = pl.multiple_of(d * QKV_ROWS, 16)
            for j in range(4):
                ref[pl.ds(pl.multiple_of(start + QKV_ROWS * j, 16), QKV_ROWS), :] = grad_weight[
                    pl.ds(row, QKV_ROWS), 128 * j : 128 * (j + 1)
                ].astype(bf16)
            pair = vec[pl.ds((d * vec_width) // 128, 2), :]
            pair = jnp.concatenate([pair, jnp.zeros((14, 128), f32)], axis=0)
            ref[pl.ds(pl.multiple_of(start + 4 * QKV_ROWS, 16), 16), :] = pair.astype(bf16)
            return 0

        lax.fori_loop(0, half, place, 0)


def weight_grad(me, tokens, grad_query, grad_keys, grad_values, vec, order, vec_width):
    half_rows = BLOCKS // 2 * Q_ROWS
    vmem = pl.BlockSpec(memory_space=pltpu.VMEM)
    return pl.pallas_call(
        functools.partial(weight_grad_kernel, order, vec_width),
        in_specs=[scalar_spec()] + [vmem] * 5,
        out_specs=[vmem, vmem],
        out_shape=[jax.ShapeDtypeStruct((half_rows, 128), bf16)] * 2,
        scratch_shapes=[pltpu.VMEM((48, 128), f32), pltpu.VMEM((1536, 512), f32)],
        compiler_params=params(),
        name="weight_grad",
    )(me, tokens, grad_query, grad_keys, grad_values, vec)


def input_grad_kernel(order, me_ref, grad_first, grad_query, grad_keys, grad_values, first, second, out, weight):
    step = pl.program_id(0)
    me = me_ref[0]

    @pl.when(step == 0)
    def _():
        half = BLOCKS // 2
        for base, ref in ((0, first), (half, second)):

            def place(i, _, base=base, ref=ref):
                d = owner_of(base + i, me, order)
                for j in range(4):
                    weight[pl.ds(pl.multiple_of(d * QKV_ROWS, 16), QKV_ROWS), 128 * j : 128 * (j + 1)] = ref[
                        pl.ds(pl.multiple_of(i * Q_ROWS + QKV_ROWS * j, 16), QKV_ROWS), :
                    ]
                return 0

            lax.fori_loop(0, half, place, 0)

    scale = 1.0 / math.sqrt(HEAD_DIM)
    total = grad_first[...] + scale * dot(grad_query[...], weight[0:512, :], NT)
    total = total + dot(grad_keys[...], weight[512:1024, :], TT)
    out[...] = total + dot(grad_values[...], weight[1024:1536, :], TT)


def input_grad(me, grad_first, grad_query, grad_keys, grad_values, first, second, order, rows=512):
    count = grad_first.shape[0]
    by_row = pl.BlockSpec((rows, 512), lambda i: (i, 0))
    by_column = pl.BlockSpec((512, rows), lambda i: (0, i))
    return pl.pallas_call(
        functools.partial(input_grad_kernel, order),
        grid=(count // rows,),
        in_specs=[scalar_spec(), by_row, by_row, by_column, by_column, whole(first.shape), whole(second.shape)],
        out_specs=by_row,
        out_shape=jax.ShapeDtypeStruct((count, 512), f32),
        scratch_shapes=[pltpu.VMEM((1536, 512), bf16)],
        compiler_params=params(),
        name="input_grad",
    )(me, grad_first, grad_query, grad_keys, grad_values, first, second)


def unpack_kernel(q_keep, q_got, r_keep, r_got, out, vec_out):
    q_sum = q_keep[...].astype(f32) + q_got[...].astype(f32)
    r_sum = r_keep[...].astype(f32) + r_got[...].astype(f32)
    at = 0
    source = q_sum
    for index, (start, rows, count) in enumerate(PANELS):
        if index == 1:
            source, at = r_sum, 0
        for j in range(count):
            out[pl.ds(start + j, rows, stride=count), :] = source[at : at + rows, :]
            at += rows
    vec_out[...] = q_sum[192:200, :]


def unpack(q_keep, q_got, r_keep, r_got):
    return pl.pallas_call(
        unpack_kernel,
        out_shape=[jax.ShapeDtypeStruct((512, 128), f32), jax.ShapeDtypeStruct((8, 128), f32)],
        name="unpack",
    )(q_keep, q_got, r_keep, r_got)


def swap(array, step, count):
    return lax.ppermute(array, AXES, [(i, i ^ step) for i in range(count)])


def gather_blocks(block, order, count):
    for step in order[:-1]:
        block = jnp.concatenate([block, swap(block, step, count)], axis=0)
    return block, swap(block, order[-1], count)


def scatter_blocks(keep, send, steps, count):
    for step in steps[:-1]:
        got = swap(send, step, count)
        half = keep.shape[0] // 2
        total = keep.astype(f32) + got.astype(f32)
        send = total[half:].astype(bf16)
        keep = total[:half].astype(bf16)
    return keep, swap(send, steps[-1], count)


def fast_layout(dp, fsdp):
    return dp == 4 and fsdp == 8


def body(dp, fsdp, tokens, lengths, assignment, weights, vectors, cotangent):
    count = dp * fsdp
    owner = lax.axis_index(AXES).astype(jnp.int32)
    owned = assignment == owner
    ends = jnp.cumsum(jnp.where(owned, lengths, 0), dtype=jnp.int32)
    ends = jnp.where(owned, ends, 1 << 30)[None, :]
    if fast_layout(dp, fsdp):
        vec_width = vectors.shape[0]
        core, x_step, y_step, z_near, z_far = fsdp, 1, 2 * fsdp, 2, 4
        gather_order = [z_far, z_near, y_step, x_step, core]
        scatter_steps = [core, x_step, y_step, z_near, z_far]
        scatter_order = scatter_steps[::-1]
        me = owner[None]
        placed = lax.dynamic_update_slice(jnp.zeros((16 * 128,), bf16), vectors, ((owner * vec_width) % 128,))
        q_block, r_block = pack(weights.reshape(512, 128), placed.reshape(16, 128))
        q_first, q_second = gather_blocks(q_block, gather_order, count)
        r_first, r_second = gather_blocks(r_block, gather_order, count)
    else:
        vec_width = 160
        gather_order = scatter_order = [1, 2, 4, 8, 16]
        me = jnp.zeros((1,), jnp.int32)
        blocks = lax.all_gather(weights, AXES, axis=0, tiled=True).reshape(count, -1)
        flat = lax.all_gather(vectors, AXES, axis=0, tiled=True).reshape(40, 128)
        square = 512 * 512 // count
        cuts = [0, 3 * square, 4 * square, 6 * square, 8 * square]
        panels = []
        for index, (start, rows, width) in enumerate(PANELS):
            piece = blocks[:, cuts[index] : cuts[index + 1]].reshape(BLOCKS, rows, width, 128)
            panels.append(piece.transpose(0, 2, 1, 3).reshape(BLOCKS, rows * width, 128))
        spots = [(d * vec_width) // 128 for d in range(BLOCKS)]
        lanes = jnp.arange(256)
        vec_blocks = []
        for d in range(BLOCKS):
            pair = jnp.concatenate([flat, jnp.zeros((8, 128), bf16)], axis=0)[spots[d] : spots[d] + 2].reshape(256)
            offset = d * vec_width - 128 * spots[d]
            pair = jnp.where((lanes >= offset) & (lanes < offset + vec_width), pair, 0)
            vec_blocks.append(jnp.concatenate([pair.reshape(2, 128), jnp.zeros((14, 128), bf16)], axis=0))
        q_all = jnp.concatenate([panels[0], jnp.stack(vec_blocks)], axis=1)
        r_all = jnp.concatenate(panels[1:], axis=1)
        half = BLOCKS // 2
        q_first, q_second = q_all[:half].reshape(-1, 128), q_all[half:].reshape(-1, 128)
        r_first, r_second = r_all[:half].reshape(-1, 128), r_all[half:].reshape(-1, 128)
    qkv, keys_extra, query_extra, vec = project(
        me, ends, tokens, q_first, q_second, gather_order, vec_width, vectors.shape[0] * count
    )
    attended, query_extra = attend(qkv, query_extra, keys_extra)
    layer_output, grad_first, grad_attended, grad_extra, r_keep, r_send, vec_grad = middle(
        me, tokens, attended, cotangent, vec, r_first, r_second, gather_order, scatter_order
    )
    grad_query, grad_keys, grad_values = attend_back(qkv, grad_attended, query_extra, keys_extra, grad_extra)
    q_keep, q_send = weight_grad(me, tokens, grad_query, grad_keys, grad_values, vec_grad, scatter_order, vec_width)
    grad_tokens = input_grad(
        me, grad_first, grad_query, grad_keys, grad_values, q_first, q_second, gather_order
    )
    if fast_layout(dp, fsdp):
        r_keep, r_got = scatter_blocks(r_keep, r_send, scatter_steps, count)
        q_keep, q_got = scatter_blocks(q_keep, q_send, scatter_steps, count)
        own_weights, own_vec = unpack(q_keep, q_got, r_keep, r_got)
        own_weights = own_weights.reshape(-1)
        own_vectors = lax.dynamic_slice(own_vec.reshape(-1), ((owner * vec_width) % 128,), (vec_width,))
    else:
        q_all = jnp.concatenate([q_keep, q_send], axis=0).astype(f32).reshape(BLOCKS, Q_ROWS, 128)
        r_all = jnp.concatenate([r_keep, r_send], axis=0).astype(f32).reshape(BLOCKS, R_ROWS, 128)
        sources = (q_all[:, : 4 * QKV_ROWS], r_all[:, :64], r_all[:, 64:192], r_all[:, 192:])
        pieces = []
        for source, (start, rows, width) in zip(sources, PANELS):
            piece = source.reshape(BLOCKS, width, rows, 128).transpose(0, 2, 1, 3)
            pieces.append(piece.reshape(count, -1))
        own_weights = lax.psum_scatter(
            jnp.concatenate(pieces, axis=1).reshape(-1), AXES, scatter_dimension=0, tiled=True
        )
        pairs = q_all[:, 4 * QKV_ROWS : 4 * QKV_ROWS + 2].reshape(BLOCKS, 256)
        rows = [
            pairs[d, (d * vec_width) % 128 : (d * vec_width) % 128 + vec_width] for d in range(BLOCKS)
        ]
        own_vectors = lax.psum_scatter(jnp.concatenate(rows), AXES, scatter_dimension=0, tiled=True)
    return (layer_output, grad_tokens, own_weights, own_vectors)


def solution(mesh):
    dp, fsdp = mesh.shape["dp"], mesh.shape["fsdp"]
    in_specs = (
        P(AXES, None),
        P(),
        P(),
        P(AXES),
        P(AXES),
        P(AXES, None),
    )
    out_specs = (
        P(AXES, None),
        P(AXES, None),
        P(AXES),
        P(AXES),
    )
    return jax.shard_map(
        functools.partial(body, dp, fsdp), mesh=mesh, in_specs=in_specs, out_specs=out_specs, check_vma=False
    )
```

```python
import functools
import math

import jax
import jax.numpy as jnp
from jax import lax
from jax.experimental import pallas as pl
from jax.experimental.pallas import tpu as pltpu
from jax.sharding import PartitionSpec as P

HEADS = 4
HEAD_DIM = 128
FF = 1024
AXES = ("dp", "fsdp")
NORM_EPS = 1e-05
BLOCKS = 32
QKV_ROWS = 48
Q_ROWS = 4 * QKV_ROWS + 16
R_ROWS = 320
FAR = -1e30
f32 = jnp.float32
bf16 = jnp.bfloat16
NT = (((1,), (1,)), ((), ()))
NN = (((1,), (0,)), ((), ()))
TN = (((0,), (0,)), ((), ()))
TT = (((0,), (1,)), ((), ()))
VMEM_BYTES = 60 << 20


def dot(a, b, dims):
    return lax.dot_general(a, b, dims, preferred_element_type=f32)


def params():
    return pltpu.CompilerParams(vmem_limit_bytes=VMEM_BYTES)


def cost(flops, moved, special=0):
    return pl.CostEstimate(flops=int(flops), bytes_accessed=int(moved), transcendentals=int(special))


def whole(shape):
    return pl.BlockSpec(shape, lambda *_: (0,) * len(shape))


def scalar_spec():
    return pl.BlockSpec(memory_space=pltpu.SMEM)


def owner_of(place, me, order):
    mask = 0
    for bit, step in enumerate(order):
        mask = mask + ((place >> bit) & 1) * step
    return jnp.bitwise_xor(me, mask)


def split3(value):
    high = value.astype(bf16)
    rest = value - high.astype(f32)
    middle = rest.astype(bf16)
    low = (rest - middle.astype(f32)).astype(bf16)
    return high, middle, low


PANELS = ((0, 48, 4), (192, 16, 4), (256, 16, 8), (384, 32, 4))


def pack_kernel(vec_width, me_ref, flat, vec, q_out, r_out, wide):
    wide[...] = flat[...].astype(f32)
    shifted = pltpu.roll(vec[...].astype(f32), (me_ref[0] * vec_width) % 128, 1)
    parts = []
    for start, rows, count in PANELS:
        for j in range(count):
            parts.append(wide[pl.ds(start + j, rows, stride=count), :].astype(bf16))
    q_out[0:192, :] = jnp.concatenate(parts[:4], axis=0)
    placed = jnp.concatenate([shifted[0:1, 0:128], shifted[0:1, 128:256], jnp.zeros((14, 128), f32)], axis=0)
    q_out[192:208, :] = placed.astype(bf16)
    r_out[...] = jnp.concatenate(parts[4:], axis=0)


def pack(me, flat, vec, vec_width):
    vmem = pl.BlockSpec(memory_space=pltpu.VMEM)
    return pl.pallas_call(
        functools.partial(pack_kernel, vec_width),
        in_specs=[scalar_spec(), vmem, vmem],
        out_shape=[
            jax.ShapeDtypeStruct((Q_ROWS, 128), bf16),
            jax.ShapeDtypeStruct((R_ROWS, 128), bf16),
        ],
        scratch_shapes=[pltpu.VMEM((512, 128), f32)],
        name="pack",
    )(me, flat, vec)


def project_kernel(masks, order, vec_width, me_ref, ends, tokens, *refs):
    pieces = refs[: len(masks)]
    qkv, keys_extra, query_extra, vec_out, weight, vec = refs[len(masks) :]
    step = pl.program_id(0)
    rows = tokens.shape[0]
    me = me_ref[0]

    @pl.when(step == 0)
    def _():
        vec[...] = jnp.zeros_like(vec)
        for mask, ref in zip(masks, pieces):
            for i in range(1 << len(order)):
                d = owner_of(i, jnp.bitwise_xor(me, mask), order)
                row = pl.multiple_of(d * QKV_ROWS, 16)
                for j in range(4):
                    at = i * Q_ROWS + QKV_ROWS * j
                    weight[pl.ds(row, QKV_ROWS), 128 * j : 128 * (j + 1)] = ref[at : at + QKV_ROWS, :]
                row = (d * vec_width) // 128
                at = i * Q_ROWS + 4 * QKV_ROWS
                vec[pl.ds(row, 2), :] = vec[pl.ds(row, 2), :] + ref[at : at + 16, :].astype(f32)[0:2, :]
        vec_out[...] = vec[...]

    x = tokens[...]
    scale = 1.0 / math.sqrt(HEAD_DIM)
    query_bias = jnp.concatenate([vec[j : j + 1, :] for j in range(4)], axis=1)
    value_bias = jnp.concatenate([vec[4 + j : 5 + j, :] for j in range(4)], axis=1)
    queries = ((dot(x, weight[0:512, :], NN) + query_bias) * scale).astype(bf16)
    key_heads = dot(x, weight[512:1024, :], NN).astype(bf16)
    values = (dot(x, weight[1024:1536, :], NN) + value_bias).astype(bf16)
    qkv[:, 0:512] = queries
    qkv[:, 512:1024] = key_heads
    qkv[:, 1024:1536] = values
    places = step * rows + lax.broadcasted_iota(jnp.int32, (rows, ends.shape[1]), 0)
    label = jnp.sum((ends[...] <= places).astype(f32), axis=1, keepdims=True)
    lane = lax.broadcasted_iota(jnp.int32, (rows, 128), 1)
    same = lane.astype(f32) == label
    keys_extra[...] = jnp.where(lane < 8, jnp.where(same, 1.0, 0.0), jnp.where(lane < 12, 1.0, 0.0)).astype(bf16)
    apart = jnp.where((lane < 8) & jnp.logical_not(same), FAR, 0.0)
    product = queries.astype(f32) * key_heads.astype(f32)
    for h in range(HEADS):
        own = jnp.sum(product[:, 128 * h : 128 * (h + 1)], axis=1, keepdims=True)
        query_extra[h] = jnp.where(lane == 8, -own, apart).astype(bf16)


def project(me, ends, tokens, pieces, masks, order, vec_width, rows=512):
    count = tokens.shape[0]
    sets = ends.shape[1]
    return pl.pallas_call(
        functools.partial(project_kernel, masks, order, vec_width),
        grid=(count // rows,),
        in_specs=[
            scalar_spec(),
            whole((1, sets)),
            pl.BlockSpec((rows, 512), lambda i: (i, 0)),
        ]
        + [whole(piece.shape) for piece in pieces],
        out_specs=[
            pl.BlockSpec((rows, 1536), lambda i: (i, 0)),
            pl.BlockSpec((rows, 128), lambda i: (i, 0)),
            pl.BlockSpec((HEADS, rows, 128), lambda i: (0, i, 0)),
            whole((48, 128)),
            whole((1536, 512)),
        ],
        out_shape=[
            jax.ShapeDtypeStruct((count, 1536), bf16),
            jax.ShapeDtypeStruct((count, 128), bf16),
            jax.ShapeDtypeStruct((HEADS, count, 128), bf16),
            jax.ShapeDtypeStruct((48, 128), f32),
            jax.ShapeDtypeStruct((1536, 512), bf16),
        ],
        scratch_shapes=[pltpu.VMEM((48, 128), f32)],
        compiler_params=params(),
        cost_estimate=cost(2 * count * 512 * 1536, 12e6),
        name="project",
    )(me, ends, tokens, *pieces)


def attend_kernel(q, k, v, query_extra, keys_extra, *refs):
    attended, query_extra_out, total, mixed, peak = refs[-5:]
    rows = q.shape[0]
    left = jnp.concatenate([k[...], keys_extra[...]], axis=1)
    right = jnp.concatenate([q[...], query_extra[0]], axis=1)
    scores = dot(left, right, NT)
    weights = jnp.exp(scores)
    total[...] = jnp.sum(weights, axis=0, keepdims=True)
    mixed[...] = dot(v[...], weights.astype(bf16), TN)
    peak[...] = jnp.zeros_like(peak)
    good = jnp.where((total[...] > 1e-20) & (total[...] < 1e30), 0.0, 1.0)

    @pl.when(jnp.sum(good) > 0.0)
    def _():
        again = dot(left, right, NT)
        top = jnp.max(again, axis=0, keepdims=True)
        safe = jnp.exp(again - top)
        total[...] = jnp.sum(safe, axis=0, keepdims=True)
        mixed[...] = dot(v[...], safe.astype(bf16), TN)
        peak[...] = top

    attended[...] = (mixed[...] * (1.0 / total[...])).T.astype(bf16)
    offset = jnp.broadcast_to(peak[...] + jnp.log(total[...]), (128, rows)).T
    high, middle, low = split3(-offset)
    lane = lax.broadcasted_iota(jnp.int32, (rows, 128), 1)
    extra = query_extra[0].astype(f32)
    extra = jnp.where(lane == 9, high.astype(f32), extra)
    extra = jnp.where(lane == 10, middle.astype(f32), extra)
    extra = jnp.where(lane == 11, low.astype(f32), extra)
    query_extra_out[0] = extra.astype(bf16)


def attend(qkv, query_extra, keys_extra, base, heads, prior, rows=1024):
    count = qkv.shape[0]
    return pl.pallas_call(
        attend_kernel,
        grid=(heads, count // rows),
        in_specs=[
            pl.BlockSpec((rows, 128), lambda h, i: (i, base + h)),
            pl.BlockSpec((count, 128), lambda h, i: (0, HEADS + base + h)),
            pl.BlockSpec((count, 128), lambda h, i: (0, 2 * HEADS + base + h)),
            pl.BlockSpec((1, rows, 128), lambda h, i: (base + h, i, 0)),
            pl.BlockSpec((count, 128), lambda h, i: (0, 0)),
        ]
        + [pl.BlockSpec(memory_space=pl.ANY) for _ in prior],
        out_specs=[
            pl.BlockSpec((rows, 128), lambda h, i: (i, base + h)),
            pl.BlockSpec((1, rows, 128), lambda h, i: (base + h, i, 0)),
        ],
        out_shape=[
            jax.ShapeDtypeStruct((count, 128 * HEADS), bf16),
            jax.ShapeDtypeStruct((HEADS, count, 128), bf16),
        ],
        scratch_shapes=[pltpu.VMEM((1, rows), f32), pltpu.VMEM((128, rows), f32), pltpu.VMEM((1, rows), f32)],
        input_output_aliases={5: 0, 6: 1} if prior else {},
        compiler_params=params(),
        cost_estimate=cost(heads * 8 * count * count * 128, 6e6, heads * count * count),
        name="attend",
    )(qkv, qkv, qkv, query_extra, keys_extra, *prior)


def mean_row(value):
    return jnp.sum(value, axis=1, keepdims=True) * (1.0 / value.shape[1])


def norm_rows(summed):
    centered = summed - mean_row(summed)
    inverse = lax.rsqrt(mean_row(centered * centered) + NORM_EPS)
    return centered * inverse, inverse


def norm_back(grad, normed, inverse):
    return inverse * (grad - mean_row(grad) - normed * mean_row(grad * normed))


def fold8(value):
    return jnp.sum(value.reshape(value.shape[0] // 8, 8, value.shape[1]), axis=0)


def middle_kernel(masks, order_in, order_out, sub, me_ref, tokens, attended, cotangent, vec, *refs):
    pieces = refs[: len(masks)]
    layer_output, grad_first_out, grad_attended_out, grad_extra, keep, send, vec_out = refs[len(masks) : -8]
    attn_weight, in_weight, out_weight, grad_attn, grad_in, grad_out, sums, hidden_sum = refs[-8:]
    step = pl.program_id(0)
    me = me_ref[0]
    half = BLOCKS // 2

    @pl.when(step == 0)
    def _():
        for mask, ref in zip(masks, pieces):

            def place(i, _, mask=mask, ref=ref):
                d = owner_of(i, jnp.bitwise_xor(me, mask), order_in)
                start = i * R_ROWS
                a_row = pl.multiple_of(d * 16, 16)
                o_row = pl.multiple_of(d * 32, 16)
                for j in range(4):
                    attn_weight[pl.ds(a_row, 16), 128 * j : 128 * (j + 1)] = ref[
                        pl.ds(pl.multiple_of(start + 16 * j, 16), 16), :
                    ]
                for j in range(8):
                    in_weight[pl.ds(a_row, 16), 128 * j : 128 * (j + 1)] = ref[
                        pl.ds(pl.multiple_of(start + 64 + 16 * j, 16), 16), :
                    ]
                for j in range(4):
                    out_weight[pl.ds(o_row, 32), 128 * j : 128 * (j + 1)] = ref[
                        pl.ds(pl.multiple_of(start + 192 + 32 * j, 16), 32), :
                    ]
                return 0

            lax.fori_loop(0, 1 << len(order_in), place, 0)
        grad_attn[...] = jnp.zeros_like(grad_attn)
        grad_in[...] = jnp.zeros_like(grad_in)
        grad_out[...] = jnp.zeros_like(grad_out)
        sums[...] = jnp.zeros_like(sums)
        hidden_sum[...] = jnp.zeros_like(hidden_sum)

    def row_of(index):
        return jnp.concatenate([vec[4 * index + j : 4 * index + j + 1, :] for j in range(4)], axis=1)

    attn_bias, ffn_bias, gain_one, shift_one, gain_two, shift_two = [row_of(i) for i in range(2, 8)]
    hidden_bias = jnp.concatenate([vec[32 + j : 33 + j, :] for j in range(8)], axis=1)

    def chain(s):
        sl = slice(s * sub, (s + 1) * sub)
        att = attended[sl, :]
        branch = dot(att, attn_weight[...], NN) + attn_bias
        yield
        normed_one, inverse_one = norm_rows(tokens[sl, :].astype(f32) + branch)
        hidden = normed_one * gain_one + shift_one
        hidden_low = hidden.astype(bf16)
        yield
        pre_act = dot(hidden_low, in_weight[...], NN) + hidden_bias
        yield
        cdf = 0.5 * (1.0 + lax.erf(pre_act * 0.7071067811865476))
        density = jnp.exp(-0.5 * pre_act * pre_act) * 0.3989422804014327
        activated = (pre_act * cdf).astype(bf16)
        slope = cdf + pre_act * density
        yield
        ffn_result = dot(activated, out_weight[...], NN) + ffn_bias
        yield
        normed_two, inverse_two = norm_rows(hidden + ffn_result)
        layer_output[sl, :] = (normed_two * gain_two + shift_two).astype(bf16)
        grad_result = cotangent[sl, :].astype(f32)
        sums[4] += fold8(grad_result * normed_two)
        sums[5] += fold8(grad_result)
        grad_second = norm_back(grad_result * gain_two, normed_two, inverse_two)
        grad_ffn = grad_second.astype(bf16)
        sums[1] += fold8(grad_ffn.astype(f32))
        yield
        grad_activated = dot(grad_ffn, out_weight[...], NT)
        grad_out[...] += dot(activated, grad_ffn, TN)
        yield
        grad_pre = (grad_activated * slope).astype(bf16)
        hidden_sum[...] += fold8(grad_pre.astype(f32))
        yield
        grad_hidden = grad_second + dot(grad_pre, in_weight[...], NT)
        grad_in[...] += dot(hidden_low, grad_pre, TN)
        yield
        sums[2] += fold8(grad_hidden * normed_one)
        sums[3] += fold8(grad_hidden)
        grad_first = norm_back(grad_hidden * gain_one, normed_one, inverse_one)
        grad_first_out[sl, :] = grad_first
        grad_branch = grad_first.astype(bf16)
        sums[0] += fold8(grad_branch.astype(f32))
        yield
        grad_attended = dot(grad_branch, attn_weight[...], NT).astype(bf16)
        grad_attn[...] += dot(att, grad_branch, TN)
        yield
        grad_attended_out[sl, :] = grad_attended
        product = grad_attended.astype(f32) * att.astype(f32)
        lane = lax.broadcasted_iota(jnp.int32, (sub, 128), 1)
        for h in range(HEADS):
            centre = jnp.sum(product[:, 128 * h : 128 * (h + 1)], axis=1, keepdims=True)
            high, middle, low = split3(-centre)
            extra = jnp.where(lane == 0, high.astype(f32), 0.0)
            extra = jnp.where(lane == 1, middle.astype(f32), extra)
            extra = jnp.where(lane == 2, low.astype(f32), extra)
            grad_extra[h, sl, :] = extra.astype(bf16)
        yield

    chains = [chain(s) for s in range(tokens.shape[0] // sub)]
    started = 0
    live = []
    while started < len(chains) or live:
        if started < len(chains):
            live.append(chains[started])
            started += 1
        remaining = []
        for c in live:
            try:
                next(c)
                remaining.append(c)
            except StopIteration:
                pass
        live = remaining

    @pl.when(step == pl.num_programs(0) - 1)
    def _():
        for base, ref in ((0, keep), (half, send)):

            def place(i, _, base=base, ref=ref):
                d = owner_of(base + i, me, order_out)
                start = i * R_ROWS
                a_row = pl.multiple_of(d * 16, 16)
                o_row = pl.multiple_of(d * 32, 16)
                for j in range(4):
                    ref[pl.ds(pl.multiple_of(start + 16 * j, 16), 16), :] = grad_attn[
                        pl.ds(a_row, 16), 128 * j : 128 * (j + 1)
                    ].astype(bf16)
                for j in range(8):
                    ref[pl.ds(pl.multiple_of(start + 64 + 16 * j, 16), 16), :] = grad_in[
                        pl.ds(a_row, 16), 128 * j : 128 * (j + 1)
                    ].astype(bf16)
                for j in range(4):
                    ref[pl.ds(pl.multiple_of(start + 192 + 32 * j, 16), 32), :] = grad_out[
                        pl.ds(o_row, 32), 128 * j : 128 * (j + 1)
                    ].astype(bf16)
                return 0

            lax.fori_loop(0, half, place, 0)
        vec_out[...] = jnp.zeros_like(vec_out)
        for i in range(6):
            row = jnp.sum(sums[i], axis=0, keepdims=True)
            for j in range(4):
                vec_out[8 + 4 * i + j : 9 + 4 * i + j, :] = row[:, 128 * j : 128 * (j + 1)]
        row = jnp.sum(hidden_sum[...], axis=0, keepdims=True)
        for j in range(8):
            vec_out[32 + j : 33 + j, :] = row[:, 128 * j : 128 * (j + 1)]


def middle(
    me, tokens, attended, cotangent, vec, pieces, masks, order_in, order_out, rows=512, sub=256
):
    count = tokens.shape[0]
    by_row = pl.BlockSpec((rows, 512), lambda i: (i, 0))
    half_rows = BLOCKS // 2 * R_ROWS
    return pl.pallas_call(
        functools.partial(middle_kernel, masks, order_in, order_out, sub),
        grid=(count // rows,),
        in_specs=[
            scalar_spec(),
            by_row,
            by_row,
            by_row,
            whole((48, 128)),
        ]
        + [whole(piece.shape) for piece in pieces],
        out_specs=[
            by_row,
            by_row,
            by_row,
            pl.BlockSpec((HEADS, rows, 128), lambda i: (0, i, 0)),
            whole((half_rows, 128)),
            whole((half_rows, 128)),
            whole((48, 128)),
        ],
        out_shape=[
            jax.ShapeDtypeStruct((count, 512), bf16),
            jax.ShapeDtypeStruct((count, 512), f32),
            jax.ShapeDtypeStruct((count, 512), bf16),
            jax.ShapeDtypeStruct((HEADS, count, 128), bf16),
            jax.ShapeDtypeStruct((half_rows, 128), bf16),
            jax.ShapeDtypeStruct((half_rows, 128), bf16),
            jax.ShapeDtypeStruct((48, 128), f32),
        ],
        scratch_shapes=[
            pltpu.VMEM((512, 512), bf16),
            pltpu.VMEM((512, FF), bf16),
            pltpu.VMEM((FF, 512), bf16),
            pltpu.VMEM((512, 512), f32),
            pltpu.VMEM((512, FF), f32),
            pltpu.VMEM((FF, 512), f32),
            pltpu.VMEM((6, 8, 512), f32),
            pltpu.VMEM((8, FF), f32),
        ],
        compiler_params=params(),
        cost_estimate=cost(6 * count * 1310720, 22e6, 3 * count * FF),
        name="middle",
    )(me, tokens, attended, cotangent, vec, *pieces)


def attend_back_kernel(
    base,
    heads,
    order,
    vec_width,
    me_ref,
    tokens,
    q,
    k,
    v,
    grad,
    query_extra,
    keys_extra,
    grad_extra,
    vec_in,
    grad_query,
    grad_keys,
    grad_values,
    keep,
    send,
    vec,
    acc,
    keys_t,
    values_t,
    grad_weight,
    held,
    sem,
):
    local = pl.program_id(0)
    step = pl.program_id(1)
    steps = pl.num_programs(1)
    width = k.shape[0]
    last = base + heads == HEADS
    copy = pltpu.make_async_copy(tokens, held, sem)

    @pl.when((local == 0) & (step == 0))
    def _():
        copy.start()
        vec[...] = vec_in[...]

    lane = lax.broadcasted_iota(jnp.int32, (width, 128), 1)
    ones = jnp.where(lane < 3, 1.0, 0.0).astype(bf16)
    scores = dot(
        jnp.concatenate([q[...], query_extra[0]], axis=1),
        jnp.concatenate([k[...], keys_extra[...]], axis=1),
        NT,
    )
    centred = dot(
        jnp.concatenate([grad[...], grad_extra[0]], axis=1), jnp.concatenate([v[...], ones], axis=1), NT
    )
    probs = jnp.exp(scores)
    probs_low = probs.astype(bf16)
    grad_scores = (probs * centred).astype(bf16)
    keys_t[step] = dot(q[...], grad_scores, TN).astype(bf16)
    values_t[step] = dot(grad[...], probs_low, TN).astype(bf16)
    grad_keys[...] = keys_t[step]
    grad_values[...] = values_t[step]
    part = dot(grad_scores, k[...], NN)

    @pl.when(step == 0)
    def _():
        acc[...] = part

    @pl.when(step > 0)
    def _():
        acc[...] += part

    @pl.when((local == 0) & (step == steps - 1))
    def _():
        copy.wait()

    @pl.when(step == steps - 1)
    def _():
        me = me_ref[0]
        scale = 1.0 / math.sqrt(HEAD_DIM)
        x = held[...]
        gq = acc[...].astype(bf16)
        grad_query[...] = gq
        gk = jnp.concatenate([keys_t[i] for i in range(keys_t.shape[0])], axis=1)
        gv = jnp.concatenate([values_t[i] for i in range(values_t.shape[0])], axis=1)
        grad_weight[0:512, :] = dot(gq, x, TN).T * scale
        grad_weight[512:1024, :] = dot(gk, x, NN).T
        grad_weight[1024:1536, :] = dot(gv, x, NN).T
        row_ones = jnp.ones((8, x.shape[0]), bf16)
        vec[pl.ds(base + local, 1), :] = dot(row_ones, gq, NN)[0:1] * scale
        vec[pl.ds(4 + base + local, 1), :] = dot(row_ones, gv, NT)[0:1]
        half = BLOCKS // 2
        block = heads * QKV_ROWS + (16 if last else 0)
        for start, ref in ((0, keep), (half, send)):

            def place(i, _, start=start, ref=ref):
                d = owner_of(start + i, me, order)
                ref[pl.ds(pl.multiple_of(i * block + local * QKV_ROWS, 16), QKV_ROWS), :] = grad_weight[
                    pl.ds(pl.multiple_of(d * QKV_ROWS, 16), QKV_ROWS), :
                ].astype(bf16)
                if last:
                    pair = vec[pl.ds((d * vec_width) // 128, 2), :]
                    pair = jnp.concatenate([pair, jnp.zeros((14, 128), f32)], axis=0)
                    ref[pl.ds(pl.multiple_of(i * block + heads * QKV_ROWS, 16), 16), :] = pair.astype(bf16)
                return 0

            lax.fori_loop(0, half, place, 0)


def attend_back(
    me, tokens, qkv, grad_attended, query_extra, keys_extra, grad_extra, vec, order, vec_width, base, heads, width=512
):
    count = qkv.shape[0]
    half_rows = BLOCKS // 2 * (heads * QKV_ROWS + (16 if base + heads == HEADS else 0))
    return pl.pallas_call(
        functools.partial(attend_back_kernel, base, heads, order, vec_width),
        grid=(heads, count // width),
        in_specs=[
            scalar_spec(),
            pl.BlockSpec(memory_space=pl.ANY),
            pl.BlockSpec((count, 128), lambda h, i: (0, base + h)),
            pl.BlockSpec((width, 128), lambda h, i: (i, HEADS + base + h)),
            pl.BlockSpec((width, 128), lambda h, i: (i, 2 * HEADS + base + h)),
            pl.BlockSpec((count, 128), lambda h, i: (0, base + h)),
            pl.BlockSpec((1, count, 128), lambda h, i: (base + h, 0, 0)),
            pl.BlockSpec((width, 128), lambda h, i: (i, 0)),
            pl.BlockSpec((1, count, 128), lambda h, i: (base + h, 0, 0)),
            whole((48, 128)),
        ],
        out_specs=[
            pl.BlockSpec((count, 128), lambda h, i: (0, h)),
            pl.BlockSpec((128, width), lambda h, i: (h, i)),
            pl.BlockSpec((128, width), lambda h, i: (h, i)),
            whole((half_rows, 128)),
            whole((half_rows, 128)),
            whole((48, 128)),
        ],
        out_shape=[
            jax.ShapeDtypeStruct((count, 128 * heads), bf16),
            jax.ShapeDtypeStruct((128 * heads, count), bf16),
            jax.ShapeDtypeStruct((128 * heads, count), bf16),
            jax.ShapeDtypeStruct((half_rows, 128), bf16),
            jax.ShapeDtypeStruct((half_rows, 128), bf16),
            jax.ShapeDtypeStruct((48, 128), f32),
        ],
        scratch_shapes=[
            pltpu.VMEM((count, 128), f32),
            pltpu.VMEM((count // width, 128, width), bf16),
            pltpu.VMEM((count // width, 128, width), bf16),
            pltpu.VMEM((1536, 128), f32),
            pltpu.VMEM((count, 512), bf16),
            pltpu.SemaphoreType.DMA,
        ],
        compiler_params=params(),
        cost_estimate=cost(heads * 20 * count * count * 128, heads * 6e6, heads * count * count),
        name="attend_back",
    )(me, tokens, qkv, qkv, qkv, grad_attended, query_extra, keys_extra, grad_extra, vec)


def input_grad_kernel(groups, *refs):
    grad_first = refs[0]
    queries, keys, values = [refs[1 + i * groups : 1 + (i + 1) * groups] for i in range(3)]
    weight, out = refs[-2], refs[-1]
    scale = 1.0 / math.sqrt(HEAD_DIM)
    gq = jnp.concatenate([r[...] for r in queries], axis=1)
    gk = jnp.concatenate([r[...] for r in keys], axis=0)
    gv = jnp.concatenate([r[...] for r in values], axis=0)
    total = grad_first[...] + scale * dot(gq, weight[0:512, :], NT)
    total = total + dot(gk, weight[512:1024, :], TT)
    out[...] = total + dot(gv, weight[1024:1536, :], TT)


def input_grad(grad_first, queries, keys, values, weight, rows=512):
    count = grad_first.shape[0]
    by_row = pl.BlockSpec((rows, 512), lambda i: (i, 0))
    return pl.pallas_call(
        functools.partial(input_grad_kernel, len(queries)),
        grid=(count // rows,),
        in_specs=[by_row]
        + [pl.BlockSpec((rows, a.shape[1]), lambda i: (i, 0)) for a in queries]
        + [pl.BlockSpec((a.shape[0], rows), lambda i: (0, i)) for a in keys + values]
        + [whole((1536, 512))],
        out_specs=by_row,
        out_shape=jax.ShapeDtypeStruct((count, 512), f32),
        compiler_params=params(),
        cost_estimate=cost(2 * count * 512 * 1536, 16e6),
        name="input_grad",
    )(grad_first, *queries, *keys, *values, weight)


def unpack_kernel(vec_width, me_ref, q_keep, q_got, r_keep, r_got, out, vec_out):
    q_sum = q_keep[...] + q_got[...].astype(f32)
    r_sum = r_keep[...] + r_got[...].astype(f32)
    at = 0
    source = q_sum
    for index, (start, rows, count) in enumerate(PANELS):
        if index == 1:
            source, at = r_sum, 0
        for j in range(count):
            out[pl.ds(start + j, rows, stride=count), :] = source[at : at + rows, :]
            at += rows
    pair = jnp.concatenate([q_sum[192:200, :], q_sum[193:201, :]], axis=1)
    vec_out[...] = pltpu.roll(pair, 256 - (me_ref[0] * vec_width) % 128, 1)


def unpack(me, q_keep, q_got, r_keep, r_got, vec_width):
    vmem = pl.BlockSpec(memory_space=pltpu.VMEM)
    return pl.pallas_call(
        functools.partial(unpack_kernel, vec_width),
        in_specs=[scalar_spec()] + [vmem] * 4,
        out_shape=[jax.ShapeDtypeStruct((512, 128), f32), jax.ShapeDtypeStruct((8, 256), f32)],
        name="unpack",
    )(me, q_keep, q_got, r_keep, r_got)


def swap(array, step, count):
    return lax.ppermute(array, AXES, [(i, i ^ step) for i in range(count)])


def after(value, *others):
    return lax.optimization_barrier((value, *others))[0]


def quarters(groups):
    totals = []
    for keep, got in groups:
        total = keep.astype(f32) + got.astype(f32)
        totals.append(total.reshape(4, 4, -1, 128))
    total = jnp.concatenate(totals, axis=2) if len(totals) > 1 else totals[0]
    return total[0], [total[i].astype(bf16).reshape(-1, 128) for i in range(1, 4)]


def halves(keep, gots, blocks):
    total = keep
    for got in gots:
        total = total + got.astype(f32).reshape(keep.shape)
    rows = blocks // 2
    return total[:rows], total[rows:].astype(bf16).reshape(-1, 128)


def fast_layout(dp, fsdp):
    return dp == 4 and fsdp == 8


def gather_far(block, z_far, z_near, count):
    block = jnp.concatenate([block, swap(block, z_far, count)], axis=0)
    return jnp.concatenate([block, swap(block, z_near, count)], axis=0)


def body(dp, fsdp, tokens, lengths, assignment, weights, vectors, cotangent):
    count = dp * fsdp
    fast = fast_layout(dp, fsdp)
    owner = lax.axis_index(AXES).astype(jnp.int32)
    owned = assignment == owner
    ends = jnp.cumsum(jnp.where(owned, lengths, 0), dtype=jnp.int32)
    ends = jnp.where(owned, ends, 1 << 30)[None, :]
    if fast:
        vec_width = vectors.shape[0]
        core, x_step, y_step, z_near, z_far = fsdp, 1, 2 * fsdp, 2, 4
        planes = [x_step, y_step, x_step + y_step]
        order_in = [z_far, z_near]
        order_out = [z_far, z_near, x_step, y_step, core]
        masks = [0] + planes
        masks = masks + [m + core for m in masks]
        me = owner[None]
        padded = jnp.pad(vectors, (0, 256 - vec_width)).reshape(1, 256)
        q_block, r_block = pack(me, weights.reshape(512, 128), jnp.broadcast_to(padded, (16, 256)), vec_width)
        q_far = gather_far(q_block, z_far, z_near, count)
        q_pieces = [q_far] + [swap(q_far, step, count) for step in planes]
        q_pieces = q_pieces + [swap(piece, core, count) for piece in q_pieces]
        r_far = gather_far(after(r_block, q_far), z_far, z_near, count)
        r_pieces = [swap(after(r_far, *q_pieces), step, count) for step in planes]
    else:
        vec_width = 160
        order_in, order_out = [1, 2], [1, 2, 4, 8, 16]
        masks = [4 * i for i in range(8)]
        me = jnp.zeros((1,), jnp.int32)
        blocks = lax.all_gather(weights, AXES, axis=0, tiled=True).reshape(count, -1)
        flat = lax.all_gather(vectors, AXES, axis=0, tiled=True).reshape(40, 128)
        square = 512 * 512 // count
        cuts = [0, 3 * square, 4 * square, 6 * square, 8 * square]
        panels = []
        for index, (start, rows, width) in enumerate(PANELS):
            piece = blocks[:, cuts[index] : cuts[index + 1]].reshape(BLOCKS, rows, width, 128)
            panels.append(piece.transpose(0, 2, 1, 3).reshape(BLOCKS, rows * width, 128))
        spots = [(d * vec_width) // 128 for d in range(BLOCKS)]
        lanes = jnp.arange(256)
        vec_blocks = []
        for d in range(BLOCKS):
            pair = jnp.concatenate([flat, jnp.zeros((8, 128), bf16)], axis=0)[spots[d] : spots[d] + 2].reshape(256)
            offset = d * vec_width - 128 * spots[d]
            pair = jnp.where((lanes >= offset) & (lanes < offset + vec_width), pair, 0)
            vec_blocks.append(jnp.concatenate([pair.reshape(2, 128), jnp.zeros((14, 128), bf16)], axis=0))
        q_all = jnp.concatenate([panels[0], jnp.stack(vec_blocks)], axis=1)
        r_all = jnp.concatenate(panels[1:], axis=1)
        q_pieces = [q_all[4 * i : 4 * i + 4].reshape(-1, 128) for i in range(8)]
        r_pieces = [r_all[4 * i : 4 * i + 4].reshape(-1, 128) for i in range(8)]
    qkv, keys_extra, query_extra, vec, weight = project(
        me, ends, tokens, q_pieces, masks, order_in, vec_width
    )
    prior = attend(qkv, query_extra, keys_extra, 0, 2, [])
    if fast:
        r_pieces = [r_far] + [after(piece, prior[0]) for piece in r_pieces]
        keys_extra = after(keys_extra, *r_pieces)
        r_pieces = r_pieces + [swap(piece, core, count) for piece in r_pieces]
    attended, query_extra = attend(qkv, query_extra, keys_extra, 2, 2, prior)
    layer_output, grad_first, grad_attended, grad_extra, r_keep, r_send, vec_grad = middle(
        me, tokens, attended, cotangent, vec, r_pieces, masks, order_in, order_out
    )
    queries, keys, values, keeps, sends, gots = [], [], [], [], [], []
    if fast:
        r_got = swap(r_send, core, count)
    for base, heads in ((0, 1), (1, 2), (3, 1)):
        gq, gk, gv, keep, send, vec_grad = attend_back(
            me,
            tokens,
            qkv,
            grad_attended,
            query_extra,
            keys_extra,
            grad_extra,
            vec_grad,
            order_out,
            vec_width,
            base,
            heads,
        )
        queries.append(gq)
        keys.append(gk)
        values.append(gv)
        keeps.append(keep)
        sends.append(send)
        if not fast:
            continue
        gots.append(swap(send, core, count))
        if base == 0:
            r_keep, r_sends = quarters([(r_keep, after(r_got, gq))])
            vec_grad = after(vec_grad, *r_sends)
            r_gots = [swap(part, step, count) for part, step in zip(r_sends, planes)]
        elif base == 1:
            r_gots = [after(part, gq) for part in r_gots]
            r_keep, r_send = halves(r_keep, r_gots, 4)
            vec_grad = after(vec_grad, r_send)
            r_got = swap(r_send, z_near, count)
    if fast:
        r_keep, r_send = halves(r_keep, [after(r_got, gq)], 2)
        r_got = swap(r_send, z_far, count)
        q_keep, q_sends = quarters(list(zip(keeps, gots)))
        grad_first = after(grad_first, *q_sends)
        q_gots = [swap(part, step, count) for part, step in zip(q_sends, planes)]
    grad_tokens = input_grad(grad_first, queries, keys, values, weight)
    if fast:
        q_gots = [after(part, grad_tokens) for part in q_gots]
        q_keep, q_send = halves(q_keep, q_gots, 4)
        q_got = swap(q_send, z_near, count)
        q_keep, q_send = halves(q_keep, [q_got], 2)
        q_got = swap(q_send, z_far, count)
        own_weights, own_vec = unpack(
            me, q_keep.reshape(-1, 128), q_got, r_keep.reshape(-1, 128), r_got, vec_width
        )
        own_weights = own_weights.reshape(-1)
        own_vectors = own_vec[0, :vec_width]
    else:
        heads = [jnp.concatenate([k, g], axis=0).astype(f32).reshape(BLOCKS, -1, 128) for k, g in zip(keeps, sends)]
        q_all = jnp.concatenate(heads, axis=1)
        r_all = jnp.concatenate([r_keep, r_send], axis=0).astype(f32).reshape(BLOCKS, R_ROWS, 128)
        sources = (q_all[:, : 4 * QKV_ROWS], r_all[:, :64], r_all[:, 64:192], r_all[:, 192:])
        pieces = []
        for source, (start, rows, width) in zip(sources, PANELS):
            piece = source.reshape(BLOCKS, width, rows, 128).transpose(0, 2, 1, 3)
            pieces.append(piece.reshape(count, -1))
        own_weights = lax.psum_scatter(
            jnp.concatenate(pieces, axis=1).reshape(-1), AXES, scatter_dimension=0, tiled=True
        )
        pairs = q_all[:, 4 * QKV_ROWS : 4 * QKV_ROWS + 2].reshape(BLOCKS, 256)
        rows = [
            pairs[d, (d * vec_width) % 128 : (d * vec_width) % 128 + vec_width] for d in range(BLOCKS)
        ]
        own_vectors = lax.psum_scatter(jnp.concatenate(rows), AXES, scatter_dimension=0, tiled=True)
    return (layer_output, grad_tokens, own_weights, own_vectors)


def solution(mesh):
    dp, fsdp = mesh.shape["dp"], mesh.shape["fsdp"]
    in_specs = (
        P(AXES, None),
        P(),
        P(),
        P(AXES),
        P(AXES),
        P(AXES, None),
    )
    out_specs = (
        P(AXES, None),
        P(AXES, None),
        P(AXES),
        P(AXES),
    )
    return jax.shard_map(
        functools.partial(body, dp, fsdp), mesh=mesh, in_specs=in_specs, out_specs=out_specs, check_vma=False
    )
```

```python
import functools
import math

import jax
import jax.numpy as jnp
from jax import lax
from jax.experimental import pallas as pl
from jax.experimental.pallas import tpu as pltpu
from jax.sharding import PartitionSpec as P

HEADS = 4
HEAD_DIM = 128
FF = 1024
AXES = ("dp", "fsdp")
NORM_EPS = 1e-05
BLOCKS = 32
QKV_ROWS = 48
Q_ROWS = 4 * QKV_ROWS + 16
R_ROWS = 320
FAR = -1e30
f32 = jnp.float32
bf16 = jnp.bfloat16
NT = (((1,), (1,)), ((), ()))
NN = (((1,), (0,)), ((), ()))
TN = (((0,), (0,)), ((), ()))
TT = (((0,), (1,)), ((), ()))
VMEM_MIB = {"pack": 2, "project": 16, "attend": 28, "middle": 36, "attend_back": 28, "input_grad": 16, "unpack": 3}


def dot(a, b, dims):
    return lax.dot_general(a, b, dims, preferred_element_type=f32)


def params(name):
    return pltpu.CompilerParams(vmem_limit_bytes=VMEM_MIB[name] << 20)


def cost(flops, moved, special=0):
    return pl.CostEstimate(flops=int(flops), bytes_accessed=int(moved), transcendentals=int(special))


def whole(shape):
    return pl.BlockSpec(shape, lambda *_: (0,) * len(shape))


def scalar_spec():
    return pl.BlockSpec(memory_space=pltpu.SMEM)


def owner_of(place, me, order):
    mask = 0
    for bit, step in enumerate(order):
        mask = mask + ((place >> bit) & 1) * step
    return jnp.bitwise_xor(me, mask)


def split3(value):
    high = value.astype(bf16)
    rest = value - high.astype(f32)
    middle = rest.astype(bf16)
    low = (rest - middle.astype(f32)).astype(bf16)
    return high, middle, low


PANELS = ((0, 48, 4), (192, 16, 4), (256, 16, 8), (384, 32, 4))


def pack_kernel(vec_width, me_ref, flat, vec, q_out, r_out, wide, line):
    wide[...] = flat[...].astype(f32)
    line[...] = jnp.zeros_like(line)
    line[0:1, 0:vec_width] = vec[...].astype(f32)
    shifted = pltpu.roll(line[...], (me_ref[0] * vec_width) % 128, 1)
    parts = []
    for start, rows, count in PANELS:
        for j in range(count):
            parts.append(wide[pl.ds(start + j, rows, stride=count), :].astype(bf16))
    q_out[0:192, :] = jnp.concatenate(parts[:4], axis=0)
    placed = jnp.concatenate([shifted[0:1, 0:128], shifted[0:1, 128:256], jnp.zeros((14, 128), f32)], axis=0)
    q_out[192:208, :] = placed.astype(bf16)
    r_out[...] = jnp.concatenate(parts[4:], axis=0)


def pack(me, flat, vec, vec_width):
    vmem = pl.BlockSpec(memory_space=pltpu.VMEM)
    return pl.pallas_call(
        functools.partial(pack_kernel, vec_width),
        in_specs=[scalar_spec(), vmem, vmem],
        out_shape=[
            jax.ShapeDtypeStruct((Q_ROWS, 128), bf16),
            jax.ShapeDtypeStruct((R_ROWS, 128), bf16),
        ],
        scratch_shapes=[pltpu.VMEM((512, 128), f32), pltpu.VMEM((8, 256), f32)],
        compiler_params=params("pack"),
        name="pack",
    )(me, flat, vec)


def project_kernel(masks, order, vec_width, me_ref, ends, tokens, *refs):
    pieces = refs[: len(masks)]
    qkv, keys_extra, query_extra, vec_out, weight, vec = refs[len(masks) :]
    step = pl.program_id(0)
    rows = tokens.shape[0]
    me = me_ref[0]

    @pl.when(step == 0)
    def _():
        vec[...] = jnp.zeros_like(vec)
        for mask, ref in zip(masks, pieces):
            for i in range(1 << len(order)):
                d = owner_of(i, jnp.bitwise_xor(me, mask), order)
                row = pl.multiple_of(d * QKV_ROWS, 16)
                for j in range(4):
                    at = i * Q_ROWS + QKV_ROWS * j
                    weight[pl.ds(row, QKV_ROWS), 128 * j : 128 * (j + 1)] = ref[at : at + QKV_ROWS, :]
                row = (d * vec_width) // 128
                at = i * Q_ROWS + 4 * QKV_ROWS
                vec[pl.ds(row, 2), :] = vec[pl.ds(row, 2), :] + ref[at : at + 16, :].astype(f32)[0:2, :]
        vec_out[...] = vec[...]

    x = tokens[...]
    scale = 1.0 / math.sqrt(HEAD_DIM)
    query_bias = jnp.concatenate([vec[j : j + 1, :] for j in range(4)], axis=1)
    value_bias = jnp.concatenate([vec[4 + j : 5 + j, :] for j in range(4)], axis=1)
    queries = ((dot(x, weight[0:512, :], NN) + query_bias) * scale).astype(bf16)
    key_heads = dot(x, weight[512:1024, :], NN).astype(bf16)
    values = (dot(x, weight[1024:1536, :], NN) + value_bias).astype(bf16)
    qkv[:, 0:512] = queries
    qkv[:, 512:1024] = key_heads
    qkv[:, 1024:1536] = values
    places = step * rows + lax.broadcasted_iota(jnp.int32, (rows, ends.shape[1]), 0)
    label = jnp.sum((ends[...] <= places).astype(f32), axis=1, keepdims=True)
    lane = lax.broadcasted_iota(jnp.int32, (rows, 128), 1)
    same = lane.astype(f32) == label
    keys_extra[...] = jnp.where(lane < 8, jnp.where(same, 1.0, 0.0), jnp.where(lane < 12, 1.0, 0.0)).astype(bf16)
    apart = jnp.where((lane < 8) & jnp.logical_not(same), FAR, 0.0)
    product = queries.astype(f32) * key_heads.astype(f32)
    extra = apart
    for h in range(HEADS):
        own = jnp.sum(product[:, 128 * h : 128 * (h + 1)], axis=1, keepdims=True)
        extra = jnp.where(lane == 8 + h, -own, extra)
    query_extra[...] = extra.astype(bf16)


def project(me, ends, tokens, pieces, masks, order, vec_width, rows=512):
    count = tokens.shape[0]
    sets = ends.shape[1]
    return pl.pallas_call(
        functools.partial(project_kernel, masks, order, vec_width),
        grid=(count // rows,),
        in_specs=[
            scalar_spec(),
            whole((1, sets)),
            pl.BlockSpec((rows, 512), lambda i: (i, 0)),
        ]
        + [whole(piece.shape) for piece in pieces],
        out_specs=[
            pl.BlockSpec((rows, 1536), lambda i: (i, 0)),
            pl.BlockSpec((rows, 128), lambda i: (i, 0)),
            pl.BlockSpec((rows, 128), lambda i: (i, 0)),
            whole((48, 128)),
            whole((1536, 512)),
        ],
        out_shape=[
            jax.ShapeDtypeStruct((count, 1536), bf16),
            jax.ShapeDtypeStruct((count, 128), bf16),
            jax.ShapeDtypeStruct((count, 128), bf16),
            jax.ShapeDtypeStruct((48, 128), f32),
            jax.ShapeDtypeStruct((1536, 512), bf16),
        ],
        scratch_shapes=[pltpu.VMEM((48, 128), f32)],
        compiler_params=params("project"),
        cost_estimate=cost(2 * count * 512 * 1536, 12e6),
        name="project",
    )(me, ends, tokens, *pieces)


def attend_kernel(base, q, k, v, query_extra, keys_extra, *refs):
    attended, weights_out, inverse_out, total, mixed = refs[-5:]
    rows = q.shape[0]
    head = base + pl.program_id(0)
    lane = lax.broadcasted_iota(jnp.int32, (rows, 128), 1)
    extra = jnp.where((lane < 8) | (lane == 8 + head), query_extra[...].astype(f32), 0.0).astype(bf16)
    left = jnp.concatenate([k[...], keys_extra[...]], axis=1)
    right = jnp.concatenate([q[...], extra], axis=1)
    weights = jnp.exp(dot(left, right, NT))
    low = weights.astype(bf16)
    weights_out[0] = low
    total[...] = jnp.sum(weights, axis=0, keepdims=True)
    mixed[...] = dot(v[...], low, TN)
    good = (total[...] > 1e-8) & (total[...] < 1e8)

    @pl.when(jnp.sum(jnp.where(good, 0.0, 1.0)) > 0.0)
    def _():
        again = dot(left, right, NT)
        safe = jnp.exp(again - jnp.max(again, axis=0, keepdims=True))
        safe_low = safe.astype(bf16)
        weights_out[0] = safe_low
        total[...] = jnp.sum(safe, axis=0, keepdims=True)
        mixed[...] = dot(v[...], safe_low, TN)

    inverse = 1.0 / total[...]
    attended[...] = (mixed[...] * inverse).T.astype(bf16)
    inverse_out[0] = inverse


def attend(qkv, query_extra, keys_extra, base, heads, prior, rows=1024):
    count = qkv.shape[0]
    return pl.pallas_call(
        functools.partial(attend_kernel, base),
        grid=(heads, count // rows),
        in_specs=[
            pl.BlockSpec((rows, 128), lambda h, i: (i, base + h)),
            pl.BlockSpec((count, 128), lambda h, i: (0, HEADS + base + h)),
            pl.BlockSpec((count, 128), lambda h, i: (0, 2 * HEADS + base + h)),
            pl.BlockSpec((rows, 128), lambda h, i: (i, 0)),
            pl.BlockSpec((count, 128), lambda h, i: (0, 0)),
        ]
        + [pl.BlockSpec(memory_space=pl.ANY) for _ in prior],
        out_specs=[
            pl.BlockSpec((rows, 128), lambda h, i: (i, base + h)),
            pl.BlockSpec((1, count, rows), lambda h, i: (base + h, 0, i)),
            pl.BlockSpec((1, 1, rows), lambda h, i: (base + h, 0, i)),
        ],
        out_shape=[
            jax.ShapeDtypeStruct((count, 128 * HEADS), bf16),
            jax.ShapeDtypeStruct((HEADS, count, count), bf16),
            jax.ShapeDtypeStruct((HEADS, 1, count), f32),
        ],
        scratch_shapes=[pltpu.VMEM((1, rows), f32), pltpu.VMEM((128, rows), f32)],
        input_output_aliases={5: 0, 6: 1, 7: 2} if prior else {},
        compiler_params=params("attend"),
        cost_estimate=cost(heads * 8 * count * count * 128, 6e6 + heads * 8.4e6, heads * count * count),
        name="attend",
    )(qkv, qkv, qkv, query_extra, keys_extra, *prior)


def mean_row(value):
    return jnp.sum(value, axis=1, keepdims=True) * (1.0 / value.shape[1])


def norm_rows(summed):
    centered = summed - mean_row(summed)
    inverse = lax.rsqrt(mean_row(centered * centered) + NORM_EPS)
    return centered * inverse, inverse


def norm_back(grad, normed, inverse):
    return inverse * (grad - mean_row(grad) - normed * mean_row(grad * normed))


def fold8(value):
    return jnp.sum(value.reshape(value.shape[0] // 8, 8, value.shape[1]), axis=0)


def middle_kernel(masks, order_in, order_out, sub, me_ref, tokens, attended, inverse, cotangent, vec, *refs):
    pieces = refs[: len(masks)]
    layer_output, grad_branch_out, grad_attended_out, grad_extra, keep, send, vec_out = refs[len(masks) : -8]
    attn_weight, in_weight, out_weight, grad_attn, grad_in, grad_out, sums, hidden_sum = refs[-8:]
    step = pl.program_id(0)
    me = me_ref[0]
    half = BLOCKS // 2

    @pl.when(step == 0)
    def _():
        for mask, ref in zip(masks, pieces):

            def place(i, _, mask=mask, ref=ref):
                d = owner_of(i, jnp.bitwise_xor(me, mask), order_in)
                start = i * R_ROWS
                a_row = pl.multiple_of(d * 16, 16)
                o_row = pl.multiple_of(d * 32, 16)
                for j in range(4):
                    attn_weight[pl.ds(a_row, 16), 128 * j : 128 * (j + 1)] = ref[
                        pl.ds(pl.multiple_of(start + 16 * j, 16), 16), :
                    ]
                for j in range(8):
                    in_weight[pl.ds(a_row, 16), 128 * j : 128 * (j + 1)] = ref[
                        pl.ds(pl.multiple_of(start + 64 + 16 * j, 16), 16), :
                    ]
                for j in range(4):
                    out_weight[pl.ds(o_row, 32), 128 * j : 128 * (j + 1)] = ref[
                        pl.ds(pl.multiple_of(start + 192 + 32 * j, 16), 32), :
                    ]
                return 0

            lax.fori_loop(0, 1 << len(order_in), place, 0)
        grad_attn[...] = jnp.zeros_like(grad_attn)
        grad_in[...] = jnp.zeros_like(grad_in)
        grad_out[...] = jnp.zeros_like(grad_out)
        sums[...] = jnp.zeros_like(sums)
        hidden_sum[...] = jnp.zeros_like(hidden_sum)

    def row_of(index):
        return jnp.concatenate([vec[4 * index + j : 4 * index + j + 1, :] for j in range(4)], axis=1)

    attn_bias, ffn_bias, gain_one, shift_one, gain_two, shift_two = [row_of(i) for i in range(2, 8)]
    hidden_bias = jnp.concatenate([vec[32 + j : 33 + j, :] for j in range(8)], axis=1)

    inverse_rows = jnp.concatenate([inverse[h] for h in range(HEADS)] + [jnp.zeros((4, tokens.shape[0]), f32)], axis=0)
    inverse_columns = inverse_rows.T

    def chain(s):
        sl = slice(s * sub, (s + 1) * sub)
        att = attended[sl, :]
        branch = dot(att, attn_weight[...], NN) + attn_bias
        yield
        normed_one, inverse_one = norm_rows(tokens[sl, :].astype(f32) + branch)
        hidden = normed_one * gain_one + shift_one
        hidden_low = hidden.astype(bf16)
        yield
        pre_act = dot(hidden_low, in_weight[...], NN) + hidden_bias
        yield
        cdf = 0.5 * (1.0 + lax.erf(pre_act * 0.7071067811865476))
        density = jnp.exp(-0.5 * pre_act * pre_act) * 0.3989422804014327
        activated = (pre_act * cdf).astype(bf16)
        slope = cdf + pre_act * density
        yield
        ffn_result = dot(activated, out_weight[...], NN) + ffn_bias
        yield
        normed_two, inverse_two = norm_rows(hidden + ffn_result)
        layer_output[sl, :] = (normed_two * gain_two + shift_two).astype(bf16)
        grad_result = cotangent[sl, :].astype(f32)
        sums[4] += fold8(grad_result * normed_two)
        sums[5] += fold8(grad_result)
        grad_second = norm_back(grad_result * gain_two, normed_two, inverse_two)
        grad_ffn = grad_second.astype(bf16)
        sums[1] += fold8(grad_ffn.astype(f32))
        yield
        grad_activated = dot(grad_ffn, out_weight[...], NT)
        grad_out[...] += dot(activated, grad_ffn, TN)
        yield
        grad_pre = (grad_activated * slope).astype(bf16)
        hidden_sum[...] += fold8(grad_pre.astype(f32))
        yield
        grad_hidden = grad_second + dot(grad_pre, in_weight[...], NT)
        grad_in[...] += dot(hidden_low, grad_pre, TN)
        yield
        sums[2] += fold8(grad_hidden * normed_one)
        sums[3] += fold8(grad_hidden)
        grad_first = norm_back(grad_hidden * gain_one, normed_one, inverse_one)
        grad_branch = grad_first.astype(bf16)
        grad_branch_out[sl, :] = grad_branch
        sums[0] += fold8(grad_branch.astype(f32))
        yield
        grad_attended = dot(grad_branch, attn_weight[...], NT)
        grad_attn[...] += dot(att, grad_branch, TN)
        yield
        lane = lax.broadcasted_iota(jnp.int32, (sub, 128), 1)
        extra = jnp.zeros((sub, 128), f32)
        for h in range(HEADS):
            cols = slice(128 * h, 128 * (h + 1))
            scaled = (grad_attended[:, cols] * inverse_columns[sl, h : h + 1]).astype(bf16)
            grad_attended_out[sl, cols] = scaled
            centre = jnp.sum(scaled.astype(f32) * att[:, cols].astype(f32), axis=1, keepdims=True)
            for i, part in enumerate(split3(-centre)):
                extra = jnp.where(lane == 4 * h + i, part.astype(f32), extra)
        grad_extra[sl, :] = extra.astype(bf16)
        yield

    chains = [chain(s) for s in range(tokens.shape[0] // sub)]
    started = 0
    live = []
    while started < len(chains) or live:
        if started < len(chains):
            live.append(chains[started])
            started += 1
        remaining = []
        for c in live:
            try:
                next(c)
                remaining.append(c)
            except StopIteration:
                pass
        live = remaining

    @pl.when(step == pl.num_programs(0) - 1)
    def _():
        for base, ref in ((0, keep), (half, send)):

            def place(i, _, base=base, ref=ref):
                d = owner_of(base + i, me, order_out)
                start = i * R_ROWS
                a_row = pl.multiple_of(d * 16, 16)
                o_row = pl.multiple_of(d * 32, 16)
                for j in range(4):
                    ref[pl.ds(pl.multiple_of(start + 16 * j, 16), 16), :] = grad_attn[
                        pl.ds(a_row, 16), 128 * j : 128 * (j + 1)
                    ].astype(bf16)
                for j in range(8):
                    ref[pl.ds(pl.multiple_of(start + 64 + 16 * j, 16), 16), :] = grad_in[
                        pl.ds(a_row, 16), 128 * j : 128 * (j + 1)
                    ].astype(bf16)
                for j in range(4):
                    ref[pl.ds(pl.multiple_of(start + 192 + 32 * j, 16), 32), :] = grad_out[
                        pl.ds(o_row, 32), 128 * j : 128 * (j + 1)
                    ].astype(bf16)
                return 0

            lax.fori_loop(0, half, place, 0)
        vec_out[...] = jnp.zeros_like(vec_out)
        for i in range(6):
            row = jnp.sum(sums[i], axis=0, keepdims=True)
            for j in range(4):
                vec_out[8 + 4 * i + j : 9 + 4 * i + j, :] = row[:, 128 * j : 128 * (j + 1)]
        row = jnp.sum(hidden_sum[...], axis=0, keepdims=True)
        for j in range(8):
            vec_out[32 + j : 33 + j, :] = row[:, 128 * j : 128 * (j + 1)]


def middle(
    me, tokens, attended, inverse, cotangent, vec, pieces, masks, order_in, order_out, rows=512, sub=256
):
    count = tokens.shape[0]
    by_row = pl.BlockSpec((rows, 512), lambda i: (i, 0))
    half_rows = BLOCKS // 2 * R_ROWS
    return pl.pallas_call(
        functools.partial(middle_kernel, masks, order_in, order_out, sub),
        grid=(count // rows,),
        in_specs=[
            scalar_spec(),
            by_row,
            by_row,
            pl.BlockSpec((HEADS, 1, rows), lambda i: (0, 0, i)),
            by_row,
            whole((48, 128)),
        ]
        + [whole(piece.shape) for piece in pieces],
        out_specs=[
            by_row,
            by_row,
            by_row,
            pl.BlockSpec((rows, 128), lambda i: (i, 0)),
            whole((half_rows, 128)),
            whole((half_rows, 128)),
            whole((48, 128)),
        ],
        out_shape=[
            jax.ShapeDtypeStruct((count, 512), bf16),
            jax.ShapeDtypeStruct((count, 512), bf16),
            jax.ShapeDtypeStruct((count, 512), bf16),
            jax.ShapeDtypeStruct((count, 128), bf16),
            jax.ShapeDtypeStruct((half_rows, 128), bf16),
            jax.ShapeDtypeStruct((half_rows, 128), bf16),
            jax.ShapeDtypeStruct((48, 128), f32),
        ],
        scratch_shapes=[
            pltpu.VMEM((512, 512), bf16),
            pltpu.VMEM((512, FF), bf16),
            pltpu.VMEM((FF, 512), bf16),
            pltpu.VMEM((512, 512), f32),
            pltpu.VMEM((512, FF), f32),
            pltpu.VMEM((FF, 512), f32),
            pltpu.VMEM((6, 8, 512), f32),
            pltpu.VMEM((8, FF), f32),
        ],
        compiler_params=params("middle"),
        cost_estimate=cost(6 * count * 1310720, 22e6, 3 * count * FF),
        name="middle",
    )(me, tokens, attended, inverse, cotangent, vec, *pieces)


def attend_back_kernel(
    base,
    heads,
    order,
    vec_width,
    me_ref,
    tokens,
    weights,
    q,
    k,
    v,
    grad,
    grad_extra,
    vec_in,
    grad_query,
    grad_keys,
    grad_values,
    keep,
    send,
    vec,
    acc,
    all_keys,
    all_values,
    grad_weight,
    held,
    sem,
):
    local = pl.program_id(0)
    step = pl.program_id(1)
    steps = pl.num_programs(1)
    width = k.shape[0]
    last = base + heads == HEADS
    copy = pltpu.make_async_copy(tokens, held, sem)

    @pl.when((local == 0) & (step == 0))
    def _():
        copy.start()
        vec[...] = vec_in[...]

    first_lane = 4 * (base + local)
    lane = lax.broadcasted_iota(jnp.int32, (width, 128), 1)
    ones = jnp.where((lane >= first_lane) & (lane < first_lane + 3), 1.0, 0.0).astype(bf16)
    centred = dot(
        jnp.concatenate([v[...], ones], axis=1), jnp.concatenate([grad[...], grad_extra[...]], axis=1), NT
    )
    grad_scores = (weights[0].astype(f32) * centred).astype(bf16)
    gv = dot(weights[0], grad[...], NN).astype(bf16)
    gk = dot(grad_scores, q[...], NN).astype(bf16)
    grad_values[...] = gv
    grad_keys[...] = gk
    all_values[step] = gv
    all_keys[step] = gk
    part = dot(k[...], grad_scores, TN)

    @pl.when(step == 0)
    def _():
        acc[...] = part

    @pl.when(step > 0)
    def _():
        acc[...] += part

    @pl.when((local == 0) & (step == steps - 1))
    def _():
        copy.wait()

    @pl.when(step == steps - 1)
    def _():
        me = me_ref[0]
        scale = 1.0 / math.sqrt(HEAD_DIM)
        x = held[...]
        gq_all = acc[...].astype(bf16)
        grad_query[...] = gq_all
        gk_all = jnp.concatenate([all_keys[i] for i in range(all_keys.shape[0])], axis=0)
        gv_all = jnp.concatenate([all_values[i] for i in range(all_values.shape[0])], axis=0)
        grad_weight[0:512, :] = dot(gq_all, x, NN).T * scale
        grad_weight[512:1024, :] = dot(gk_all, x, TN).T
        grad_weight[1024:1536, :] = dot(gv_all, x, TN).T
        row_ones = jnp.ones((8, x.shape[0]), bf16)
        vec[pl.ds(base + local, 1), :] = dot(row_ones, gq_all, NT)[0:1] * scale
        vec[pl.ds(4 + base + local, 1), :] = dot(row_ones, gv_all, NN)[0:1]
        half = BLOCKS // 2
        block = heads * QKV_ROWS + (16 if last else 0)
        for start, ref in ((0, keep), (half, send)):

            def place(i, _, start=start, ref=ref):
                d = owner_of(start + i, me, order)
                ref[pl.ds(pl.multiple_of(i * block + local * QKV_ROWS, 16), QKV_ROWS), :] = grad_weight[
                    pl.ds(pl.multiple_of(d * QKV_ROWS, 16), QKV_ROWS), :
                ].astype(bf16)
                if last:
                    pair = vec[pl.ds((d * vec_width) // 128, 2), :]
                    pair = jnp.concatenate([pair, jnp.zeros((14, 128), f32)], axis=0)
                    ref[pl.ds(pl.multiple_of(i * block + heads * QKV_ROWS, 16), 16), :] = pair.astype(bf16)
                return 0

            lax.fori_loop(0, half, place, 0)


def attend_back(me, tokens, weights, qkv, grad_attended, grad_extra, vec, order, vec_width, base, heads, width=1024):
    count = qkv.shape[0]
    half_rows = BLOCKS // 2 * (heads * QKV_ROWS + (16 if base + heads == HEADS else 0))
    return pl.pallas_call(
        functools.partial(attend_back_kernel, base, heads, order, vec_width),
        grid=(heads, count // width),
        in_specs=[
            scalar_spec(),
            pl.BlockSpec(memory_space=pl.ANY),
            pl.BlockSpec((1, width, count), lambda h, i: (base + h, i, 0)),
            pl.BlockSpec((count, 128), lambda h, i: (0, base + h)),
            pl.BlockSpec((width, 128), lambda h, i: (i, HEADS + base + h)),
            pl.BlockSpec((width, 128), lambda h, i: (i, 2 * HEADS + base + h)),
            pl.BlockSpec((count, 128), lambda h, i: (0, base + h)),
            whole((count, 128)),
            whole((48, 128)),
        ],
        out_specs=[
            pl.BlockSpec((128, count), lambda h, i: (h, 0)),
            pl.BlockSpec((width, 128), lambda h, i: (i, h)),
            pl.BlockSpec((width, 128), lambda h, i: (i, h)),
            whole((half_rows, 128)),
            whole((half_rows, 128)),
            whole((48, 128)),
        ],
        out_shape=[
            jax.ShapeDtypeStruct((128 * heads, count), bf16),
            jax.ShapeDtypeStruct((count, 128 * heads), bf16),
            jax.ShapeDtypeStruct((count, 128 * heads), bf16),
            jax.ShapeDtypeStruct((half_rows, 128), bf16),
            jax.ShapeDtypeStruct((half_rows, 128), bf16),
            jax.ShapeDtypeStruct((48, 128), f32),
        ],
        scratch_shapes=[
            pltpu.VMEM((128, count), f32),
            pltpu.VMEM((count // width, width, 128), bf16),
            pltpu.VMEM((count // width, width, 128), bf16),
            pltpu.VMEM((1536, 128), f32),
            pltpu.VMEM((count, 512), bf16),
            pltpu.SemaphoreType.DMA,
        ],
        compiler_params=params("attend_back"),
        cost_estimate=cost(heads * 20 * count * count * 128, heads * 12e6, heads * count * count),
        name="attend_back",
    )(me, tokens, weights, qkv, qkv, qkv, grad_attended, grad_extra, vec)


def input_grad_kernel(groups, *refs):
    grad_branch = refs[0]
    queries, keys, values = [refs[1 + i * groups : 1 + (i + 1) * groups] for i in range(3)]
    weight, out = refs[-2], refs[-1]
    scale = 1.0 / math.sqrt(HEAD_DIM)
    gq = jnp.concatenate([r[...] for r in queries], axis=0)
    gk = jnp.concatenate([r[...] for r in keys], axis=1)
    gv = jnp.concatenate([r[...] for r in values], axis=1)
    total = grad_branch[...].astype(f32) + scale * dot(gq, weight[0:512, :], TT)
    total = total + dot(gk, weight[512:1024, :], NT)
    out[...] = total + dot(gv, weight[1024:1536, :], NT)


def input_grad(grad_branch, queries, keys, values, weight, rows=512):
    count = grad_branch.shape[0]
    by_row = pl.BlockSpec((rows, 512), lambda i: (i, 0))
    return pl.pallas_call(
        functools.partial(input_grad_kernel, len(queries)),
        grid=(count // rows,),
        in_specs=[by_row]
        + [pl.BlockSpec((a.shape[0], rows), lambda i: (0, i)) for a in queries]
        + [pl.BlockSpec((rows, a.shape[1]), lambda i: (i, 0)) for a in keys + values]
        + [whole((1536, 512))],
        out_specs=by_row,
        out_shape=jax.ShapeDtypeStruct((count, 512), f32),
        compiler_params=params("input_grad"),
        cost_estimate=cost(2 * count * 512 * 1536, 16e6),
        name="input_grad",
    )(grad_branch, *queries, *keys, *values, weight)


def unpack_kernel(vec_width, me_ref, *refs):
    q_parts, r_parts = refs[:4], refs[4:6]
    out, vec_out, line = refs[6:]
    q_sum, r_sum = q_parts[0][...], r_parts[0][...]
    for part in q_parts[1:]:
        q_sum = q_sum + part[...].astype(f32)
    for part in r_parts[1:]:
        r_sum = r_sum + part[...].astype(f32)
    at = 0
    source = q_sum
    for index, (start, rows, count) in enumerate(PANELS):
        if index == 1:
            source, at = r_sum, 0
        for j in range(count):
            out[pl.ds(start + j, rows, stride=count), :] = source[at : at + rows, :]
            at += rows
    pair = jnp.concatenate([q_sum[192:200, :], q_sum[193:201, :]], axis=1)
    line[...] = pltpu.roll(pair, 256 - (me_ref[0] * vec_width) % 128, 1)
    vec_out[...] = line[0:1, 0:vec_width]


def unpack(me, q_parts, r_parts, vec_width):
    vmem = pl.BlockSpec(memory_space=pltpu.VMEM)
    return pl.pallas_call(
        functools.partial(unpack_kernel, vec_width),
        in_specs=[scalar_spec()] + [vmem] * 6,
        out_shape=[jax.ShapeDtypeStruct((512, 128), f32), jax.ShapeDtypeStruct((1, vec_width), f32)],
        scratch_shapes=[pltpu.VMEM((8, 256), f32)],
        compiler_params=params("unpack"),
        name="unpack",
    )(me, *q_parts, *r_parts)


def swap(array, step, count):
    return lax.ppermute(array, AXES, [(i, i ^ step) for i in range(count)])


def after(value, *others):
    return lax.optimization_barrier((value, *others))[0]


def quarters(groups):
    parts = []
    for keep, got in groups:
        keep, got = keep.reshape(4, 4, -1, 128), got.reshape(4, 4, -1, 128)
        parts.append([keep[i].astype(f32) + got[i].astype(f32) for i in range(4)])
    totals = [jnp.concatenate(same, axis=1) if len(same) > 1 else same[0] for same in zip(*parts)]
    return totals[0], [total.astype(bf16).reshape(-1, 128) for total in totals[1:]]


def halves(keep, gots):
    total = keep
    for got in gots:
        total = total + got.astype(f32).reshape(keep.shape)
    half = total.shape[0] // 2
    return total[:half], total[half:].astype(bf16).reshape(-1, 128)


def fourths(keep, gots):
    total = keep
    for got in gots:
        total = total + got.astype(f32).reshape(keep.shape)
    return [total[0]] + [total[i].astype(bf16) for i in range(1, 4)]


def fast_layout(dp, fsdp):
    return dp == 4 and fsdp == 8


def gather_line(block, steps, count):
    return jnp.concatenate([block] + [swap(block, step, count) for step in steps], axis=0)


def body(dp, fsdp, tokens, lengths, assignment, weights, vectors, cotangent):
    count = dp * fsdp
    fast = fast_layout(dp, fsdp)
    owner = lax.axis_index(AXES).astype(jnp.int32)
    owned = assignment == owner
    ends = jnp.cumsum(jnp.where(owned, lengths, 0), dtype=jnp.int32)
    ends = jnp.where(owned, ends, 1 << 30)[None, :]
    if fast:
        vec_width = vectors.shape[0]
        core, x_step, y_step, z_near, z_far = fsdp, 1, 2 * fsdp, 2, 4
        planes = [x_step, y_step, x_step + y_step]
        line = [z_near, z_far, z_near + z_far]
        order_in, order_rest = [z_near, z_far], [z_far, z_near]
        order_out = [z_near, z_far, x_step, y_step, core]
        order_rest_out = order_rest + order_out[2:]
        masks = [0] + planes
        masks = masks + [m + core for m in masks]
        me = owner[None]
        q_block, r_block = pack(me, weights.reshape(512, 128), vectors.reshape(1, vec_width), vec_width)
        q_far = gather_line(q_block, line, count)
        q_pieces = [q_far] + [swap(q_far, step, count) for step in planes]
        q_pieces = q_pieces + [swap(piece, core, count) for piece in q_pieces]
        r_far = gather_line(after(r_block, q_far), [z_far], count)
        r_far = gather_line(r_far, [z_near], count)
        r_pieces = [swap(after(r_far, *q_pieces), step, count) for step in planes]
    else:
        vec_width = 160
        order_in, order_rest, order_out = [1, 2], [1, 2], [1, 2, 4, 8, 16]
        order_rest_out = order_out
        masks = [4 * i for i in range(8)]
        me = jnp.zeros((1,), jnp.int32)
        blocks = lax.all_gather(weights, AXES, axis=0, tiled=True).reshape(count, -1)
        flat = lax.all_gather(vectors, AXES, axis=0, tiled=True).reshape(40, 128)
        square = 512 * 512 // count
        cuts = [0, 3 * square, 4 * square, 6 * square, 8 * square]
        panels = []
        for index, (start, rows, width) in enumerate(PANELS):
            piece = blocks[:, cuts[index] : cuts[index + 1]].reshape(BLOCKS, rows, width, 128)
            panels.append(piece.transpose(0, 2, 1, 3).reshape(BLOCKS, rows * width, 128))
        spots = [(d * vec_width) // 128 for d in range(BLOCKS)]
        lanes = jnp.arange(256)
        vec_blocks = []
        for d in range(BLOCKS):
            pair = jnp.concatenate([flat, jnp.zeros((8, 128), bf16)], axis=0)[spots[d] : spots[d] + 2].reshape(256)
            offset = d * vec_width - 128 * spots[d]
            pair = jnp.where((lanes >= offset) & (lanes < offset + vec_width), pair, 0)
            vec_blocks.append(jnp.concatenate([pair.reshape(2, 128), jnp.zeros((14, 128), bf16)], axis=0))
        q_all = jnp.concatenate([panels[0], jnp.stack(vec_blocks)], axis=1)
        r_all = jnp.concatenate(panels[1:], axis=1)
        q_pieces = [q_all[4 * i : 4 * i + 4].reshape(-1, 128) for i in range(8)]
        r_pieces = [r_all[4 * i : 4 * i + 4].reshape(-1, 128) for i in range(8)]
    qkv, keys_extra, query_extra, vec, weight = project(
        me, ends, tokens, q_pieces, masks, order_in, vec_width
    )
    prior = attend(qkv, query_extra, keys_extra, 0, 2, [])
    if fast:
        r_pieces = [r_far] + [after(piece, prior[0]) for piece in r_pieces]
        keys_extra = after(keys_extra, *r_pieces)
        r_pieces = r_pieces + [swap(piece, core, count) for piece in r_pieces]
    attended, probs, inverse = attend(qkv, query_extra, keys_extra, 2, 2, prior)
    layer_output, grad_branch, grad_attended, grad_extra, r_keep, r_send, vec_grad = middle(
        me, tokens, attended, inverse, cotangent, vec, r_pieces, masks, order_rest, order_rest_out
    )
    queries, keys, values, keeps, sends, gots = [], [], [], [], [], []
    if fast:
        r_got = swap(r_send, core, count)
    for base, heads in ((0, 1), (1, 2), (3, 1)):
        gq, gk, gv, keep, send, vec_grad = attend_back(
            me, tokens, probs, qkv, grad_attended, grad_extra, vec_grad, order_out, vec_width, base, heads
        )
        queries.append(gq)
        keys.append(gk)
        values.append(gv)
        keeps.append(keep)
        sends.append(send)
        if not fast:
            continue
        gots.append(swap(send, core, count))
        if base == 0:
            r_keep, r_sends = quarters([(r_keep, after(r_got, gq))])
            vec_grad = after(vec_grad, *r_sends)
            r_gots = [swap(part, step, count) for part, step in zip(r_sends, planes)]
        elif base == 1:
            r_gots = [after(part, gq) for part in r_gots]
            r_keep, r_send = halves(r_keep, r_gots)
            vec_grad = after(vec_grad, r_send)
            r_got = swap(r_send, z_near, count)
    if fast:
        r_keep, r_send = halves(r_keep, [after(r_got, gq)])
        r_parts = [r_keep.reshape(-1, 128), swap(r_send, z_far, count)]
        gots = [after(got, gq) for got in gots]
        q_keep, q_sends = quarters(list(zip(keeps, gots)))
        grad_branch = after(grad_branch, *q_sends)
        q_gots = [swap(part, step, count) for part, step in zip(q_sends, planes)]
    grad_tokens = input_grad(grad_branch, queries, keys, values, weight)
    if fast:
        q_gots = [after(part, grad_tokens) for part in q_gots]
        q_parts = fourths(q_keep, q_gots)
        q_parts = q_parts[:1] + [swap(part, step, count) for part, step in zip(q_parts[1:], line)]
        own_weights, own_vectors = unpack(me, q_parts, r_parts, vec_width)
        own_weights = own_weights.reshape(-1)
        own_vectors = own_vectors.reshape(-1)
    else:
        heads = [jnp.concatenate([k, g], axis=0).astype(f32).reshape(BLOCKS, -1, 128) for k, g in zip(keeps, sends)]
        q_all = jnp.concatenate(heads, axis=1)
        r_all = jnp.concatenate([r_keep, r_send], axis=0).astype(f32).reshape(BLOCKS, R_ROWS, 128)
        sources = (q_all[:, : 4 * QKV_ROWS], r_all[:, :64], r_all[:, 64:192], r_all[:, 192:])
        pieces = []
        for source, (start, rows, width) in zip(sources, PANELS):
            piece = source.reshape(BLOCKS, width, rows, 128).transpose(0, 2, 1, 3)
            pieces.append(piece.reshape(count, -1))
        own_weights = lax.psum_scatter(
            jnp.concatenate(pieces, axis=1).reshape(-1), AXES, scatter_dimension=0, tiled=True
        )
        pairs = q_all[:, 4 * QKV_ROWS : 4 * QKV_ROWS + 2].reshape(BLOCKS, 256)
        rows = [
            pairs[d, (d * vec_width) % 128 : (d * vec_width) % 128 + vec_width] for d in range(BLOCKS)
        ]
        own_vectors = lax.psum_scatter(jnp.concatenate(rows), AXES, scatter_dimension=0, tiled=True)
    return (layer_output, grad_tokens, own_weights, own_vectors)


def solution(mesh):
    dp, fsdp = mesh.shape["dp"], mesh.shape["fsdp"]
    in_specs = (
        P(AXES, None),
        P(),
        P(),
        P(AXES),
        P(AXES),
        P(AXES, None),
    )
    out_specs = (
        P(AXES, None),
        P(AXES, None),
        P(AXES),
        P(AXES),
    )
    return jax.shard_map(
        functools.partial(body, dp, fsdp), mesh=mesh, in_specs=in_specs, out_specs=out_specs, check_vma=False
    )
```

```python
import functools
import math

import jax
import jax.numpy as jnp
from jax import lax
from jax.experimental import pallas as pl
from jax.experimental.pallas import tpu as pltpu
from jax.sharding import PartitionSpec as P

HEADS = 4
HEAD_DIM = 128
FF = 1024
AXES = ("dp", "fsdp")
NORM_EPS = 1e-05
BLOCKS = 32
QKV_ROWS = 48
Q_ROWS = 4 * QKV_ROWS + 16
R_ROWS = 320
FAR = -1e30
f32 = jnp.float32
bf16 = jnp.bfloat16
NT = (((1,), (1,)), ((), ()))
NN = (((1,), (0,)), ((), ()))
TN = (((0,), (0,)), ((), ()))
TT = (((0,), (1,)), ((), ()))
VMEM_MIB = {"pack": 2, "project": 14, "attend": 18, "middle": 26, "attend_back": 28, "input_grad": 14, "unpack": 3}


def dot(a, b, dims):
    return lax.dot_general(a, b, dims, preferred_element_type=f32)


def params(name):
    return pltpu.CompilerParams(vmem_limit_bytes=VMEM_MIB[name] << 20)


def cost(flops, moved, special=0):
    return pl.CostEstimate(flops=int(flops), bytes_accessed=int(moved), transcendentals=int(special))


def whole(shape):
    return pl.BlockSpec(shape, lambda *_: (0,) * len(shape))


def scalar_spec():
    return pl.BlockSpec(memory_space=pltpu.SMEM)


def owner_of(place, me, order):
    mask = 0
    for bit, step in enumerate(order):
        mask = mask + ((place >> bit) & 1) * step
    return jnp.bitwise_xor(me, mask)


def split3(value):
    high = value.astype(bf16)
    rest = value - high.astype(f32)
    middle = rest.astype(bf16)
    low = (rest - middle.astype(f32)).astype(bf16)
    return high, middle, low


PANELS = ((0, 48, 4), (192, 16, 4), (256, 16, 8), (384, 32, 4))


def pack_kernel(vec_width, me_ref, flat, vec, q_out, r_out, wide, line):
    wide[...] = flat[...].astype(f32)
    line[...] = jnp.zeros_like(line)
    line[0:1, 0:vec_width] = vec[...].astype(f32)
    shifted = pltpu.roll(line[...], (me_ref[0] * vec_width) % 128, 1)
    parts = []
    for start, rows, count in PANELS:
        for j in range(count):
            parts.append(wide[pl.ds(start + j, rows, stride=count), :].astype(bf16))
    q_out[0:192, :] = jnp.concatenate(parts[:4], axis=0)
    placed = jnp.concatenate([shifted[0:1, 0:128], shifted[0:1, 128:256], jnp.zeros((14, 128), f32)], axis=0)
    q_out[192:208, :] = placed.astype(bf16)
    r_out[...] = jnp.concatenate(parts[4:], axis=0)


def pack(me, flat, vec, vec_width):
    vmem = pl.BlockSpec(memory_space=pltpu.VMEM)
    return pl.pallas_call(
        functools.partial(pack_kernel, vec_width),
        in_specs=[scalar_spec(), vmem, vmem],
        out_shape=[
            jax.ShapeDtypeStruct((Q_ROWS, 128), bf16),
            jax.ShapeDtypeStruct((R_ROWS, 128), bf16),
        ],
        scratch_shapes=[pltpu.VMEM((512, 128), f32), pltpu.VMEM((8, 256), f32)],
        compiler_params=params("pack"),
        name="pack",
    )(me, flat, vec)


def project_kernel(masks, order, vec_width, me_ref, ends, tokens, *refs):
    pieces = refs[: len(masks)]
    qkv, keys_extra, query_extra, vec_out, weight, vec = refs[len(masks) :]
    step = pl.program_id(0)
    rows = tokens.shape[0]
    me = me_ref[0]

    @pl.when(step == 0)
    def _():
        vec[...] = jnp.zeros_like(vec)
        for mask, ref in zip(masks, pieces):
            for i in range(1 << len(order)):
                d = owner_of(i, jnp.bitwise_xor(me, mask), order)
                row = pl.multiple_of(d * QKV_ROWS, 16)
                for j in range(4):
                    at = i * Q_ROWS + QKV_ROWS * j
                    weight[pl.ds(row, QKV_ROWS), 128 * j : 128 * (j + 1)] = ref[at : at + QKV_ROWS, :]
                row = (d * vec_width) // 128
                at = i * Q_ROWS + 4 * QKV_ROWS
                vec[pl.ds(row, 2), :] = vec[pl.ds(row, 2), :] + ref[at : at + 16, :].astype(f32)[0:2, :]
        vec_out[...] = vec[...]

    x = tokens[...]
    scale = 1.0 / math.sqrt(HEAD_DIM)
    query_bias = jnp.concatenate([vec[j : j + 1, :] for j in range(4)], axis=1)
    value_bias = jnp.concatenate([vec[4 + j : 5 + j, :] for j in range(4)], axis=1)
    queries = ((dot(x, weight[0:512, :], NN) + query_bias) * scale).astype(bf16)
    key_heads = dot(x, weight[512:1024, :], NN).astype(bf16)
    values = (dot(x, weight[1024:1536, :], NN) + value_bias).astype(bf16)
    qkv[:, 0:512] = queries
    qkv[:, 512:1024] = key_heads
    qkv[:, 1024:1536] = values
    places = step * rows + lax.broadcasted_iota(jnp.int32, (rows, ends.shape[1]), 0)
    label = jnp.sum((ends[...] <= places).astype(f32), axis=1, keepdims=True)
    lane = lax.broadcasted_iota(jnp.int32, (rows, 128), 1)
    same = lane.astype(f32) == label
    keys_extra[...] = jnp.where(lane < 8, jnp.where(same, 1.0, 0.0), jnp.where(lane < 32, 1.0, 0.0)).astype(bf16)
    apart = jnp.where((lane < 8) & jnp.logical_not(same), FAR, 0.0)
    product = queries.astype(f32) * key_heads.astype(f32)
    extra = apart
    for h in range(HEADS):
        own = jnp.sum(product[:, 128 * h : 128 * (h + 1)], axis=1, keepdims=True)
        extra = jnp.where(lane == 8 + h, -own, extra)
    query_extra[...] = extra.astype(bf16)


def project(me, ends, tokens, pieces, masks, order, vec_width, rows=512):
    count = tokens.shape[0]
    sets = ends.shape[1]
    return pl.pallas_call(
        functools.partial(project_kernel, masks, order, vec_width),
        grid=(count // rows,),
        in_specs=[
            scalar_spec(),
            whole((1, sets)),
            pl.BlockSpec((rows, 512), lambda i: (i, 0)),
        ]
        + [whole(piece.shape) for piece in pieces],
        out_specs=[
            pl.BlockSpec((rows, 1536), lambda i: (i, 0)),
            pl.BlockSpec((rows, 128), lambda i: (i, 0)),
            pl.BlockSpec((rows, 128), lambda i: (i, 0)),
            whole((48, 128)),
            whole((1536, 512)),
        ],
        out_shape=[
            jax.ShapeDtypeStruct((count, 1536), bf16),
            jax.ShapeDtypeStruct((count, 128), bf16),
            jax.ShapeDtypeStruct((count, 128), bf16),
            jax.ShapeDtypeStruct((48, 128), f32),
            jax.ShapeDtypeStruct((1536, 512), bf16),
        ],
        scratch_shapes=[pltpu.VMEM((48, 128), f32)],
        compiler_params=params("project"),
        cost_estimate=cost(2 * count * 512 * 1536, 12e6),
        name="project",
    )(me, ends, tokens, *pieces)


def own_lanes(lane, head):
    return (lane < 8) | (lane == 8 + head) | ((lane >= 16 + 4 * head) & (lane < 19 + 4 * head))


def attend_kernel(base, q, k, v, query_extra, keys_extra, *refs):
    attended, offset_out, total, mixed, peak = refs[-5:]
    rows = q.shape[0]
    head = base + pl.program_id(0)
    lane = lax.broadcasted_iota(jnp.int32, (rows, 128), 1)
    extra = jnp.where(own_lanes(lane, head), query_extra[...].astype(f32), 0.0).astype(bf16)
    left = jnp.concatenate([k[...], keys_extra[...]], axis=1)
    right = jnp.concatenate([q[...], extra], axis=1)
    weights = jnp.exp(dot(left, right, NT))
    total[...] = jnp.sum(weights, axis=0, keepdims=True)
    mixed[...] = dot(v[...], weights.astype(bf16), TN)
    peak[...] = jnp.zeros_like(peak)
    good = (total[...] > 1e-20) & (total[...] < 1e30)

    @pl.when(jnp.sum(jnp.where(good, 0.0, 1.0)) > 0.0)
    def _():
        again = dot(left, right, NT)
        top = jnp.max(again, axis=0, keepdims=True)
        safe = jnp.exp(again - top)
        total[...] = jnp.sum(safe, axis=0, keepdims=True)
        mixed[...] = dot(v[...], safe.astype(bf16), TN)
        peak[...] = top

    attended[...] = (mixed[...] * (1.0 / total[...])).T.astype(bf16)
    offset_out[0] = peak[...] + jnp.log(total[...])


def attend(qkv, query_extra, keys_extra, base, heads, prior, rows=1024):
    count = qkv.shape[0]
    return pl.pallas_call(
        functools.partial(attend_kernel, base),
        grid=(heads, count // rows),
        in_specs=[
            pl.BlockSpec((rows, 128), lambda h, i: (i, base + h)),
            pl.BlockSpec((count, 128), lambda h, i: (0, HEADS + base + h)),
            pl.BlockSpec((count, 128), lambda h, i: (0, 2 * HEADS + base + h)),
            pl.BlockSpec((rows, 128), lambda h, i: (i, 0)),
            pl.BlockSpec((count, 128), lambda h, i: (0, 0)),
        ]
        + [pl.BlockSpec(memory_space=pl.ANY) for _ in prior],
        out_specs=[
            pl.BlockSpec((rows, 128), lambda h, i: (i, base + h)),
            pl.BlockSpec((1, 1, rows), lambda h, i: (base + h, 0, i)),
        ],
        out_shape=[
            jax.ShapeDtypeStruct((count, 128 * HEADS), bf16),
            jax.ShapeDtypeStruct((HEADS, 1, count), f32),
        ],
        scratch_shapes=[pltpu.VMEM((1, rows), f32), pltpu.VMEM((128, rows), f32), pltpu.VMEM((1, rows), f32)],
        input_output_aliases={5: 0, 6: 1} if prior else {},
        compiler_params=params("attend"),
        cost_estimate=cost(heads * 8 * count * count * 128, 6e6, heads * count * count),
        name="attend",
    )(qkv, qkv, qkv, query_extra, keys_extra, *prior)


def mean_row(value):
    return jnp.sum(value, axis=1, keepdims=True) * (1.0 / value.shape[1])


def norm_rows(summed):
    centered = summed - mean_row(summed)
    inverse = lax.rsqrt(mean_row(centered * centered) + NORM_EPS)
    return centered * inverse, inverse


def norm_back(grad, normed, inverse):
    return inverse * (grad - mean_row(grad) - normed * mean_row(grad * normed))


def fold8(value):
    return jnp.sum(value.reshape(value.shape[0] // 8, 8, value.shape[1]), axis=0)


def middle_kernel(masks, order_in, order_out, sub, me_ref, tokens, attended, offset, query_extra, cotangent, vec, *refs):
    pieces = refs[: len(masks)]
    layer_output, grad_branch_out, grad_attended_out, grad_extra, query_extra_out, keep, send, vec_out = refs[
        len(masks) : -8
    ]
    attn_weight, in_weight, out_weight, grad_attn, grad_in, grad_out, sums, hidden_sum = refs[-8:]
    step = pl.program_id(0)
    me = me_ref[0]
    half = BLOCKS // 2

    @pl.when(step == 0)
    def _():
        for mask, ref in zip(masks, pieces):

            def place(i, _, mask=mask, ref=ref):
                d = owner_of(i, jnp.bitwise_xor(me, mask), order_in)
                start = i * R_ROWS
                a_row = pl.multiple_of(d * 16, 16)
                o_row = pl.multiple_of(d * 32, 16)
                for j in range(4):
                    attn_weight[pl.ds(a_row, 16), 128 * j : 128 * (j + 1)] = ref[
                        pl.ds(pl.multiple_of(start + 16 * j, 16), 16), :
                    ]
                for j in range(8):
                    in_weight[pl.ds(a_row, 16), 128 * j : 128 * (j + 1)] = ref[
                        pl.ds(pl.multiple_of(start + 64 + 16 * j, 16), 16), :
                    ]
                for j in range(4):
                    out_weight[pl.ds(o_row, 32), 128 * j : 128 * (j + 1)] = ref[
                        pl.ds(pl.multiple_of(start + 192 + 32 * j, 16), 32), :
                    ]
                return 0

            lax.fori_loop(0, 1 << len(order_in), place, 0, unroll=True)
        grad_attn[...] = jnp.zeros_like(grad_attn)
        grad_in[...] = jnp.zeros_like(grad_in)
        grad_out[...] = jnp.zeros_like(grad_out)
        sums[...] = jnp.zeros_like(sums)
        hidden_sum[...] = jnp.zeros_like(hidden_sum)

    def row_of(index):
        return jnp.concatenate([vec[4 * index + j : 4 * index + j + 1, :] for j in range(4)], axis=1)

    attn_bias, ffn_bias, gain_one, shift_one, gain_two, shift_two = [row_of(i) for i in range(2, 8)]
    hidden_bias = jnp.concatenate([vec[32 + j : 33 + j, :] for j in range(8)], axis=1)

    offset_rows = jnp.concatenate([offset[h] for h in range(HEADS)] + [jnp.zeros((4, tokens.shape[0]), f32)], axis=0)
    offsets = offset_rows.T
    lane = lax.broadcasted_iota(jnp.int32, (tokens.shape[0], 128), 1)
    extra = query_extra[...].astype(f32)
    for h in range(HEADS):
        for i, part in enumerate(split3(-offsets[:, h : h + 1])):
            extra = jnp.where(lane == 16 + 4 * h + i, part.astype(f32), extra)
    query_extra_out[...] = extra.astype(bf16)

    kept = [{} for _ in range(tokens.shape[0] // sub)]

    def chain(s):
        sl = slice(s * sub, (s + 1) * sub)
        att = attended[sl, :]
        branch = dot(att, attn_weight[...], NN) + attn_bias
        yield
        normed_one, inverse_one = norm_rows(tokens[sl, :].astype(f32) + branch)
        hidden = normed_one * gain_one + shift_one
        hidden_low = hidden.astype(bf16)
        yield
        pre_act = dot(hidden_low, in_weight[...], NN) + hidden_bias
        yield
        cdf = 0.5 * (1.0 + lax.erf(pre_act * 0.7071067811865476))
        density = jnp.exp(-0.5 * pre_act * pre_act) * 0.3989422804014327
        activated = (pre_act * cdf).astype(bf16)
        slope = cdf + pre_act * density
        yield
        ffn_result = dot(activated, out_weight[...], NN) + ffn_bias
        yield
        normed_two, inverse_two = norm_rows(hidden + ffn_result)
        layer_output[sl, :] = (normed_two * gain_two + shift_two).astype(bf16)
        grad_result = cotangent[sl, :].astype(f32)
        sums[4] += fold8(grad_result * normed_two)
        sums[5] += fold8(grad_result)
        grad_second = norm_back(grad_result * gain_two, normed_two, inverse_two)
        grad_ffn = grad_second.astype(bf16)
        sums[1] += fold8(grad_ffn.astype(f32))
        yield
        grad_activated = dot(grad_ffn, out_weight[...], NT)
        kept[s][0] = (activated, grad_ffn)
        yield
        grad_pre = (grad_activated * slope).astype(bf16)
        hidden_sum[...] += fold8(grad_pre.astype(f32))
        yield
        grad_hidden = grad_second + dot(grad_pre, in_weight[...], NT)
        kept[s][1] = (hidden_low, grad_pre)
        yield
        sums[2] += fold8(grad_hidden * normed_one)
        sums[3] += fold8(grad_hidden)
        grad_first = norm_back(grad_hidden * gain_one, normed_one, inverse_one)
        grad_branch = grad_first.astype(bf16)
        grad_branch_out[sl, :] = grad_branch
        sums[0] += fold8(grad_branch.astype(f32))
        yield
        grad_attended = dot(grad_branch, attn_weight[...], NT)
        kept[s][2] = (att, grad_branch)
        yield
        low = grad_attended.astype(bf16)
        grad_attended_out[sl, :] = low
        lane = lax.broadcasted_iota(jnp.int32, (sub, 128), 1)
        extra = jnp.zeros((sub, 128), f32)
        for h in range(HEADS):
            cols = slice(128 * h, 128 * (h + 1))
            low_cols = low[:, cols].astype(f32)
            centre = jnp.sum(low_cols * att[:, cols].astype(f32), axis=1, keepdims=True)
            for i, part in enumerate(split3(-centre)):
                extra = jnp.where(lane == 4 * h + i, part.astype(f32), extra)
        grad_extra[sl, :] = extra.astype(bf16)
        yield

    chains = [chain(s) for s in range(tokens.shape[0] // sub)]
    started = 0
    live = []
    while started < len(chains) or live:
        if started < len(chains):
            live.append(chains[started])
            started += 1
        remaining = []
        for c in live:
            try:
                next(c)
                remaining.append(c)
            except StopIteration:
                pass
        live = remaining
        for i, ref in enumerate((grad_out, grad_in, grad_attn)):
            if all(i in k for k in kept):
                left = jnp.concatenate([k[i][0] for k in kept], axis=0)
                right = jnp.concatenate([k.pop(i)[1] for k in kept], axis=0)
                ref[...] += dot(left, right, TN)

    @pl.when(step == pl.num_programs(0) - 1)
    def _():
        for base, ref in ((0, keep), (half, send)):

            def place(i, _, base=base, ref=ref):
                d = owner_of(base + i, me, order_out)
                start = i * R_ROWS
                a_row = pl.multiple_of(d * 16, 16)
                o_row = pl.multiple_of(d * 32, 16)
                for j in range(4):
                    ref[pl.ds(pl.multiple_of(start + 16 * j, 16), 16), :] = grad_attn[
                        pl.ds(a_row, 16), 128 * j : 128 * (j + 1)
                    ].astype(bf16)
                for j in range(8):
                    ref[pl.ds(pl.multiple_of(start + 64 + 16 * j, 16), 16), :] = grad_in[
                        pl.ds(a_row, 16), 128 * j : 128 * (j + 1)
                    ].astype(bf16)
                for j in range(4):
                    ref[pl.ds(pl.multiple_of(start + 192 + 32 * j, 16), 32), :] = grad_out[
                        pl.ds(o_row, 32), 128 * j : 128 * (j + 1)
                    ].astype(bf16)
                return 0

            lax.fori_loop(0, half, place, 0, unroll=4)
        vec_out[...] = jnp.zeros_like(vec_out)
        for i in range(6):
            row = jnp.sum(sums[i], axis=0, keepdims=True)
            for j in range(4):
                vec_out[8 + 4 * i + j : 9 + 4 * i + j, :] = row[:, 128 * j : 128 * (j + 1)]
        row = jnp.sum(hidden_sum[...], axis=0, keepdims=True)
        for j in range(8):
            vec_out[32 + j : 33 + j, :] = row[:, 128 * j : 128 * (j + 1)]


def middle(
    me, tokens, attended, offset, query_extra, cotangent, vec, pieces, masks, order_in, order_out, rows=512, sub=256
):
    count = tokens.shape[0]
    by_row = pl.BlockSpec((rows, 512), lambda i: (i, 0))
    half_rows = BLOCKS // 2 * R_ROWS
    return pl.pallas_call(
        functools.partial(middle_kernel, masks, order_in, order_out, sub),
        grid=(count // rows,),
        in_specs=[
            scalar_spec(),
            by_row,
            by_row,
            pl.BlockSpec((HEADS, 1, rows), lambda i: (0, 0, i)),
            pl.BlockSpec((rows, 128), lambda i: (i, 0)),
            by_row,
            whole((48, 128)),
        ]
        + [whole(piece.shape) for piece in pieces],
        out_specs=[
            by_row,
            by_row,
            by_row,
            pl.BlockSpec((rows, 128), lambda i: (i, 0)),
            pl.BlockSpec((rows, 128), lambda i: (i, 0)),
            whole((half_rows, 128)),
            whole((half_rows, 128)),
            whole((48, 128)),
        ],
        out_shape=[
            jax.ShapeDtypeStruct((count, 512), bf16),
            jax.ShapeDtypeStruct((count, 512), bf16),
            jax.ShapeDtypeStruct((count, 512), bf16),
            jax.ShapeDtypeStruct((count, 128), bf16),
            jax.ShapeDtypeStruct((count, 128), bf16),
            jax.ShapeDtypeStruct((half_rows, 128), bf16),
            jax.ShapeDtypeStruct((half_rows, 128), bf16),
            jax.ShapeDtypeStruct((48, 128), f32),
        ],
        scratch_shapes=[
            pltpu.VMEM((512, 512), bf16),
            pltpu.VMEM((512, FF), bf16),
            pltpu.VMEM((FF, 512), bf16),
            pltpu.VMEM((512, 512), f32),
            pltpu.VMEM((512, FF), f32),
            pltpu.VMEM((FF, 512), f32),
            pltpu.VMEM((6, 8, 512), f32),
            pltpu.VMEM((8, FF), f32),
        ],
        compiler_params=params("middle"),
        cost_estimate=cost(6 * count * 1310720, 22e6, 3 * count * FF),
        name="middle",
    )(me, tokens, attended, offset, query_extra, cotangent, vec, *pieces)


def attend_back_kernel(
    base,
    heads,
    order,
    vec_width,
    me_ref,
    tokens,
    q,
    k,
    v,
    grad,
    query_extra,
    keys_extra,
    grad_extra,
    vec_in,
    grad_query,
    grad_keys,
    grad_values,
    keep,
    send,
    vec,
    acc,
    all_keys,
    all_values,
    grad_weight,
    held,
    sem,
):
    local = pl.program_id(0)
    step = pl.program_id(1)
    steps = pl.num_programs(1)
    width = k.shape[0]
    last = base + heads == HEADS
    copy = pltpu.make_async_copy(tokens, held, sem)

    @pl.when((local == 0) & (step == 0))
    def _():
        copy.start()
        vec[...] = vec_in[...]

    head = base + local
    lane = lax.broadcasted_iota(jnp.int32, (width, 128), 1)
    ones = jnp.where((lane >= 4 * head) & (lane < 4 * head + 3), 1.0, 0.0).astype(bf16)
    extra = jnp.where(own_lanes(lane, head), keys_extra[...].astype(f32), 0.0).astype(bf16)
    scores = dot(
        jnp.concatenate([q[...], query_extra[...]], axis=1), jnp.concatenate([k[...], extra], axis=1), NT
    )
    centred = dot(
        jnp.concatenate([grad[...], grad_extra[...]], axis=1), jnp.concatenate([v[...], ones], axis=1), NT
    )
    probs = jnp.exp(scores)
    probs_low = probs.astype(bf16)
    grad_scores = (probs * centred).astype(bf16)
    gv = dot(grad[...], probs_low, TN).astype(bf16)
    gk = dot(q[...], grad_scores, TN).astype(bf16)
    grad_values[...] = gv
    grad_keys[...] = gk
    all_values[step] = gv
    all_keys[step] = gk
    part = dot(grad_scores, k[...], NN)

    @pl.when(step == 0)
    def _():
        acc[...] = part

    @pl.when(step > 0)
    def _():
        acc[...] += part

    @pl.when((local == 0) & (step == steps - 1))
    def _():
        copy.wait()

    @pl.when(step == steps - 1)
    def _():
        me = me_ref[0]
        scale = 1.0 / math.sqrt(HEAD_DIM)
        x = held[...]
        gq_all = acc[...].astype(bf16)
        grad_query[...] = gq_all
        gk_all = jnp.concatenate([all_keys[i] for i in range(all_keys.shape[0])], axis=1)
        gv_all = jnp.concatenate([all_values[i] for i in range(all_values.shape[0])], axis=1)
        grad_weight[0:512, :] = dot(gq_all, x, TN).T * scale
        grad_weight[512:1024, :] = dot(gk_all, x, NN).T
        grad_weight[1024:1536, :] = dot(gv_all, x, NN).T
        row_ones = jnp.ones((8, x.shape[0]), bf16)
        vec[pl.ds(base + local, 1), :] = dot(row_ones, gq_all, NN)[0:1] * scale
        vec[pl.ds(4 + base + local, 1), :] = dot(row_ones, gv_all, NT)[0:1]
        half = BLOCKS // 2
        block = heads * QKV_ROWS + (16 if last else 0)
        for start, ref in ((0, keep), (half, send)):

            def place(i, _, start=start, ref=ref):
                d = owner_of(start + i, me, order)
                ref[pl.ds(pl.multiple_of(i * block + local * QKV_ROWS, 16), QKV_ROWS), :] = grad_weight[
                    pl.ds(pl.multiple_of(d * QKV_ROWS, 16), QKV_ROWS), :
                ].astype(bf16)
                if last:
                    pair = vec[pl.ds((d * vec_width) // 128, 2), :]
                    pair = jnp.concatenate([pair, jnp.zeros((14, 128), f32)], axis=0)
                    ref[pl.ds(pl.multiple_of(i * block + heads * QKV_ROWS, 16), 16), :] = pair.astype(bf16)
                return 0

            lax.fori_loop(0, half, place, 0, unroll=4)


def attend_back(
    me, tokens, qkv, grad_attended, query_extra, keys_extra, grad_extra, vec, order, vec_width, base, heads, width=1024
):
    count = qkv.shape[0]
    half_rows = BLOCKS // 2 * (heads * QKV_ROWS + (16 if base + heads == HEADS else 0))
    return pl.pallas_call(
        functools.partial(attend_back_kernel, base, heads, order, vec_width),
        grid=(heads, count // width),
        in_specs=[
            scalar_spec(),
            pl.BlockSpec(memory_space=pl.ANY),
            pl.BlockSpec((count, 128), lambda h, i: (0, base + h)),
            pl.BlockSpec((width, 128), lambda h, i: (i, HEADS + base + h)),
            pl.BlockSpec((width, 128), lambda h, i: (i, 2 * HEADS + base + h)),
            pl.BlockSpec((count, 128), lambda h, i: (0, base + h)),
            whole((count, 128)),
            pl.BlockSpec((width, 128), lambda h, i: (i, 0)),
            whole((count, 128)),
            whole((48, 128)),
        ],
        out_specs=[
            pl.BlockSpec((count, 128), lambda h, i: (0, h)),
            pl.BlockSpec((128, width), lambda h, i: (h, i)),
            pl.BlockSpec((128, width), lambda h, i: (h, i)),
            whole((half_rows, 128)),
            whole((half_rows, 128)),
            whole((48, 128)),
        ],
        out_shape=[
            jax.ShapeDtypeStruct((count, 128 * heads), bf16),
            jax.ShapeDtypeStruct((128 * heads, count), bf16),
            jax.ShapeDtypeStruct((128 * heads, count), bf16),
            jax.ShapeDtypeStruct((half_rows, 128), bf16),
            jax.ShapeDtypeStruct((half_rows, 128), bf16),
            jax.ShapeDtypeStruct((48, 128), f32),
        ],
        scratch_shapes=[
            pltpu.VMEM((count, 128), f32),
            pltpu.VMEM((count // width, 128, width), bf16),
            pltpu.VMEM((count // width, 128, width), bf16),
            pltpu.VMEM((1536, 128), f32),
            pltpu.VMEM((count, 512), bf16),
            pltpu.SemaphoreType.DMA,
        ],
        compiler_params=params("attend_back"),
        cost_estimate=cost(heads * 20 * count * count * 128, heads * 12e6, heads * count * count),
        name="attend_back",
    )(me, tokens, qkv, qkv, qkv, grad_attended, query_extra, keys_extra, grad_extra, vec)


def input_grad_kernel(groups, *refs):
    grad_branch = refs[0]
    queries, keys, values = [refs[1 + i * groups : 1 + (i + 1) * groups] for i in range(3)]
    weight, out = refs[-2], refs[-1]
    scale = 1.0 / math.sqrt(HEAD_DIM)
    gq = jnp.concatenate([r[...] for r in queries], axis=1)
    gk = jnp.concatenate([r[...] for r in keys], axis=0)
    gv = jnp.concatenate([r[...] for r in values], axis=0)
    total = grad_branch[...].astype(f32) + scale * dot(gq, weight[0:512, :], NT)
    total = total + dot(gk, weight[512:1024, :], TT)
    out[...] = total + dot(gv, weight[1024:1536, :], TT)


def input_grad(grad_branch, queries, keys, values, weight, rows=512):
    count = grad_branch.shape[0]
    by_row = pl.BlockSpec((rows, 512), lambda i: (i, 0))
    return pl.pallas_call(
        functools.partial(input_grad_kernel, len(queries)),
        grid=(count // rows,),
        in_specs=[by_row]
        + [pl.BlockSpec((rows, a.shape[1]), lambda i: (i, 0)) for a in queries]
        + [pl.BlockSpec((a.shape[0], rows), lambda i: (0, i)) for a in keys + values]
        + [whole((1536, 512))],
        out_specs=by_row,
        out_shape=jax.ShapeDtypeStruct((count, 512), f32),
        compiler_params=params("input_grad"),
        cost_estimate=cost(2 * count * 512 * 1536, 16e6),
        name="input_grad",
    )(grad_branch, *queries, *keys, *values, weight)


def unpack_kernel(vec_width, me_ref, *refs):
    q_parts, r_parts = refs[:4], refs[4:6]
    out, vec_out, line = refs[6:]
    q_sum, r_sum = q_parts[0][...], r_parts[0][...]
    for part in q_parts[1:]:
        q_sum = q_sum + part[...].astype(f32)
    for part in r_parts[1:]:
        r_sum = r_sum + part[...].astype(f32)
    at = 0
    source = q_sum
    for index, (start, rows, count) in enumerate(PANELS):
        if index == 1:
            source, at = r_sum, 0
        for j in range(count):
            out[pl.ds(start + j, rows, stride=count), :] = source[at : at + rows, :]
            at += rows
    pair = jnp.concatenate([q_sum[192:200, :], q_sum[193:201, :]], axis=1)
    line[...] = pltpu.roll(pair, 256 - (me_ref[0] * vec_width) % 128, 1)
    vec_out[...] = line[0:1, 0:vec_width]


def unpack(me, q_parts, r_parts, vec_width):
    vmem = pl.BlockSpec(memory_space=pltpu.VMEM)
    return pl.pallas_call(
        functools.partial(unpack_kernel, vec_width),
        in_specs=[scalar_spec()] + [vmem] * 6,
        out_shape=[jax.ShapeDtypeStruct((512, 128), f32), jax.ShapeDtypeStruct((1, vec_width), f32)],
        scratch_shapes=[pltpu.VMEM((8, 256), f32)],
        compiler_params=params("unpack"),
        name="unpack",
    )(me, *q_parts, *r_parts)


def swap(array, step, count):
    return lax.ppermute(array, AXES, [(i, i ^ step) for i in range(count)])


def swap_each(parts, steps, count):
    pairs = list(zip(parts, steps))
    return [swap(part, step, count) for part, step in pairs[::-1]][::-1]


def after(value, *others):
    return lax.optimization_barrier((value, *others))[0]


def quarters(groups):
    parts = []
    for keep, got in groups:
        keep, got = keep.reshape(4, 4, -1, 128), got.reshape(4, 4, -1, 128)
        parts.append([keep[i].astype(f32) + got[i].astype(f32) for i in range(4)])
    totals = [jnp.concatenate(same, axis=1) if len(same) > 1 else same[0] for same in zip(*parts)]
    return totals[0], [total.astype(bf16).reshape(-1, 128) for total in totals[1:]]


def halves(keep, gots):
    total = keep
    for got in gots:
        total = total + got.astype(f32).reshape(keep.shape)
    half = total.shape[0] // 2
    return total[:half], total[half:].astype(bf16).reshape(-1, 128)


def fourths(keep, gots):
    total = keep
    for got in gots:
        total = total + got.astype(f32).reshape(keep.shape)
    return [total[0]] + [total[i].astype(bf16) for i in range(1, 4)]


def fast_layout(dp, fsdp):
    return dp == 4 and fsdp == 8


def gather_line(block, steps, count):
    return jnp.concatenate([block] + [swap(block, step, count) for step in steps], axis=0)


def body(dp, fsdp, tokens, lengths, assignment, weights, vectors, cotangent):
    count = dp * fsdp
    fast = fast_layout(dp, fsdp)
    owner = lax.axis_index(AXES).astype(jnp.int32)
    owned = assignment == owner
    ends = jnp.cumsum(jnp.where(owned, lengths, 0), dtype=jnp.int32)
    ends = jnp.where(owned, ends, 1 << 30)[None, :]
    if fast:
        vec_width = vectors.shape[0]
        core, x_step, y_step, z_near, z_far = fsdp, 1, 2 * fsdp, 2, 4
        planes = [x_step, y_step, x_step + y_step]
        spread = [x_step + y_step, y_step, x_step]
        line = [z_near, z_far, z_near + z_far]
        order_in, order_rest = [z_near, z_far], [z_far, z_near]
        order_out = [z_near, z_far, x_step, y_step, core]
        order_rest_out = order_rest + order_out[2:]
        masks = [0] + spread
        masks = masks + [m + core for m in masks]
        me = owner[None]
        q_block, r_block = pack(me, pltpu.with_memory_space_constraint(weights.reshape(512, 128), pltpu.HBM), vectors.reshape(1, vec_width), vec_width)
        lines = [swap(q_block, step, count) for step in line[::-1]][::-1]
        q_far = jnp.concatenate([q_block, lines[0], lines[1], after(lines[2], ends)], axis=0)
        q_core = swap(q_far, core, count)
        q_pieces = [q_far] + [swap(q_far, step, count) for step in spread]
        r_far = gather_line(after(r_block, q_core), [z_far], count)
        r_far = gather_line(r_far, [z_near], count)
        q_pieces = q_pieces + [q_core] + [swap(piece, core, count) for piece in q_pieces[1:]]
        r_pieces = [swap(after(r_far, *q_pieces), step, count) for step in spread]
    else:
        vec_width = 160
        order_in, order_rest, order_out = [1, 2], [1, 2], [1, 2, 4, 8, 16]
        order_rest_out = order_out
        masks = [4 * i for i in range(8)]
        me = jnp.zeros((1,), jnp.int32)
        blocks = lax.all_gather(weights, AXES, axis=0, tiled=True).reshape(count, -1)
        flat = lax.all_gather(vectors, AXES, axis=0, tiled=True).reshape(40, 128)
        square = 512 * 512 // count
        cuts = [0, 3 * square, 4 * square, 6 * square, 8 * square]
        panels = []
        for index, (start, rows, width) in enumerate(PANELS):
            piece = blocks[:, cuts[index] : cuts[index + 1]].reshape(BLOCKS, rows, width, 128)
            panels.append(piece.transpose(0, 2, 1, 3).reshape(BLOCKS, rows * width, 128))
        spots = [(d * vec_width) // 128 for d in range(BLOCKS)]
        lanes = jnp.arange(256)
        vec_blocks = []
        for d in range(BLOCKS):
            pair = jnp.concatenate([flat, jnp.zeros((8, 128), bf16)], axis=0)[spots[d] : spots[d] + 2].reshape(256)
            offset = d * vec_width - 128 * spots[d]
            pair = jnp.where((lanes >= offset) & (lanes < offset + vec_width), pair, 0)
            vec_blocks.append(jnp.concatenate([pair.reshape(2, 128), jnp.zeros((14, 128), bf16)], axis=0))
        q_all = jnp.concatenate([panels[0], jnp.stack(vec_blocks)], axis=1)
        r_all = jnp.concatenate(panels[1:], axis=1)
        q_pieces = [q_all[4 * i : 4 * i + 4].reshape(-1, 128) for i in range(8)]
        r_pieces = [r_all[4 * i : 4 * i + 4].reshape(-1, 128) for i in range(8)]
    qkv, keys_extra, query_extra, vec, weight = project(
        me, ends, pltpu.with_memory_space_constraint(tokens, pltpu.HBM), q_pieces, masks, order_in, vec_width
    )
    prior = attend(qkv, query_extra, keys_extra, 0, 3, [])
    if fast:
        r_pieces = [r_far] + [after(piece, prior[0]) for piece in r_pieces]
        keys_extra = after(keys_extra, *r_pieces)
        r_pieces = r_pieces + [swap(piece, core, count) for piece in r_pieces]
    attended, offset = attend(qkv, query_extra, keys_extra, 3, 1, prior)
    layer_output, grad_branch, grad_attended, grad_extra, query_extra, r_keep, r_send, vec_grad = middle(
        me, tokens, attended, offset, query_extra, cotangent, vec, r_pieces, masks, order_rest, order_rest_out
    )
    queries, keys, values, keeps, sends, gots = [], [], [], [], [], []
    if fast:
        r_got = swap(r_send, core, count)
    for base, heads in ((0, 1), (1, 2), (3, 1)):
        gq, gk, gv, keep, send, vec_grad = attend_back(
            me,
            tokens,
            qkv,
            grad_attended,
            query_extra,
            keys_extra,
            grad_extra,
            vec_grad,
            order_out,
            vec_width,
            base,
            heads,
        )
        queries.append(gq)
        keys.append(gk)
        values.append(gv)
        keeps.append(keep)
        sends.append(send)
        if not fast:
            continue
        gots.append(swap(send, core, count))
        if base == 0:
            r_keep, r_sends = quarters([(r_keep, after(r_got, gq))])
            vec_grad = after(vec_grad, *r_sends)
            r_gots = swap_each(r_sends, planes, count)
        elif base == 1:
            r_gots = [after(part, gq) for part in r_gots]
            r_keep, r_send = halves(r_keep, r_gots)
            vec_grad = after(vec_grad, r_send)
            r_got = swap(r_send, z_near, count)
    if fast:
        r_keep, r_send = halves(r_keep, [after(r_got, gq)])
        gots = [after(got, gq) for got in gots]
        q_keep, q_sends = quarters(list(zip(keeps, gots)))
        grad_branch = after(grad_branch, *q_sends)
        q_gots = swap_each(q_sends, planes, count)
    grad_tokens = input_grad(grad_branch, queries, keys, values, weight)
    if fast:
        r_parts = [r_keep.reshape(-1, 128), swap(after(r_send, grad_tokens), z_far, count)]
        q_gots = [after(part, grad_tokens) for part in q_gots]
        q_parts = fourths(q_keep, q_gots)
        q_parts = q_parts[:1] + swap_each(q_parts[1:], line, count)
        own_weights, own_vectors = unpack(me, q_parts, r_parts, vec_width)
        own_weights = own_weights.reshape(-1)
        own_vectors = own_vectors.reshape(-1)
    else:
        heads = [jnp.concatenate([k, g], axis=0).astype(f32).reshape(BLOCKS, -1, 128) for k, g in zip(keeps, sends)]
        q_all = jnp.concatenate(heads, axis=1)
        r_all = jnp.concatenate([r_keep, r_send], axis=0).astype(f32).reshape(BLOCKS, R_ROWS, 128)
        sources = (q_all[:, : 4 * QKV_ROWS], r_all[:, :64], r_all[:, 64:192], r_all[:, 192:])
        pieces = []
        for source, (start, rows, width) in zip(sources, PANELS):
            piece = source.reshape(BLOCKS, width, rows, 128).transpose(0, 2, 1, 3)
            pieces.append(piece.reshape(count, -1))
        own_weights = lax.psum_scatter(
            jnp.concatenate(pieces, axis=1).reshape(-1), AXES, scatter_dimension=0, tiled=True
        )
        pairs = q_all[:, 4 * QKV_ROWS : 4 * QKV_ROWS + 2].reshape(BLOCKS, 256)
        rows = [
            pairs[d, (d * vec_width) % 128 : (d * vec_width) % 128 + vec_width] for d in range(BLOCKS)
        ]
        own_vectors = lax.psum_scatter(jnp.concatenate(rows), AXES, scatter_dimension=0, tiled=True)
    return (layer_output, grad_tokens, own_weights, own_vectors)


def solution(mesh):
    dp, fsdp = mesh.shape["dp"], mesh.shape["fsdp"]
    in_specs = (
        P(AXES, None),
        P(),
        P(),
        P(AXES),
        P(AXES),
        P(AXES, None),
    )
    out_specs = (
        P(AXES, None),
        P(AXES, None),
        P(AXES),
        P(AXES),
    )
    return jax.shard_map(
        functools.partial(body, dp, fsdp), mesh=mesh, in_specs=in_specs, out_specs=out_specs, check_vma=False
    )
```

```python
import functools
import math

import jax
import jax.numpy as jnp
from jax import lax
from jax.experimental import pallas as pl
from jax.experimental.pallas import tpu as pltpu
from jax.sharding import PartitionSpec as P

HEADS = 4
HEAD_DIM = 128
FF = 1024
AXES = ("dp", "fsdp")
NORM_EPS = 1e-05
BLOCKS = 32
QKV_ROWS = 48
Q_ROWS = 4 * QKV_ROWS + 16
R_ROWS = 320
FAR = -1e30
f32 = jnp.float32
bf16 = jnp.bfloat16
NT = (((1,), (1,)), ((), ()))
NN = (((1,), (0,)), ((), ()))
TN = (((0,), (0,)), ((), ()))
TT = (((0,), (1,)), ((), ()))
VMEM_MIB = {"pack": 2, "project": 14, "attend": 18, "middle": 26, "attend_back": 28, "input_grad": 14, "unpack": 3}


def dot(a, b, dims):
    return lax.dot_general(a, b, dims, preferred_element_type=f32)


def params(name):
    return pltpu.CompilerParams(vmem_limit_bytes=VMEM_MIB[name] << 20)


def cost(flops, moved, special=0):
    return pl.CostEstimate(flops=int(flops), bytes_accessed=int(moved), transcendentals=int(special))


def whole(shape):
    return pl.BlockSpec(shape, lambda *_: (0,) * len(shape))


def scalar_spec():
    return pl.BlockSpec(memory_space=pltpu.SMEM)


def owner_of(place, me, order):
    mask = 0
    for bit, step in enumerate(order):
        mask = mask + ((place >> bit) & 1) * step
    return jnp.bitwise_xor(me, mask)


def split3(value):
    high = value.astype(bf16)
    rest = value - high.astype(f32)
    middle = rest.astype(bf16)
    low = (rest - middle.astype(f32)).astype(bf16)
    return high, middle, low


PANELS = ((0, 48, 4), (192, 16, 4), (256, 16, 8), (384, 32, 4))


def pack_kernel(vec_width, me_ref, flat, vec, q_out, r_out, wide, line):
    wide[...] = flat[...].astype(f32)
    line[...] = jnp.zeros_like(line)
    line[0:1, 0:vec_width] = vec[...].astype(f32)
    shifted = pltpu.roll(line[...], (me_ref[0] * vec_width) % 128, 1)
    parts = []
    for start, rows, count in PANELS:
        for j in range(count):
            parts.append(wide[pl.ds(start + j, rows, stride=count), :].astype(bf16))
    q_out[0:192, :] = jnp.concatenate(parts[:4], axis=0)
    placed = jnp.concatenate([shifted[0:1, 0:128], shifted[0:1, 128:256], jnp.zeros((14, 128), f32)], axis=0)
    q_out[192:208, :] = placed.astype(bf16)
    r_out[...] = jnp.concatenate(parts[4:], axis=0)


def pack(me, flat, vec, vec_width):
    vmem = pl.BlockSpec(memory_space=pltpu.VMEM)
    return pl.pallas_call(
        functools.partial(pack_kernel, vec_width),
        in_specs=[scalar_spec(), vmem, vmem],
        out_shape=[
            jax.ShapeDtypeStruct((Q_ROWS, 128), bf16),
            jax.ShapeDtypeStruct((R_ROWS, 128), bf16),
        ],
        scratch_shapes=[pltpu.VMEM((512, 128), f32), pltpu.VMEM((8, 256), f32)],
        compiler_params=params("pack"),
        name="pack",
    )(me, flat, vec)


def project_kernel(masks, order, vec_width, me_ref, ends, tokens, *refs):
    pieces = refs[: len(masks)]
    qkv, keys_extra, query_extra, vec_out, weight, vec = refs[len(masks) :]
    step = pl.program_id(0)
    rows = tokens.shape[0]
    me = me_ref[0]

    @pl.when(step == 0)
    def _():
        vec[...] = jnp.zeros_like(vec)
        for mask, ref in zip(masks, pieces):
            for i in range(1 << len(order)):
                d = owner_of(i, jnp.bitwise_xor(me, mask), order)
                row = pl.multiple_of(d * QKV_ROWS, 16)
                for j in range(4):
                    at = i * Q_ROWS + QKV_ROWS * j
                    weight[pl.ds(row, QKV_ROWS), 128 * j : 128 * (j + 1)] = ref[at : at + QKV_ROWS, :]
                row = (d * vec_width) // 128
                at = i * Q_ROWS + 4 * QKV_ROWS
                vec[pl.ds(row, 2), :] = vec[pl.ds(row, 2), :] + ref[at : at + 16, :].astype(f32)[0:2, :]
        vec_out[...] = vec[...]

    x = tokens[...]
    scale = 1.0 / math.sqrt(HEAD_DIM)
    query_bias = jnp.concatenate([vec[j : j + 1, :] for j in range(4)], axis=1)
    value_bias = jnp.concatenate([vec[4 + j : 5 + j, :] for j in range(4)], axis=1)
    queries = ((dot(x, weight[0:512, :], NN) + query_bias) * scale).astype(bf16)
    key_heads = dot(x, weight[512:1024, :], NN).astype(bf16)
    values = (dot(x, weight[1024:1536, :], NN) + value_bias).astype(bf16)
    qkv[:, 0:512] = queries
    qkv[:, 512:1024] = key_heads
    qkv[:, 1024:1536] = values
    places = step * rows + lax.broadcasted_iota(jnp.int32, (rows, ends.shape[1]), 0)
    label = jnp.sum((ends[...] <= places).astype(f32), axis=1, keepdims=True)
    lane = lax.broadcasted_iota(jnp.int32, (rows, 128), 1)
    same = lane.astype(f32) == label
    keys_extra[...] = jnp.where(lane < 8, jnp.where(same, 1.0, 0.0), jnp.where(lane < 32, 1.0, 0.0)).astype(bf16)
    apart = jnp.where((lane < 8) & jnp.logical_not(same), FAR, 0.0)
    product = queries.astype(f32) * key_heads.astype(f32)
    extra = apart
    for h in range(HEADS):
        own = jnp.sum(product[:, 128 * h : 128 * (h + 1)], axis=1, keepdims=True)
        extra = jnp.where(lane == 8 + h, -own, extra)
    query_extra[...] = extra.astype(bf16)


def project(me, ends, tokens, pieces, masks, order, vec_width, rows=512):
    count = tokens.shape[0]
    sets = ends.shape[1]
    return pl.pallas_call(
        functools.partial(project_kernel, masks, order, vec_width),
        grid=(count // rows,),
        in_specs=[
            scalar_spec(),
            whole((1, sets)),
            pl.BlockSpec((rows, 512), lambda i: (i, 0)),
        ]
        + [whole(piece.shape) for piece in pieces],
        out_specs=[
            pl.BlockSpec((rows, 1536), lambda i: (i, 0)),
            pl.BlockSpec((rows, 128), lambda i: (i, 0)),
            pl.BlockSpec((rows, 128), lambda i: (i, 0)),
            whole((48, 128)),
            whole((1536, 512)),
        ],
        out_shape=[
            jax.ShapeDtypeStruct((count, 1536), bf16),
            jax.ShapeDtypeStruct((count, 128), bf16),
            jax.ShapeDtypeStruct((count, 128), bf16),
            jax.ShapeDtypeStruct((48, 128), f32),
            jax.ShapeDtypeStruct((1536, 512), bf16),
        ],
        scratch_shapes=[pltpu.VMEM((48, 128), f32)],
        compiler_params=params("project"),
        cost_estimate=cost(2 * count * 512 * 1536, 12e6),
        name="project",
    )(me, ends, tokens, *pieces)


def own_lanes(lane, head):
    return (lane < 8) | (lane == 8 + head) | ((lane >= 16 + 4 * head) & (lane < 19 + 4 * head))


def attend_kernel(base, q, k, v, query_extra, keys_extra, *refs):
    attended, offset_out, total, mixed, peak = refs[-5:]
    rows = q.shape[0]
    head = base + pl.program_id(0)
    lane = lax.broadcasted_iota(jnp.int32, (rows, 128), 1)
    extra = jnp.where(own_lanes(lane, head), query_extra[...].astype(f32), 0.0).astype(bf16)
    left = jnp.concatenate([k[...], keys_extra[...]], axis=1)
    right = jnp.concatenate([q[...], extra], axis=1)
    weights = jnp.exp(dot(left, right, NT))
    total[...] = jnp.sum(weights, axis=0, keepdims=True)
    mixed[...] = dot(v[...], weights.astype(bf16), TN)
    peak[...] = jnp.zeros_like(peak)
    good = (total[...] > 1e-20) & (total[...] < 1e30)

    @pl.when(jnp.sum(jnp.where(good, 0.0, 1.0)) > 0.0)
    def _():
        def part(j, _):
            place = pl.ds(pl.multiple_of(j * 128, 128), 128)
            lane = lax.broadcasted_iota(jnp.int32, (128, 128), 1)
            extra = jnp.where(own_lanes(lane, head), query_extra[place, :].astype(f32), 0.0).astype(bf16)
            again = dot(left, jnp.concatenate([q[place, :], extra], axis=1), NT)
            top = jnp.max(again, axis=0, keepdims=True)
            safe = jnp.exp(again - top)
            total[:, place] = jnp.sum(safe, axis=0, keepdims=True)
            mixed[:, place] = dot(v[...], safe.astype(bf16), TN)
            peak[:, place] = top
            return 0

        lax.fori_loop(0, rows // 128, part, 0)

    attended[...] = (mixed[...] * (1.0 / total[...])).T.astype(bf16)
    offset_out[0] = peak[...] + jnp.log(total[...])


def attend(qkv, query_extra, keys_extra, base, heads, prior, rows=1024):
    count = qkv.shape[0]
    return pl.pallas_call(
        functools.partial(attend_kernel, base),
        grid=(heads, count // rows),
        in_specs=[
            pl.BlockSpec((rows, 128), lambda h, i: (i, base + h)),
            pl.BlockSpec((count, 128), lambda h, i: (0, HEADS + base + h)),
            pl.BlockSpec((count, 128), lambda h, i: (0, 2 * HEADS + base + h)),
            pl.BlockSpec((rows, 128), lambda h, i: (i, 0)),
            pl.BlockSpec((count, 128), lambda h, i: (0, 0)),
        ]
        + [pl.BlockSpec(memory_space=pl.ANY) for _ in prior],
        out_specs=[
            pl.BlockSpec((rows, 128), lambda h, i: (i, base + h)),
            pl.BlockSpec((1, 1, rows), lambda h, i: (base + h, 0, i)),
        ],
        out_shape=[
            jax.ShapeDtypeStruct((count, 128 * HEADS), bf16),
            jax.ShapeDtypeStruct((HEADS, 1, count), f32),
        ],
        scratch_shapes=[pltpu.VMEM((1, rows), f32), pltpu.VMEM((128, rows), f32), pltpu.VMEM((1, rows), f32)],
        input_output_aliases={5: 0, 6: 1} if prior else {},
        compiler_params=params("attend"),
        cost_estimate=cost(heads * 8 * count * count * 128, 6e6, heads * count * count),
        name="attend",
    )(qkv, qkv, qkv, query_extra, keys_extra, *prior)


def mean_row(value):
    return jnp.sum(value, axis=1, keepdims=True) * (1.0 / value.shape[1])


def norm_rows(summed):
    centered = summed - mean_row(summed)
    inverse = lax.rsqrt(mean_row(centered * centered) + NORM_EPS)
    return centered * inverse, inverse


def norm_back(grad, normed, inverse):
    return inverse * (grad - mean_row(grad) - normed * mean_row(grad * normed))


def fold8(value):
    return jnp.sum(value.reshape(value.shape[0] // 8, 8, value.shape[1]), axis=0)


def middle_kernel(masks, order_in, order_out, sub, me_ref, tokens, attended, offset, query_extra, cotangent, vec, *refs):
    pieces = refs[: len(masks)]
    layer_output, grad_branch_out, grad_attended_out, grad_extra, query_extra_out, keep, send, vec_out = refs[
        len(masks) : -8
    ]
    attn_weight, in_weight, out_weight, grad_attn, grad_in, grad_out, sums, hidden_sum = refs[-8:]
    step = pl.program_id(0)
    me = me_ref[0]
    half = BLOCKS // 2

    @pl.when(step == 0)
    def _():
        for mask, ref in zip(masks, pieces):

            def place(i, _, mask=mask, ref=ref):
                d = owner_of(i, jnp.bitwise_xor(me, mask), order_in)
                start = i * R_ROWS
                a_row = pl.multiple_of(d * 16, 16)
                o_row = pl.multiple_of(d * 32, 16)
                for j in range(4):
                    attn_weight[pl.ds(a_row, 16), 128 * j : 128 * (j + 1)] = ref[
                        pl.ds(pl.multiple_of(start + 16 * j, 16), 16), :
                    ]
                for j in range(8):
                    in_weight[pl.ds(a_row, 16), 128 * j : 128 * (j + 1)] = ref[
                        pl.ds(pl.multiple_of(start + 64 + 16 * j, 16), 16), :
                    ]
                for j in range(4):
                    out_weight[pl.ds(o_row, 32), 128 * j : 128 * (j + 1)] = ref[
                        pl.ds(pl.multiple_of(start + 192 + 32 * j, 16), 32), :
                    ]
                return 0

            lax.fori_loop(0, 1 << len(order_in), place, 0, unroll=True)
        grad_attn[...] = jnp.zeros_like(grad_attn)
        grad_in[...] = jnp.zeros_like(grad_in)
        grad_out[...] = jnp.zeros_like(grad_out)
        sums[...] = jnp.zeros_like(sums)
        hidden_sum[...] = jnp.zeros_like(hidden_sum)

    def row_of(index):
        return jnp.concatenate([vec[4 * index + j : 4 * index + j + 1, :] for j in range(4)], axis=1)

    attn_bias, ffn_bias, gain_one, shift_one, gain_two, shift_two = [row_of(i) for i in range(2, 8)]
    hidden_bias = jnp.concatenate([vec[32 + j : 33 + j, :] for j in range(8)], axis=1)

    offset_rows = jnp.concatenate([offset[h] for h in range(HEADS)] + [jnp.zeros((4, tokens.shape[0]), f32)], axis=0)
    offsets = offset_rows.T
    lane = lax.broadcasted_iota(jnp.int32, (tokens.shape[0], 128), 1)
    extra = query_extra[...].astype(f32)
    for h in range(HEADS):
        for i, part in enumerate(split3(-offsets[:, h : h + 1])):
            extra = jnp.where(lane == 16 + 4 * h + i, part.astype(f32), extra)
    query_extra_out[...] = extra.astype(bf16)

    kept = [{} for _ in range(tokens.shape[0] // sub)]

    def chain(s):
        sl = slice(s * sub, (s + 1) * sub)
        att = attended[sl, :]
        branch = dot(att, attn_weight[...], NN) + attn_bias
        yield
        normed_one, inverse_one = norm_rows(tokens[sl, :].astype(f32) + branch)
        hidden = normed_one * gain_one + shift_one
        hidden_low = hidden.astype(bf16)
        yield
        pre_act = dot(hidden_low, in_weight[...], NN) + hidden_bias
        yield
        cdf = 0.5 * (1.0 + lax.erf(pre_act * 0.7071067811865476))
        density = jnp.exp(-0.5 * pre_act * pre_act) * 0.3989422804014327
        activated = (pre_act * cdf).astype(bf16)
        slope = cdf + pre_act * density
        yield
        ffn_result = dot(activated, out_weight[...], NN) + ffn_bias
        yield
        normed_two, inverse_two = norm_rows(hidden + ffn_result)
        layer_output[sl, :] = (normed_two * gain_two + shift_two).astype(bf16)
        grad_result = cotangent[sl, :].astype(f32)
        sums[4] += fold8(grad_result * normed_two)
        sums[5] += fold8(grad_result)
        grad_second = norm_back(grad_result * gain_two, normed_two, inverse_two)
        grad_ffn = grad_second.astype(bf16)
        sums[1] += fold8(grad_ffn.astype(f32))
        yield
        grad_activated = dot(grad_ffn, out_weight[...], NT)
        kept[s][0] = (activated, grad_ffn)
        yield
        grad_pre = (grad_activated * slope).astype(bf16)
        hidden_sum[...] += fold8(grad_pre.astype(f32))
        yield
        grad_hidden = grad_second + dot(grad_pre, in_weight[...], NT)
        kept[s][1] = (hidden_low, grad_pre)
        yield
        sums[2] += fold8(grad_hidden * normed_one)
        sums[3] += fold8(grad_hidden)
        grad_first = norm_back(grad_hidden * gain_one, normed_one, inverse_one)
        grad_branch = grad_first.astype(bf16)
        grad_branch_out[sl, :] = grad_branch
        sums[0] += fold8(grad_branch.astype(f32))
        yield
        grad_attended = dot(grad_branch, attn_weight[...], NT)
        kept[s][2] = (att, grad_branch)
        yield
        low = grad_attended.astype(bf16)
        grad_attended_out[sl, :] = low
        lane = lax.broadcasted_iota(jnp.int32, (sub, 128), 1)
        extra = jnp.zeros((sub, 128), f32)
        for h in range(HEADS):
            cols = slice(128 * h, 128 * (h + 1))
            low_cols = low[:, cols].astype(f32)
            centre = jnp.sum(low_cols * att[:, cols].astype(f32), axis=1, keepdims=True)
            for i, part in enumerate(split3(-centre)):
                extra = jnp.where(lane == 4 * h + i, part.astype(f32), extra)
        grad_extra[sl, :] = extra.astype(bf16)
        yield

    chains = [chain(s) for s in range(tokens.shape[0] // sub)]
    started = 0
    live = []
    while started < len(chains) or live:
        if started < len(chains):
            live.append(chains[started])
            started += 1
        remaining = []
        for c in live:
            try:
                next(c)
                remaining.append(c)
            except StopIteration:
                pass
        live = remaining
        for i, ref in enumerate((grad_out, grad_in, grad_attn)):
            if all(i in k for k in kept):
                left = jnp.concatenate([k[i][0] for k in kept], axis=0)
                right = jnp.concatenate([k.pop(i)[1] for k in kept], axis=0)
                ref[...] += dot(left, right, TN)

    @pl.when(step == pl.num_programs(0) - 1)
    def _():
        for base, ref in ((0, keep), (half, send)):

            def place(i, _, base=base, ref=ref):
                d = owner_of(base + i, me, order_out)
                start = i * R_ROWS
                a_row = pl.multiple_of(d * 16, 16)
                o_row = pl.multiple_of(d * 32, 16)
                for j in range(4):
                    ref[pl.ds(pl.multiple_of(start + 16 * j, 16), 16), :] = grad_attn[
                        pl.ds(a_row, 16), 128 * j : 128 * (j + 1)
                    ].astype(bf16)
                for j in range(8):
                    ref[pl.ds(pl.multiple_of(start + 64 + 16 * j, 16), 16), :] = grad_in[
                        pl.ds(a_row, 16), 128 * j : 128 * (j + 1)
                    ].astype(bf16)
                for j in range(4):
                    ref[pl.ds(pl.multiple_of(start + 192 + 32 * j, 16), 32), :] = grad_out[
                        pl.ds(o_row, 32), 128 * j : 128 * (j + 1)
                    ].astype(bf16)
                return 0

            lax.fori_loop(0, half, place, 0, unroll=4)
        vec_out[...] = jnp.zeros_like(vec_out)
        for i in range(6):
            row = jnp.sum(sums[i], axis=0, keepdims=True)
            for j in range(4):
                vec_out[8 + 4 * i + j : 9 + 4 * i + j, :] = row[:, 128 * j : 128 * (j + 1)]
        row = jnp.sum(hidden_sum[...], axis=0, keepdims=True)
        for j in range(8):
            vec_out[32 + j : 33 + j, :] = row[:, 128 * j : 128 * (j + 1)]


def middle(
    me, tokens, attended, offset, query_extra, cotangent, vec, pieces, masks, order_in, order_out, rows=512, sub=256
):
    count = tokens.shape[0]
    by_row = pl.BlockSpec((rows, 512), lambda i: (i, 0))
    half_rows = BLOCKS // 2 * R_ROWS
    return pl.pallas_call(
        functools.partial(middle_kernel, masks, order_in, order_out, sub),
        grid=(count // rows,),
        in_specs=[
            scalar_spec(),
            by_row,
            by_row,
            pl.BlockSpec((HEADS, 1, rows), lambda i: (0, 0, i)),
            pl.BlockSpec((rows, 128), lambda i: (i, 0)),
            by_row,
            whole((48, 128)),
        ]
        + [whole(piece.shape) for piece in pieces],
        out_specs=[
            by_row,
            by_row,
            by_row,
            pl.BlockSpec((rows, 128), lambda i: (i, 0)),
            pl.BlockSpec((rows, 128), lambda i: (i, 0)),
            whole((half_rows, 128)),
            whole((half_rows, 128)),
            whole((48, 128)),
        ],
        out_shape=[
            jax.ShapeDtypeStruct((count, 512), bf16),
            jax.ShapeDtypeStruct((count, 512), bf16),
            jax.ShapeDtypeStruct((count, 512), bf16),
            jax.ShapeDtypeStruct((count, 128), bf16),
            jax.ShapeDtypeStruct((count, 128), bf16),
            jax.ShapeDtypeStruct((half_rows, 128), bf16),
            jax.ShapeDtypeStruct((half_rows, 128), bf16),
            jax.ShapeDtypeStruct((48, 128), f32),
        ],
        scratch_shapes=[
            pltpu.VMEM((512, 512), bf16),
            pltpu.VMEM((512, FF), bf16),
            pltpu.VMEM((FF, 512), bf16),
            pltpu.VMEM((512, 512), f32),
            pltpu.VMEM((512, FF), f32),
            pltpu.VMEM((FF, 512), f32),
            pltpu.VMEM((6, 8, 512), f32),
            pltpu.VMEM((8, FF), f32),
        ],
        compiler_params=params("middle"),
        cost_estimate=cost(6 * count * 1310720, 22e6, 3 * count * FF),
        name="middle",
    )(me, tokens, attended, offset, query_extra, cotangent, vec, *pieces)


def attend_back_kernel(
    base,
    heads,
    order,
    vec_width,
    me_ref,
    tokens,
    q,
    k,
    v,
    grad,
    query_extra,
    keys_extra,
    grad_extra,
    vec_in,
    grad_query,
    grad_keys,
    grad_values,
    keep,
    send,
    vec,
    acc,
    all_keys,
    all_values,
    grad_weight,
    held,
    sem,
):
    local = pl.program_id(0)
    step = pl.program_id(1)
    steps = pl.num_programs(1)
    width = k.shape[0]
    last = base + heads == HEADS
    copy = pltpu.make_async_copy(tokens, held, sem)

    @pl.when((local == 0) & (step == 0))
    def _():
        copy.start()
        vec[...] = vec_in[...]

    head = base + local
    lane = lax.broadcasted_iota(jnp.int32, (width, 128), 1)
    ones = jnp.where((lane >= 4 * head) & (lane < 4 * head + 3), 1.0, 0.0).astype(bf16)
    extra = jnp.where(own_lanes(lane, head), keys_extra[...].astype(f32), 0.0).astype(bf16)
    scores = dot(
        jnp.concatenate([q[...], query_extra[...]], axis=1), jnp.concatenate([k[...], extra], axis=1), NT
    )
    centred = dot(
        jnp.concatenate([grad[...], grad_extra[...]], axis=1), jnp.concatenate([v[...], ones], axis=1), NT
    )
    probs = jnp.exp(scores)
    probs_low = probs.astype(bf16)
    grad_scores = (probs * centred).astype(bf16)
    gv = dot(grad[...], probs_low, TN).astype(bf16)
    gk = dot(q[...], grad_scores, TN).astype(bf16)
    grad_values[...] = gv
    grad_keys[...] = gk
    all_values[step] = gv
    all_keys[step] = gk
    part = dot(grad_scores, k[...], NN)

    @pl.when(step == 0)
    def _():
        acc[...] = part

    @pl.when(step > 0)
    def _():
        acc[...] += part

    @pl.when((local == 0) & (step == steps - 1))
    def _():
        copy.wait()

    @pl.when(step == steps - 1)
    def _():
        me = me_ref[0]
        scale = 1.0 / math.sqrt(HEAD_DIM)
        x = held[...]
        gq_all = acc[...].astype(bf16)
        grad_query[...] = gq_all
        gk_all = jnp.concatenate([all_keys[i] for i in range(all_keys.shape[0])], axis=1)
        gv_all = jnp.concatenate([all_values[i] for i in range(all_values.shape[0])], axis=1)
        grad_weight[0:512, :] = dot(gq_all, x, TN).T * scale
        grad_weight[512:1024, :] = dot(gk_all, x, NN).T
        grad_weight[1024:1536, :] = dot(gv_all, x, NN).T
        row_ones = jnp.ones((8, x.shape[0]), bf16)
        vec[pl.ds(base + local, 1), :] = dot(row_ones, gq_all, NN)[0:1] * scale
        vec[pl.ds(4 + base + local, 1), :] = dot(row_ones, gv_all, NT)[0:1]
        half = BLOCKS // 2
        block = heads * QKV_ROWS + (16 if last else 0)
        for start, ref in ((0, keep), (half, send)):

            def place(i, _, start=start, ref=ref):
                d = owner_of(start + i, me, order)
                ref[pl.ds(pl.multiple_of(i * block + local * QKV_ROWS, 16), QKV_ROWS), :] = grad_weight[
                    pl.ds(pl.multiple_of(d * QKV_ROWS, 16), QKV_ROWS), :
                ].astype(bf16)
                if last:
                    pair = vec[pl.ds((d * vec_width) // 128, 2), :]
                    pair = jnp.concatenate([pair, jnp.zeros((14, 128), f32)], axis=0)
                    ref[pl.ds(pl.multiple_of(i * block + heads * QKV_ROWS, 16), 16), :] = pair.astype(bf16)
                return 0

            lax.fori_loop(0, half, place, 0, unroll=4)


def attend_back(
    me, tokens, qkv, grad_attended, query_extra, keys_extra, grad_extra, vec, order, vec_width, base, heads, width=512
):
    count = qkv.shape[0]
    half_rows = BLOCKS // 2 * (heads * QKV_ROWS + (16 if base + heads == HEADS else 0))
    return pl.pallas_call(
        functools.partial(attend_back_kernel, base, heads, order, vec_width),
        grid=(heads, count // width),
        in_specs=[
            scalar_spec(),
            pl.BlockSpec(memory_space=pl.ANY),
            pl.BlockSpec((count, 128), lambda h, i: (0, base + h)),
            pl.BlockSpec((width, 128), lambda h, i: (i, HEADS + base + h)),
            pl.BlockSpec((width, 128), lambda h, i: (i, 2 * HEADS + base + h)),
            pl.BlockSpec((count, 128), lambda h, i: (0, base + h)),
            whole((count, 128)),
            pl.BlockSpec((width, 128), lambda h, i: (i, 0)),
            whole((count, 128)),
            whole((48, 128)),
        ],
        out_specs=[
            pl.BlockSpec((count, 128), lambda h, i: (0, h)),
            pl.BlockSpec((128, width), lambda h, i: (h, i)),
            pl.BlockSpec((128, width), lambda h, i: (h, i)),
            whole((half_rows, 128)),
            whole((half_rows, 128)),
            whole((48, 128)),
        ],
        out_shape=[
            jax.ShapeDtypeStruct((count, 128 * heads), bf16),
            jax.ShapeDtypeStruct((128 * heads, count), bf16),
            jax.ShapeDtypeStruct((128 * heads, count), bf16),
            jax.ShapeDtypeStruct((half_rows, 128), bf16),
            jax.ShapeDtypeStruct((half_rows, 128), bf16),
            jax.ShapeDtypeStruct((48, 128), f32),
        ],
        scratch_shapes=[
            pltpu.VMEM((count, 128), f32),
            pltpu.VMEM((count // width, 128, width), bf16),
            pltpu.VMEM((count // width, 128, width), bf16),
            pltpu.VMEM((1536, 128), f32),
            pltpu.VMEM((count, 512), bf16),
            pltpu.SemaphoreType.DMA,
        ],
        compiler_params=params("attend_back"),
        cost_estimate=cost(heads * 20 * count * count * 128, heads * 12e6, heads * count * count),
        name="attend_back",
    )(me, tokens, qkv, qkv, qkv, grad_attended, query_extra, keys_extra, grad_extra, vec)


def input_grad_kernel(groups, *refs):
    grad_branch = refs[0]
    queries, keys, values = [refs[1 + i * groups : 1 + (i + 1) * groups] for i in range(3)]
    weight, out = refs[-2], refs[-1]
    scale = 1.0 / math.sqrt(HEAD_DIM)
    gq = jnp.concatenate([r[...] for r in queries], axis=1)
    gk = jnp.concatenate([r[...] for r in keys], axis=0)
    gv = jnp.concatenate([r[...] for r in values], axis=0)
    total = grad_branch[...].astype(f32) + scale * dot(gq, weight[0:512, :], NT)
    total = total + dot(gk, weight[512:1024, :], TT)
    out[...] = total + dot(gv, weight[1024:1536, :], TT)


def input_grad(grad_branch, queries, keys, values, weight, rows=512):
    count = grad_branch.shape[0]
    by_row = pl.BlockSpec((rows, 512), lambda i: (i, 0))
    return pl.pallas_call(
        functools.partial(input_grad_kernel, len(queries)),
        grid=(count // rows,),
        in_specs=[by_row]
        + [pl.BlockSpec((rows, a.shape[1]), lambda i: (i, 0)) for a in queries]
        + [pl.BlockSpec((a.shape[0], rows), lambda i: (0, i)) for a in keys + values]
        + [whole((1536, 512))],
        out_specs=by_row,
        out_shape=jax.ShapeDtypeStruct((count, 512), f32),
        compiler_params=params("input_grad"),
        cost_estimate=cost(2 * count * 512 * 1536, 16e6),
        name="input_grad",
    )(grad_branch, *queries, *keys, *values, weight)


def unpack_kernel(vec_width, me_ref, *refs):
    q_parts, r_parts = refs[:4], refs[4:6]
    out, vec_out, line = refs[6:]
    q_sum, r_sum = q_parts[0][...], r_parts[0][...]
    for part in q_parts[1:]:
        q_sum = q_sum + part[...].astype(f32)
    for part in r_parts[1:]:
        r_sum = r_sum + part[...].astype(f32)
    at = 0
    source = q_sum
    for index, (start, rows, count) in enumerate(PANELS):
        if index == 1:
            source, at = r_sum, 0
        for j in range(count):
            out[pl.ds(start + j, rows, stride=count), :] = source[at : at + rows, :]
            at += rows
    pair = jnp.concatenate([q_sum[192:200, :], q_sum[193:201, :]], axis=1)
    line[...] = pltpu.roll(pair, 256 - (me_ref[0] * vec_width) % 128, 1)
    vec_out[...] = line[0:1, 0:vec_width]


def unpack(me, q_parts, r_parts, vec_width):
    vmem = pl.BlockSpec(memory_space=pltpu.VMEM)
    return pl.pallas_call(
        functools.partial(unpack_kernel, vec_width),
        in_specs=[scalar_spec()] + [vmem] * 6,
        out_shape=[jax.ShapeDtypeStruct((512, 128), f32), jax.ShapeDtypeStruct((1, vec_width), f32)],
        scratch_shapes=[pltpu.VMEM((8, 256), f32)],
        compiler_params=params("unpack"),
        name="unpack",
    )(me, *q_parts, *r_parts)


def swap(array, step, count):
    return lax.ppermute(array, AXES, [(i, i ^ step) for i in range(count)])


def swap_each(parts, steps, count):
    pairs = list(zip(parts, steps))
    return [swap(part, step, count) for part, step in pairs[::-1]][::-1]


def after(value, *others):
    return lax.optimization_barrier((value, *others))[0]


def quarters(groups):
    parts = []
    for keep, got in groups:
        keep, got = keep.reshape(4, 4, -1, 128), got.reshape(4, 4, -1, 128)
        parts.append([keep[i].astype(f32) + got[i].astype(f32) for i in range(4)])
    totals = [jnp.concatenate(same, axis=1) if len(same) > 1 else same[0] for same in zip(*parts)]
    return totals[0], [total.astype(bf16).reshape(-1, 128) for total in totals[1:]]


def halves(keep, gots):
    total = keep
    for got in gots:
        total = total + got.astype(f32).reshape(keep.shape)
    half = total.shape[0] // 2
    return total[:half], total[half:].astype(bf16).reshape(-1, 128)


def fourths(keep, gots):
    total = keep
    for got in gots:
        total = total + got.astype(f32).reshape(keep.shape)
    return [total[0]] + [total[i].astype(bf16) for i in range(1, 4)]


def fast_layout(dp, fsdp):
    return dp == 4 and fsdp == 8


def gather_line(block, steps, count):
    return jnp.concatenate([block] + [swap(block, step, count) for step in steps], axis=0)


def body(dp, fsdp, tokens, lengths, assignment, weights, vectors, cotangent):
    count = dp * fsdp
    fast = fast_layout(dp, fsdp)
    owner = lax.axis_index(AXES).astype(jnp.int32)
    owned = assignment == owner
    ends = jnp.cumsum(jnp.where(owned, lengths, 0), dtype=jnp.int32)
    ends = jnp.where(owned, ends, 1 << 30)[None, :]
    if fast:
        vec_width = vectors.shape[0]
        core, x_step, y_step, z_near, z_far = fsdp, 1, 2 * fsdp, 2, 4
        planes = [x_step, y_step, x_step + y_step]
        spread = [x_step + y_step, y_step, x_step]
        line = [z_near, z_far, z_near + z_far]
        order_in, order_rest = [z_near, z_far], [z_far, z_near]
        order_out = [z_near, z_far, x_step, y_step, core]
        order_rest_out = order_rest + order_out[2:]
        masks = [0] + spread
        masks = masks + [m + core for m in masks]
        me = owner[None]
        q_block, r_block = pack(me, pltpu.with_memory_space_constraint(weights.reshape(512, 128), pltpu.HBM), vectors.reshape(1, vec_width), vec_width)
        lines = [swap(q_block, step, count) for step in line[::-1]][::-1]
        q_far = jnp.concatenate([q_block, lines[0], lines[1], after(lines[2], ends)], axis=0)
        q_core = swap(q_far, core, count)
        q_pieces = [q_far] + [swap(q_far, step, count) for step in spread]
        r_far = gather_line(after(r_block, q_core), [z_far], count)
        r_far = gather_line(r_far, [z_near], count)
        q_pieces = q_pieces + [q_core] + [swap(piece, core, count) for piece in q_pieces[1:]]
        r_pieces = [swap(after(r_far, *q_pieces), step, count) for step in spread]
    else:
        vec_width = 160
        order_in, order_rest, order_out = [1, 2], [1, 2], [1, 2, 4, 8, 16]
        order_rest_out = order_out
        masks = [4 * i for i in range(8)]
        me = jnp.zeros((1,), jnp.int32)
        blocks = lax.all_gather(weights, AXES, axis=0, tiled=True).reshape(count, -1)
        flat = lax.all_gather(vectors, AXES, axis=0, tiled=True).reshape(40, 128)
        square = 512 * 512 // count
        cuts = [0, 3 * square, 4 * square, 6 * square, 8 * square]
        panels = []
        for index, (start, rows, width) in enumerate(PANELS):
            piece = blocks[:, cuts[index] : cuts[index + 1]].reshape(BLOCKS, rows, width, 128)
            panels.append(piece.transpose(0, 2, 1, 3).reshape(BLOCKS, rows * width, 128))
        spots = [(d * vec_width) // 128 for d in range(BLOCKS)]
        lanes = jnp.arange(256)
        vec_blocks = []
        for d in range(BLOCKS):
            pair = jnp.concatenate([flat, jnp.zeros((8, 128), bf16)], axis=0)[spots[d] : spots[d] + 2].reshape(256)
            offset = d * vec_width - 128 * spots[d]
            pair = jnp.where((lanes >= offset) & (lanes < offset + vec_width), pair, 0)
            vec_blocks.append(jnp.concatenate([pair.reshape(2, 128), jnp.zeros((14, 128), bf16)], axis=0))
        q_all = jnp.concatenate([panels[0], jnp.stack(vec_blocks)], axis=1)
        r_all = jnp.concatenate(panels[1:], axis=1)
        q_pieces = [q_all[4 * i : 4 * i + 4].reshape(-1, 128) for i in range(8)]
        r_pieces = [r_all[4 * i : 4 * i + 4].reshape(-1, 128) for i in range(8)]
    qkv, keys_extra, query_extra, vec, weight = project(
        me, ends, pltpu.with_memory_space_constraint(tokens, pltpu.HBM), q_pieces, masks, order_in, vec_width
    )
    prior = attend(qkv, query_extra, keys_extra, 0, 3, [])
    if fast:
        r_pieces = [r_far] + [after(piece, prior[0]) for piece in r_pieces]
        keys_extra = after(keys_extra, *r_pieces)
        r_pieces = r_pieces + [swap(piece, core, count) for piece in r_pieces]
    attended, offset = attend(qkv, query_extra, keys_extra, 3, 1, prior)
    layer_output, grad_branch, grad_attended, grad_extra, query_extra, r_keep, r_send, vec_grad = middle(
        me, tokens, attended, offset, query_extra, cotangent, vec, r_pieces, masks, order_rest, order_rest_out
    )
    queries, keys, values, keeps, sends, gots = [], [], [], [], [], []
    if fast:
        r_got = swap(r_send, core, count)
    for base, heads in ((0, 1), (1, 2), (3, 1)):
        gq, gk, gv, keep, send, vec_grad = attend_back(
            me,
            tokens,
            qkv,
            grad_attended,
            query_extra,
            keys_extra,
            grad_extra,
            vec_grad,
            order_out,
            vec_width,
            base,
            heads,
        )
        queries.append(gq)
        keys.append(gk)
        values.append(gv)
        keeps.append(keep)
        sends.append(send)
        if not fast:
            continue
        gots.append(swap(send, core, count))
        if base == 0:
            r_keep, r_sends = quarters([(r_keep, after(r_got, gq))])
            vec_grad = after(vec_grad, *r_sends)
            r_gots = swap_each(r_sends, planes, count)
        elif base == 1:
            r_gots = [after(part, gq) for part in r_gots]
            r_keep, r_send = halves(r_keep, r_gots)
            vec_grad = after(vec_grad, r_send)
            r_got = swap(r_send, z_near, count)
    if fast:
        r_keep, r_send = halves(r_keep, [after(r_got, gq)])
        gots = [after(got, gq) for got in gots]
        q_keep, q_sends = quarters(list(zip(keeps, gots)))
        grad_branch = after(grad_branch, *q_sends)
        q_gots = swap_each(q_sends, planes, count)
    grad_tokens = input_grad(grad_branch, queries, keys, values, weight)
    if fast:
        r_parts = [r_keep.reshape(-1, 128), swap(after(r_send, grad_tokens), z_far, count)]
        q_gots = [after(part, grad_tokens) for part in q_gots]
        q_parts = fourths(q_keep, q_gots)
        q_parts = q_parts[:1] + swap_each(q_parts[1:], line, count)
        own_weights, own_vectors = unpack(me, q_parts, r_parts, vec_width)
        own_weights = own_weights.reshape(-1)
        own_vectors = own_vectors.reshape(-1)
    else:
        heads = [jnp.concatenate([k, g], axis=0).astype(f32).reshape(BLOCKS, -1, 128) for k, g in zip(keeps, sends)]
        q_all = jnp.concatenate(heads, axis=1)
        r_all = jnp.concatenate([r_keep, r_send], axis=0).astype(f32).reshape(BLOCKS, R_ROWS, 128)
        sources = (q_all[:, : 4 * QKV_ROWS], r_all[:, :64], r_all[:, 64:192], r_all[:, 192:])
        pieces = []
        for source, (start, rows, width) in zip(sources, PANELS):
            piece = source.reshape(BLOCKS, width, rows, 128).transpose(0, 2, 1, 3)
            pieces.append(piece.reshape(count, -1))
        own_weights = lax.psum_scatter(
            jnp.concatenate(pieces, axis=1).reshape(-1), AXES, scatter_dimension=0, tiled=True
        )
        pairs = q_all[:, 4 * QKV_ROWS : 4 * QKV_ROWS + 2].reshape(BLOCKS, 256)
        rows = [
            pairs[d, (d * vec_width) % 128 : (d * vec_width) % 128 + vec_width] for d in range(BLOCKS)
        ]
        own_vectors = lax.psum_scatter(jnp.concatenate(rows), AXES, scatter_dimension=0, tiled=True)
    return (layer_output, grad_tokens, own_weights, own_vectors)


def solution(mesh):
    dp, fsdp = mesh.shape["dp"], mesh.shape["fsdp"]
    in_specs = (
        P(AXES, None),
        P(),
        P(),
        P(AXES),
        P(AXES),
        P(AXES, None),
    )
    out_specs = (
        P(AXES, None),
        P(AXES, None),
        P(AXES),
        P(AXES),
    )
    return jax.shard_map(
        functools.partial(body, dp, fsdp), mesh=mesh, in_specs=in_specs, out_specs=out_specs, check_vma=False
    )
```

```python
import functools
import math

import jax
import jax.numpy as jnp
from jax import lax
from jax.experimental import pallas as pl
from jax.experimental.pallas import tpu as pltpu
from jax.sharding import PartitionSpec as P

HEADS = 4
HEAD_DIM = 128
FF = 1024
AXES = ("dp", "fsdp")
NORM_EPS = 1e-05
BLOCKS = 32
QKV_ROWS = 48
Q_ROWS = 4 * QKV_ROWS + 16
R_ROWS = 320
FAR = -1e30
f32 = jnp.float32
bf16 = jnp.bfloat16
NT = (((1,), (1,)), ((), ()))
NN = (((1,), (0,)), ((), ()))
TN = (((0,), (0,)), ((), ()))
TT = (((0,), (1,)), ((), ()))
VMEM_MIB = {"pack": 2, "project": 14, "attend": 18, "middle": 26, "attend_back": 28, "input_grad": 14, "unpack": 3}


def dot(a, b, dims):
    return lax.dot_general(a, b, dims, preferred_element_type=f32)


def params(name):
    return pltpu.CompilerParams(vmem_limit_bytes=VMEM_MIB[name] << 20)


def cost(flops, moved, special=0):
    return pl.CostEstimate(flops=int(flops), bytes_accessed=int(moved), transcendentals=int(special))


def whole(shape):
    return pl.BlockSpec(shape, lambda *_: (0,) * len(shape))


def scalar_spec():
    return pl.BlockSpec(memory_space=pltpu.SMEM)


def owner_of(place, me, order):
    mask = 0
    for bit, step in enumerate(order):
        mask = mask + ((place >> bit) & 1) * step
    return jnp.bitwise_xor(me, mask)


def split3(value):
    high = value.astype(bf16)
    rest = value - high.astype(f32)
    middle = rest.astype(bf16)
    low = (rest - middle.astype(f32)).astype(bf16)
    return high, middle, low


PANELS = ((0, 48, 4), (192, 16, 4), (256, 16, 8), (384, 32, 4))


def pack_kernel(vec_width, me_ref, flat, vec, q_out, r_out, wide, line):
    wide[...] = flat[...].astype(f32)
    line[...] = jnp.zeros_like(line)
    line[0:1, 0:vec_width] = vec[...].astype(f32)
    shifted = pltpu.roll(line[...], (me_ref[0] * vec_width) % 128, 1)
    parts = []
    for start, rows, count in PANELS:
        for j in range(count):
            parts.append(wide[pl.ds(start + j, rows, stride=count), :].astype(bf16))
    q_out[0:192, :] = jnp.concatenate(parts[:4], axis=0)
    placed = jnp.concatenate([shifted[0:1, 0:128], shifted[0:1, 128:256], jnp.zeros((14, 128), f32)], axis=0)
    q_out[192:208, :] = placed.astype(bf16)
    r_out[...] = jnp.concatenate(parts[4:], axis=0)


def pack(me, flat, vec, vec_width):
    vmem = pl.BlockSpec(memory_space=pltpu.VMEM)
    return pl.pallas_call(
        functools.partial(pack_kernel, vec_width),
        in_specs=[scalar_spec(), vmem, vmem],
        out_shape=[
            jax.ShapeDtypeStruct((Q_ROWS, 128), bf16),
            jax.ShapeDtypeStruct((R_ROWS, 128), bf16),
        ],
        scratch_shapes=[pltpu.VMEM((512, 128), f32), pltpu.VMEM((8, 256), f32)],
        compiler_params=params("pack"),
        name="pack",
    )(me, flat, vec)


def project_kernel(masks, order, vec_width, me_ref, ends, tokens, *refs):
    pieces = refs[: len(masks)]
    qkv, keys_extra, query_extra, vec_out, weight, vec = refs[len(masks) :]
    step = pl.program_id(0)
    rows = tokens.shape[0]
    me = me_ref[0]

    @pl.when(step == 0)
    def _():
        vec[...] = jnp.zeros_like(vec)
        for mask, ref in zip(masks, pieces):
            for i in range(1 << len(order)):
                d = owner_of(i, jnp.bitwise_xor(me, mask), order)
                row = pl.multiple_of(d * QKV_ROWS, 16)
                for j in range(4):
                    at = i * Q_ROWS + QKV_ROWS * j
                    weight[pl.ds(row, QKV_ROWS), 128 * j : 128 * (j + 1)] = ref[at : at + QKV_ROWS, :]
                row = (d * vec_width) // 128
                at = i * Q_ROWS + 4 * QKV_ROWS
                vec[pl.ds(row, 2), :] = vec[pl.ds(row, 2), :] + ref[at : at + 16, :].astype(f32)[0:2, :]
        vec_out[...] = vec[...]

    x = tokens[...]
    scale = 1.0 / math.sqrt(HEAD_DIM)
    query_bias = jnp.concatenate([vec[j : j + 1, :] for j in range(4)], axis=1)
    value_bias = jnp.concatenate([vec[4 + j : 5 + j, :] for j in range(4)], axis=1)
    queries = ((dot(x, weight[0:512, :], NN) + query_bias) * scale).astype(bf16)
    key_heads = dot(x, weight[512:1024, :], NN).astype(bf16)
    values = (dot(x, weight[1024:1536, :], NN) + value_bias).astype(bf16)
    qkv[:, 0:512] = queries
    qkv[:, 512:1024] = key_heads
    qkv[:, 1024:1536] = values
    places = step * rows + lax.broadcasted_iota(jnp.int32, (rows, ends.shape[1]), 0)
    label = jnp.sum((ends[...] <= places).astype(f32), axis=1, keepdims=True)
    lane = lax.broadcasted_iota(jnp.int32, (rows, 128), 1)
    same = lane.astype(f32) == label
    keys_extra[...] = jnp.where(lane < 8, jnp.where(same, 1.0, 0.0), jnp.where(lane < 32, 1.0, 0.0)).astype(bf16)
    apart = jnp.where((lane < 8) & jnp.logical_not(same), FAR, 0.0)
    product = queries.astype(f32) * key_heads.astype(f32)
    extra = apart
    for h in range(HEADS):
        own = jnp.sum(product[:, 128 * h : 128 * (h + 1)], axis=1, keepdims=True)
        extra = jnp.where(lane == 8 + h, -own, extra)
    query_extra[...] = extra.astype(bf16)


def project(me, ends, tokens, pieces, masks, order, vec_width, rows=512):
    count = tokens.shape[0]
    sets = ends.shape[1]
    return pl.pallas_call(
        functools.partial(project_kernel, masks, order, vec_width),
        grid=(count // rows,),
        in_specs=[
            scalar_spec(),
            whole((1, sets)),
            pl.BlockSpec((rows, 512), lambda i: (i, 0)),
        ]
        + [whole(piece.shape) for piece in pieces],
        out_specs=[
            pl.BlockSpec((rows, 1536), lambda i: (i, 0)),
            pl.BlockSpec((rows, 128), lambda i: (i, 0)),
            pl.BlockSpec((rows, 128), lambda i: (i, 0)),
            whole((48, 128)),
            whole((1536, 512)),
        ],
        out_shape=[
            jax.ShapeDtypeStruct((count, 1536), bf16),
            jax.ShapeDtypeStruct((count, 128), bf16),
            jax.ShapeDtypeStruct((count, 128), bf16),
            jax.ShapeDtypeStruct((48, 128), f32),
            jax.ShapeDtypeStruct((1536, 512), bf16),
        ],
        scratch_shapes=[pltpu.VMEM((48, 128), f32)],
        compiler_params=params("project"),
        cost_estimate=cost(2 * count * 512 * 1536, 12e6),
        name="project",
    )(me, ends, tokens, *pieces)


def own_lanes(lane, head):
    return (lane < 8) | (lane == 8 + head) | ((lane >= 16 + 4 * head) & (lane < 19 + 4 * head))


def attend_kernel(base, q, k, v, query_extra, keys_extra, *refs):
    attended, offset_out, total, mixed, peak = refs[-5:]
    rows = q.shape[0]
    head = base + pl.program_id(0)
    lane = lax.broadcasted_iota(jnp.int32, (rows, 128), 1)
    extra = jnp.where(own_lanes(lane, head), query_extra[...].astype(f32), 0.0).astype(bf16)
    left = jnp.concatenate([k[...], keys_extra[...]], axis=1)
    right = jnp.concatenate([q[...], extra], axis=1)
    weights = jnp.exp(dot(left, right, NT))
    total[...] = jnp.sum(weights, axis=0, keepdims=True)
    mixed[...] = dot(v[...], weights.astype(bf16), TN)
    peak[...] = jnp.zeros_like(peak)
    good = (total[...] > 1e-20) & (total[...] < 1e30)

    @pl.when(jnp.sum(jnp.where(good, 0.0, 1.0)) > 0.0)
    def _():
        def part(j, _):
            place = pl.ds(pl.multiple_of(j * 128, 128), 128)
            lane = lax.broadcasted_iota(jnp.int32, (128, 128), 1)
            extra = jnp.where(own_lanes(lane, head), query_extra[place, :].astype(f32), 0.0).astype(bf16)
            again = dot(left, jnp.concatenate([q[place, :], extra], axis=1), NT)
            top = jnp.max(again, axis=0, keepdims=True)
            safe = jnp.exp(again - top)
            total[:, place] = jnp.sum(safe, axis=0, keepdims=True)
            mixed[:, place] = dot(v[...], safe.astype(bf16), TN)
            peak[:, place] = top
            return 0

        lax.fori_loop(0, rows // 128, part, 0)

    attended[...] = (mixed[...] * (1.0 / total[...])).T.astype(bf16)
    offset_out[0] = peak[...] + jnp.log(total[...])


def attend(qkv, query_extra, keys_extra, base, heads, prior, rows=1024):
    count = qkv.shape[0]
    return pl.pallas_call(
        functools.partial(attend_kernel, base),
        grid=(heads, count // rows),
        in_specs=[
            pl.BlockSpec((rows, 128), lambda h, i: (i, base + h)),
            pl.BlockSpec((count, 128), lambda h, i: (0, HEADS + base + h)),
            pl.BlockSpec((count, 128), lambda h, i: (0, 2 * HEADS + base + h)),
            pl.BlockSpec((rows, 128), lambda h, i: (i, 0)),
            pl.BlockSpec((count, 128), lambda h, i: (0, 0)),
        ]
        + [pl.BlockSpec(memory_space=pl.ANY) for _ in prior],
        out_specs=[
            pl.BlockSpec((rows, 128), lambda h, i: (i, base + h)),
            pl.BlockSpec((1, 1, rows), lambda h, i: (base + h, 0, i)),
        ],
        out_shape=[
            jax.ShapeDtypeStruct((count, 128 * HEADS), bf16),
            jax.ShapeDtypeStruct((HEADS, 1, count), f32),
        ],
        scratch_shapes=[pltpu.VMEM((1, rows), f32), pltpu.VMEM((128, rows), f32), pltpu.VMEM((1, rows), f32)],
        input_output_aliases={5: 0, 6: 1} if prior else {},
        compiler_params=params("attend"),
        cost_estimate=cost(heads * 8 * count * count * 128, 6e6, heads * count * count),
        name="attend",
    )(qkv, qkv, qkv, query_extra, keys_extra, *prior)


def mean_row(value):
    return jnp.sum(value, axis=1, keepdims=True) * (1.0 / value.shape[1])


def norm_rows(summed):
    centered = summed - mean_row(summed)
    inverse = lax.rsqrt(mean_row(centered * centered) + NORM_EPS)
    return centered * inverse, inverse


def norm_back(grad, normed, inverse):
    return inverse * (grad - mean_row(grad) - normed * mean_row(grad * normed))


def fold8(value):
    return jnp.sum(value.reshape(value.shape[0] // 8, 8, value.shape[1]), axis=0)


def middle_kernel(masks, order_in, order_out, sub, me_ref, tokens, attended, offset, query_extra, cotangent, vec, *refs):
    pieces = refs[: len(masks)]
    layer_output, grad_branch_out, grad_attended_out, grad_extra, query_extra_out, keep, send, vec_out = refs[
        len(masks) : -8
    ]
    attn_weight, in_weight, out_weight, grad_attn, grad_in, grad_out, sums, hidden_sum = refs[-8:]
    step = pl.program_id(0)
    me = me_ref[0]
    half = BLOCKS // 2

    @pl.when(step == 0)
    def _():
        for mask, ref in zip(masks, pieces):

            def place(i, _, mask=mask, ref=ref):
                d = owner_of(i, jnp.bitwise_xor(me, mask), order_in)
                start = i * R_ROWS
                a_row = pl.multiple_of(d * 16, 16)
                o_row = pl.multiple_of(d * 32, 16)
                for j in range(4):
                    attn_weight[pl.ds(a_row, 16), 128 * j : 128 * (j + 1)] = ref[
                        pl.ds(pl.multiple_of(start + 16 * j, 16), 16), :
                    ]
                for j in range(8):
                    in_weight[pl.ds(a_row, 16), 128 * j : 128 * (j + 1)] = ref[
                        pl.ds(pl.multiple_of(start + 64 + 16 * j, 16), 16), :
                    ]
                for j in range(4):
                    out_weight[pl.ds(o_row, 32), 128 * j : 128 * (j + 1)] = ref[
                        pl.ds(pl.multiple_of(start + 192 + 32 * j, 16), 32), :
                    ]
                return 0

            lax.fori_loop(0, 1 << len(order_in), place, 0, unroll=True)
        grad_attn[...] = jnp.zeros_like(grad_attn)
        grad_in[...] = jnp.zeros_like(grad_in)
        grad_out[...] = jnp.zeros_like(grad_out)
        sums[...] = jnp.zeros_like(sums)
        hidden_sum[...] = jnp.zeros_like(hidden_sum)

    def row_of(index):
        return jnp.concatenate([vec[4 * index + j : 4 * index + j + 1, :] for j in range(4)], axis=1)

    attn_bias, ffn_bias, gain_one, shift_one, gain_two, shift_two = [row_of(i) for i in range(2, 8)]
    hidden_bias = jnp.concatenate([vec[32 + j : 33 + j, :] for j in range(8)], axis=1)

    offset_rows = jnp.concatenate([offset[h] for h in range(HEADS)] + [jnp.zeros((4, tokens.shape[0]), f32)], axis=0)
    offsets = offset_rows.T
    lane = lax.broadcasted_iota(jnp.int32, (tokens.shape[0], 128), 1)
    extra = query_extra[...].astype(f32)
    for h in range(HEADS):
        for i, part in enumerate(split3(-offsets[:, h : h + 1])):
            extra = jnp.where(lane == 16 + 4 * h + i, part.astype(f32), extra)
    query_extra_out[...] = extra.astype(bf16)

    kept = [{} for _ in range(tokens.shape[0] // sub)]

    def chain(s):
        sl = slice(s * sub, (s + 1) * sub)
        att = attended[sl, :]
        branch = dot(att, attn_weight[...], NN) + attn_bias
        yield
        normed_one, inverse_one = norm_rows(tokens[sl, :].astype(f32) + branch)
        hidden = normed_one * gain_one + shift_one
        hidden_low = hidden.astype(bf16)
        yield
        pre_act = dot(hidden_low, in_weight[...], NN) + hidden_bias
        yield
        cdf = 0.5 * (1.0 + lax.erf(pre_act * 0.7071067811865476))
        density = jnp.exp(-0.5 * pre_act * pre_act) * 0.3989422804014327
        activated = (pre_act * cdf).astype(bf16)
        slope = cdf + pre_act * density
        yield
        ffn_result = dot(activated, out_weight[...], NN) + ffn_bias
        yield
        normed_two, inverse_two = norm_rows(hidden + ffn_result)
        layer_output[sl, :] = (normed_two * gain_two + shift_two).astype(bf16)
        grad_result = cotangent[sl, :].astype(f32)
        sums[4] += fold8(grad_result * normed_two)
        sums[5] += fold8(grad_result)
        grad_second = norm_back(grad_result * gain_two, normed_two, inverse_two)
        grad_ffn = grad_second.astype(bf16)
        sums[1] += fold8(grad_ffn.astype(f32))
        yield
        grad_activated = dot(grad_ffn, out_weight[...], NT)
        kept[s][0] = (activated, grad_ffn)
        yield
        grad_pre = (grad_activated * slope).astype(bf16)
        hidden_sum[...] += fold8(grad_pre.astype(f32))
        yield
        grad_hidden = grad_second + dot(grad_pre, in_weight[...], NT)
        kept[s][1] = (hidden_low, grad_pre)
        yield
        sums[2] += fold8(grad_hidden * normed_one)
        sums[3] += fold8(grad_hidden)
        grad_first = norm_back(grad_hidden * gain_one, normed_one, inverse_one)
        grad_branch = grad_first.astype(bf16)
        grad_branch_out[sl, :] = grad_branch
        sums[0] += fold8(grad_branch.astype(f32))
        yield
        grad_attended = dot(grad_branch, attn_weight[...], NT)
        kept[s][2] = (att, grad_branch)
        yield
        low = grad_attended.astype(bf16)
        grad_attended_out[sl, :] = low
        lane = lax.broadcasted_iota(jnp.int32, (sub, 128), 1)
        extra = jnp.zeros((sub, 128), f32)
        for h in range(HEADS):
            cols = slice(128 * h, 128 * (h + 1))
            low_cols = low[:, cols].astype(f32)
            centre = jnp.sum(low_cols * att[:, cols].astype(f32), axis=1, keepdims=True)
            for i, part in enumerate(split3(-centre)):
                extra = jnp.where(lane == 4 * h + i, part.astype(f32), extra)
        grad_extra[sl, :] = extra.astype(bf16)
        yield

    chains = [chain(s) for s in range(tokens.shape[0] // sub)]
    started = 0
    live = []
    while started < len(chains) or live:
        if started < len(chains):
            live.append(chains[started])
            started += 1
        remaining = []
        for c in live:
            try:
                next(c)
                remaining.append(c)
            except StopIteration:
                pass
        live = remaining
        for i, ref in enumerate((grad_out, grad_in, grad_attn)):
            if all(i in k for k in kept):
                left = jnp.concatenate([k[i][0] for k in kept], axis=0)
                right = jnp.concatenate([k.pop(i)[1] for k in kept], axis=0)
                ref[...] += dot(left, right, TN)

    @pl.when(step == pl.num_programs(0) - 1)
    def _():
        for base, ref in ((0, keep), (half, send)):

            def place(i, _, base=base, ref=ref):
                d = owner_of(base + i, me, order_out)
                start = i * R_ROWS
                a_row = pl.multiple_of(d * 16, 16)
                o_row = pl.multiple_of(d * 32, 16)
                for j in range(4):
                    ref[pl.ds(pl.multiple_of(start + 16 * j, 16), 16), :] = grad_attn[
                        pl.ds(a_row, 16), 128 * j : 128 * (j + 1)
                    ].astype(bf16)
                for j in range(8):
                    ref[pl.ds(pl.multiple_of(start + 64 + 16 * j, 16), 16), :] = grad_in[
                        pl.ds(a_row, 16), 128 * j : 128 * (j + 1)
                    ].astype(bf16)
                for j in range(4):
                    ref[pl.ds(pl.multiple_of(start + 192 + 32 * j, 16), 32), :] = grad_out[
                        pl.ds(o_row, 32), 128 * j : 128 * (j + 1)
                    ].astype(bf16)
                return 0

            lax.fori_loop(0, half, place, 0, unroll=True)
        vec_out[...] = jnp.zeros_like(vec_out)
        for i in range(6):
            row = jnp.sum(sums[i], axis=0, keepdims=True)
            for j in range(4):
                vec_out[8 + 4 * i + j : 9 + 4 * i + j, :] = row[:, 128 * j : 128 * (j + 1)]
        row = jnp.sum(hidden_sum[...], axis=0, keepdims=True)
        for j in range(8):
            vec_out[32 + j : 33 + j, :] = row[:, 128 * j : 128 * (j + 1)]


def middle(
    me, tokens, attended, offset, query_extra, cotangent, vec, pieces, masks, order_in, order_out, rows=512, sub=256
):
    count = tokens.shape[0]
    by_row = pl.BlockSpec((rows, 512), lambda i: (i, 0))
    half_rows = BLOCKS // 2 * R_ROWS
    return pl.pallas_call(
        functools.partial(middle_kernel, masks, order_in, order_out, sub),
        grid=(count // rows,),
        in_specs=[
            scalar_spec(),
            by_row,
            by_row,
            pl.BlockSpec((HEADS, 1, rows), lambda i: (0, 0, i)),
            pl.BlockSpec((rows, 128), lambda i: (i, 0)),
            by_row,
            whole((48, 128)),
        ]
        + [whole(piece.shape) for piece in pieces],
        out_specs=[
            by_row,
            by_row,
            by_row,
            pl.BlockSpec((rows, 128), lambda i: (i, 0)),
            pl.BlockSpec((rows, 128), lambda i: (i, 0)),
            whole((half_rows, 128)),
            whole((half_rows, 128)),
            whole((48, 128)),
        ],
        out_shape=[
            jax.ShapeDtypeStruct((count, 512), bf16),
            jax.ShapeDtypeStruct((count, 512), bf16),
            jax.ShapeDtypeStruct((count, 512), bf16),
            jax.ShapeDtypeStruct((count, 128), bf16),
            jax.ShapeDtypeStruct((count, 128), bf16),
            jax.ShapeDtypeStruct((half_rows, 128), bf16),
            jax.ShapeDtypeStruct((half_rows, 128), bf16),
            jax.ShapeDtypeStruct((48, 128), f32),
        ],
        scratch_shapes=[
            pltpu.VMEM((512, 512), bf16),
            pltpu.VMEM((512, FF), bf16),
            pltpu.VMEM((FF, 512), bf16),
            pltpu.VMEM((512, 512), f32),
            pltpu.VMEM((512, FF), f32),
            pltpu.VMEM((FF, 512), f32),
            pltpu.VMEM((6, 8, 512), f32),
            pltpu.VMEM((8, FF), f32),
        ],
        compiler_params=params("middle"),
        cost_estimate=cost(6 * count * 1310720, 22e6, 3 * count * FF),
        name="middle",
    )(me, tokens, attended, offset, query_extra, cotangent, vec, *pieces)


def attend_back_kernel(
    base,
    heads,
    order,
    vec_width,
    me_ref,
    tokens,
    q,
    k,
    v,
    grad,
    query_extra,
    keys_extra,
    grad_extra,
    vec_in,
    grad_query,
    grad_keys,
    grad_values,
    keep,
    send,
    vec,
    acc,
    all_keys,
    all_values,
    grad_weight,
    held,
    sem,
):
    local = pl.program_id(0)
    step = pl.program_id(1)
    steps = pl.num_programs(1)
    width = k.shape[0]
    last = base + heads == HEADS
    copy = pltpu.make_async_copy(tokens, held, sem)

    @pl.when((local == 0) & (step == 0))
    def _():
        copy.start()
        vec[...] = vec_in[...]

    head = base + local
    lane = lax.broadcasted_iota(jnp.int32, (width, 128), 1)
    ones = jnp.where((lane >= 4 * head) & (lane < 4 * head + 3), 1.0, 0.0).astype(bf16)
    extra = jnp.where(own_lanes(lane, head), keys_extra[...].astype(f32), 0.0).astype(bf16)
    scores = dot(
        jnp.concatenate([q[...], query_extra[...]], axis=1), jnp.concatenate([k[...], extra], axis=1), NT
    )
    centred = dot(
        jnp.concatenate([grad[...], grad_extra[...]], axis=1), jnp.concatenate([v[...], ones], axis=1), NT
    )
    probs = jnp.exp(scores)
    probs_low = probs.astype(bf16)
    grad_scores = (probs * centred).astype(bf16)
    gv = dot(grad[...], probs_low, TN).astype(bf16)
    gk = dot(q[...], grad_scores, TN).astype(bf16)
    grad_values[...] = gv
    grad_keys[...] = gk
    all_values[step] = gv
    all_keys[step] = gk
    part = dot(grad_scores, k[...], NN)

    @pl.when(step == 0)
    def _():
        acc[...] = part

    @pl.when(step > 0)
    def _():
        acc[...] += part

    @pl.when((local == 0) & (step == steps - 1))
    def _():
        copy.wait()

    @pl.when(step == steps - 1)
    def _():
        me = me_ref[0]
        scale = 1.0 / math.sqrt(HEAD_DIM)
        x = held[...]
        gq_all = acc[...].astype(bf16)
        grad_query[...] = gq_all
        gk_all = jnp.concatenate([all_keys[i] for i in range(all_keys.shape[0])], axis=1)
        gv_all = jnp.concatenate([all_values[i] for i in range(all_values.shape[0])], axis=1)
        sums = dot(jnp.concatenate([gq_all.T, gk_all, gv_all], axis=0), x, NN)
        grad_weight[0:512, :] = (sums[0:128].T * scale).astype(bf16)
        grad_weight[512:1024, :] = sums[128:256].T.astype(bf16)
        grad_weight[1024:1536, :] = sums[256:384].T.astype(bf16)
        row_ones = jnp.ones((8, x.shape[0]), bf16)
        vec[pl.ds(base + local, 1), :] = dot(row_ones, gq_all, NN)[0:1] * scale
        vec[pl.ds(4 + base + local, 1), :] = dot(row_ones, gv_all, NT)[0:1]
        half = BLOCKS // 2
        block = heads * QKV_ROWS + (16 if last else 0)
        for start, ref in ((0, keep), (half, send)):

            def place(i, _, start=start, ref=ref):
                d = owner_of(start + i, me, order)
                ref[pl.ds(pl.multiple_of(i * block + local * QKV_ROWS, 16), QKV_ROWS), :] = grad_weight[
                    pl.ds(pl.multiple_of(d * QKV_ROWS, 16), QKV_ROWS), :
                ]
                if last:
                    pair = vec[pl.ds((d * vec_width) // 128, 2), :]
                    pair = jnp.concatenate([pair, jnp.zeros((14, 128), f32)], axis=0)
                    ref[pl.ds(pl.multiple_of(i * block + heads * QKV_ROWS, 16), 16), :] = pair.astype(bf16)
                return 0

            lax.fori_loop(0, half, place, 0, unroll=True)


def attend_back(
    me, tokens, qkv, grad_attended, query_extra, keys_extra, grad_extra, vec, order, vec_width, base, heads, width=512
):
    count = qkv.shape[0]
    half_rows = BLOCKS // 2 * (heads * QKV_ROWS + (16 if base + heads == HEADS else 0))
    return pl.pallas_call(
        functools.partial(attend_back_kernel, base, heads, order, vec_width),
        grid=(heads, count // width),
        in_specs=[
            scalar_spec(),
            pl.BlockSpec(memory_space=pl.ANY),
            pl.BlockSpec((count, 128), lambda h, i: (0, base + h)),
            pl.BlockSpec((width, 128), lambda h, i: (i, HEADS + base + h)),
            pl.BlockSpec((width, 128), lambda h, i: (i, 2 * HEADS + base + h)),
            pl.BlockSpec((count, 128), lambda h, i: (0, base + h)),
            whole((count, 128)),
            pl.BlockSpec((width, 128), lambda h, i: (i, 0)),
            whole((count, 128)),
            whole((48, 128)),
        ],
        out_specs=[
            pl.BlockSpec((count, 128), lambda h, i: (0, h)),
            pl.BlockSpec((128, width), lambda h, i: (h, i)),
            pl.BlockSpec((128, width), lambda h, i: (h, i)),
            whole((half_rows, 128)),
            whole((half_rows, 128)),
            whole((48, 128)),
        ],
        out_shape=[
            jax.ShapeDtypeStruct((count, 128 * heads), bf16),
            jax.ShapeDtypeStruct((128 * heads, count), bf16),
            jax.ShapeDtypeStruct((128 * heads, count), bf16),
            jax.ShapeDtypeStruct((half_rows, 128), bf16),
            jax.ShapeDtypeStruct((half_rows, 128), bf16),
            jax.ShapeDtypeStruct((48, 128), f32),
        ],
        scratch_shapes=[
            pltpu.VMEM((count, 128), f32),
            pltpu.VMEM((count // width, 128, width), bf16),
            pltpu.VMEM((count // width, 128, width), bf16),
            pltpu.VMEM((1536, 128), bf16),
            pltpu.VMEM((count, 512), bf16),
            pltpu.SemaphoreType.DMA,
        ],
        compiler_params=params("attend_back"),
        cost_estimate=cost(heads * 20 * count * count * 128, heads * 12e6, heads * count * count),
        name="attend_back",
    )(me, tokens, qkv, qkv, qkv, grad_attended, query_extra, keys_extra, grad_extra, vec)


def input_grad_kernel(groups, *refs):
    grad_branch = refs[0]
    queries, keys, values = [refs[1 + i * groups : 1 + (i + 1) * groups] for i in range(3)]
    weight, out = refs[-2], refs[-1]
    scale = 1.0 / math.sqrt(HEAD_DIM)
    gq = jnp.concatenate([r[...] for r in queries], axis=1)
    gk = jnp.concatenate([r[...] for r in keys], axis=0)
    gv = jnp.concatenate([r[...] for r in values], axis=0)
    total = grad_branch[...].astype(f32) + scale * dot(gq, weight[0:512, :], NT)
    total = total + dot(gk, weight[512:1024, :], TT)
    out[...] = total + dot(gv, weight[1024:1536, :], TT)


def input_grad(grad_branch, queries, keys, values, weight, rows=1024):
    count = grad_branch.shape[0]
    by_row = pl.BlockSpec((rows, 512), lambda i: (i, 0))
    return pl.pallas_call(
        functools.partial(input_grad_kernel, len(queries)),
        grid=(count // rows,),
        in_specs=[by_row]
        + [pl.BlockSpec((rows, a.shape[1]), lambda i: (i, 0)) for a in queries]
        + [pl.BlockSpec((a.shape[0], rows), lambda i: (0, i)) for a in keys + values]
        + [whole((1536, 512))],
        out_specs=by_row,
        out_shape=jax.ShapeDtypeStruct((count, 512), f32),
        compiler_params=params("input_grad"),
        cost_estimate=cost(2 * count * 512 * 1536, 16e6),
        name="input_grad",
    )(grad_branch, *queries, *keys, *values, weight)


def unpack_kernel(vec_width, me_ref, *refs):
    q_parts, r_parts = refs[:4], refs[4:6]
    out, vec_out, line = refs[6:]
    q_sum, r_sum = q_parts[0][...], r_parts[0][...]
    for part in q_parts[1:]:
        q_sum = q_sum + part[...].astype(f32)
    for part in r_parts[1:]:
        r_sum = r_sum + part[...].astype(f32)
    at = 0
    source = q_sum
    for index, (start, rows, count) in enumerate(PANELS):
        if index == 1:
            source, at = r_sum, 0
        for j in range(count):
            out[pl.ds(start + j, rows, stride=count), :] = source[at : at + rows, :]
            at += rows
    pair = jnp.concatenate([q_sum[192:200, :], q_sum[193:201, :]], axis=1)
    line[...] = pltpu.roll(pair, 256 - (me_ref[0] * vec_width) % 128, 1)
    vec_out[...] = line[0:1, 0:vec_width]


def unpack(me, q_parts, r_parts, vec_width):
    vmem = pl.BlockSpec(memory_space=pltpu.VMEM)
    return pl.pallas_call(
        functools.partial(unpack_kernel, vec_width),
        in_specs=[scalar_spec()] + [vmem] * 6,
        out_shape=[jax.ShapeDtypeStruct((512, 128), f32), jax.ShapeDtypeStruct((1, vec_width), f32)],
        scratch_shapes=[pltpu.VMEM((8, 256), f32)],
        compiler_params=params("unpack"),
        name="unpack",
    )(me, *q_parts, *r_parts)


def swap(array, step, count):
    return lax.ppermute(array, AXES, [(i, i ^ step) for i in range(count)])


def swap_each(parts, steps, count):
    pairs = list(zip(parts, steps))
    return [swap(part, step, count) for part, step in pairs[::-1]][::-1]


def after(value, *others):
    return lax.optimization_barrier((value, *others))[0]


def quarters(groups):
    parts = []
    for keep, got in groups:
        keep, got = keep.reshape(4, 4, -1, 128), got.reshape(4, 4, -1, 128)
        parts.append([keep[i].astype(f32) + got[i].astype(f32) for i in range(4)])
    totals = [jnp.concatenate(same, axis=1) if len(same) > 1 else same[0] for same in zip(*parts)]
    return totals[0], [total.astype(bf16).reshape(-1, 128) for total in totals[1:]]


def halves(keep, gots):
    total = keep
    for got in gots:
        total = total + got.astype(f32).reshape(keep.shape)
    half = total.shape[0] // 2
    return total[:half], total[half:].astype(bf16).reshape(-1, 128)


def fourths(keep, gots):
    total = keep
    for got in gots:
        total = total + got.astype(f32).reshape(keep.shape)
    return [total[0]] + [total[i].astype(bf16) for i in range(1, 4)]


def fast_layout(dp, fsdp):
    return dp == 4 and fsdp == 8


def gather_line(block, steps, count):
    return jnp.concatenate([block] + [swap(block, step, count) for step in steps], axis=0)


def body(dp, fsdp, tokens, lengths, assignment, weights, vectors, cotangent):
    count = dp * fsdp
    fast = fast_layout(dp, fsdp)
    owner = lax.axis_index(AXES).astype(jnp.int32)
    owned = assignment == owner
    ends = jnp.cumsum(jnp.where(owned, lengths, 0), dtype=jnp.int32)
    ends = jnp.where(owned, ends, 1 << 30)[None, :]
    if fast:
        vec_width = vectors.shape[0]
        core, x_step, y_step, z_near, z_far = fsdp, 1, 2 * fsdp, 2, 4
        planes = [x_step, y_step, x_step + y_step]
        spread = [x_step + y_step, y_step, x_step]
        line = [z_near, z_far, z_near + z_far]
        order_in, order_rest = [z_near, z_far], [z_far, z_near]
        order_out = [z_near, z_far, x_step, y_step, core]
        order_rest_out = order_rest + order_out[2:]
        masks = [0] + spread
        masks = masks + [m + core for m in masks]
        me = owner[None]
        q_block, r_block = pack(me, pltpu.with_memory_space_constraint(weights.reshape(512, 128), pltpu.HBM), vectors.reshape(1, vec_width), vec_width)
        lines = [swap(q_block, step, count) for step in line[::-1]][::-1]
        q_far = jnp.concatenate([q_block, lines[0], lines[1], after(lines[2], ends)], axis=0)
        q_core = swap(q_far, core, count)
        q_pieces = [q_far] + [swap(q_far, step, count) for step in spread]
        r_far = gather_line(after(r_block, q_core), [z_far], count)
        r_far = gather_line(r_far, [z_near], count)
        q_pieces = q_pieces + [q_core] + [swap(piece, core, count) for piece in q_pieces[1:]]
        r_pieces = [swap(after(r_far, *q_pieces), step, count) for step in spread]
    else:
        vec_width = 160
        order_in, order_rest, order_out = [1, 2], [1, 2], [1, 2, 4, 8, 16]
        order_rest_out = order_out
        masks = [4 * i for i in range(8)]
        me = jnp.zeros((1,), jnp.int32)
        blocks = lax.all_gather(weights, AXES, axis=0, tiled=True).reshape(count, -1)
        flat = lax.all_gather(vectors, AXES, axis=0, tiled=True).reshape(40, 128)
        square = 512 * 512 // count
        cuts = [0, 3 * square, 4 * square, 6 * square, 8 * square]
        panels = []
        for index, (start, rows, width) in enumerate(PANELS):
            piece = blocks[:, cuts[index] : cuts[index + 1]].reshape(BLOCKS, rows, width, 128)
            panels.append(piece.transpose(0, 2, 1, 3).reshape(BLOCKS, rows * width, 128))
        spots = [(d * vec_width) // 128 for d in range(BLOCKS)]
        lanes = jnp.arange(256)
        vec_blocks = []
        for d in range(BLOCKS):
            pair = jnp.concatenate([flat, jnp.zeros((8, 128), bf16)], axis=0)[spots[d] : spots[d] + 2].reshape(256)
            offset = d * vec_width - 128 * spots[d]
            pair = jnp.where((lanes >= offset) & (lanes < offset + vec_width), pair, 0)
            vec_blocks.append(jnp.concatenate([pair.reshape(2, 128), jnp.zeros((14, 128), bf16)], axis=0))
        q_all = jnp.concatenate([panels[0], jnp.stack(vec_blocks)], axis=1)
        r_all = jnp.concatenate(panels[1:], axis=1)
        q_pieces = [q_all[4 * i : 4 * i + 4].reshape(-1, 128) for i in range(8)]
        r_pieces = [r_all[4 * i : 4 * i + 4].reshape(-1, 128) for i in range(8)]
    qkv, keys_extra, query_extra, vec, weight = project(
        me, ends, pltpu.with_memory_space_constraint(tokens, pltpu.HBM), q_pieces, masks, order_in, vec_width
    )
    prior = attend(qkv, query_extra, keys_extra, 0, 3, [])
    if fast:
        r_pieces = [r_far] + [after(piece, prior[0]) for piece in r_pieces]
        keys_extra = after(keys_extra, *r_pieces)
        r_pieces = r_pieces + [swap(piece, core, count) for piece in r_pieces]
    attended, offset = attend(qkv, query_extra, keys_extra, 3, 1, prior)
    layer_output, grad_branch, grad_attended, grad_extra, query_extra, r_keep, r_send, vec_grad = middle(
        me, tokens, attended, offset, query_extra, cotangent, vec, r_pieces, masks, order_rest, order_rest_out
    )
    queries, keys, values, keeps, sends, gots = [], [], [], [], [], []
    if fast:
        r_got = swap(r_send, core, count)
    for base, heads in ((0, 1), (1, 2), (3, 1)):
        gq, gk, gv, keep, send, vec_grad = attend_back(
            me,
            tokens,
            qkv,
            grad_attended,
            query_extra,
            keys_extra,
            grad_extra,
            vec_grad,
            order_out,
            vec_width,
            base,
            heads,
        )
        queries.append(gq)
        keys.append(gk)
        values.append(gv)
        keeps.append(keep)
        sends.append(send)
        if not fast:
            continue
        gots.append(swap(send, core, count))
        if base == 0:
            r_keep, r_sends = quarters([(r_keep, after(r_got, gq))])
            vec_grad = after(vec_grad, *r_sends)
            r_gots = swap_each(r_sends, planes, count)
        elif base == 1:
            r_gots = [after(part, gq) for part in r_gots]
            r_keep, r_send = halves(r_keep, r_gots)
            vec_grad = after(vec_grad, r_send)
            r_got = swap(r_send, z_near, count)
    if fast:
        r_keep, r_send = halves(r_keep, [after(r_got, gq)])
        gots = [after(got, gq) for got in gots]
        q_keep, q_sends = quarters(list(zip(keeps, gots)))
        grad_branch = after(grad_branch, *q_sends)
        q_gots = swap_each(q_sends, planes, count)
    grad_tokens = input_grad(grad_branch, queries, keys, values, weight)
    if fast:
        r_parts = [r_keep.reshape(-1, 128), swap(after(r_send, grad_tokens), z_far, count)]
        q_gots = [after(part, grad_tokens) for part in q_gots]
        q_parts = fourths(q_keep, q_gots)
        q_parts = q_parts[:1] + swap_each(q_parts[1:], line, count)
        own_weights, own_vectors = unpack(me, q_parts, r_parts, vec_width)
        own_weights = own_weights.reshape(-1)
        own_vectors = own_vectors.reshape(-1)
    else:
        heads = [jnp.concatenate([k, g], axis=0).astype(f32).reshape(BLOCKS, -1, 128) for k, g in zip(keeps, sends)]
        q_all = jnp.concatenate(heads, axis=1)
        r_all = jnp.concatenate([r_keep, r_send], axis=0).astype(f32).reshape(BLOCKS, R_ROWS, 128)
        sources = (q_all[:, : 4 * QKV_ROWS], r_all[:, :64], r_all[:, 64:192], r_all[:, 192:])
        pieces = []
        for source, (start, rows, width) in zip(sources, PANELS):
            piece = source.reshape(BLOCKS, width, rows, 128).transpose(0, 2, 1, 3)
            pieces.append(piece.reshape(count, -1))
        own_weights = lax.psum_scatter(
            jnp.concatenate(pieces, axis=1).reshape(-1), AXES, scatter_dimension=0, tiled=True
        )
        pairs = q_all[:, 4 * QKV_ROWS : 4 * QKV_ROWS + 2].reshape(BLOCKS, 256)
        rows = [
            pairs[d, (d * vec_width) % 128 : (d * vec_width) % 128 + vec_width] for d in range(BLOCKS)
        ]
        own_vectors = lax.psum_scatter(jnp.concatenate(rows), AXES, scatter_dimension=0, tiled=True)
    return (layer_output, grad_tokens, own_weights, own_vectors)


def solution(mesh):
    dp, fsdp = mesh.shape["dp"], mesh.shape["fsdp"]
    in_specs = (
        P(AXES, None),
        P(),
        P(),
        P(AXES),
        P(AXES),
        P(AXES, None),
    )
    out_specs = (
        P(AXES, None),
        P(AXES, None),
        P(AXES),
        P(AXES),
    )
    return jax.shard_map(
        functools.partial(body, dp, fsdp), mesh=mesh, in_specs=in_specs, out_specs=out_specs, check_vma=False
    )
```

```python
import functools
import math

import jax
import jax.numpy as jnp
from jax import lax
from jax.experimental import pallas as pl
from jax.experimental.pallas import tpu as pltpu
from jax.sharding import PartitionSpec as P

HEADS = 4
HEAD_DIM = 128
FF = 1024
AXES = ("dp", "fsdp")
NORM_EPS = 1e-05
BLOCKS = 32
QKV_ROWS = 48
Q_ROWS = 4 * QKV_ROWS + 16
R_ROWS = 320
FAR = -1e30
f32 = jnp.float32
bf16 = jnp.bfloat16
NT = (((1,), (1,)), ((), ()))
NN = (((1,), (0,)), ((), ()))
TN = (((0,), (0,)), ((), ()))
TT = (((0,), (1,)), ((), ()))
VMEM_MIB = {"pack": 2, "project": 22, "attend": 18, "middle": 26, "attend_back": 28, "input_grad": 14, "unpack": 3}


def dot(a, b, dims):
    return lax.dot_general(a, b, dims, preferred_element_type=f32)


def params(name):
    return pltpu.CompilerParams(vmem_limit_bytes=VMEM_MIB[name] << 20)


def cost(flops, moved, special=0):
    return pl.CostEstimate(flops=int(flops), bytes_accessed=int(moved), transcendentals=int(special))


def whole(shape):
    return pl.BlockSpec(shape, lambda *_: (0,) * len(shape))


def resident():
    return pl.BlockSpec(memory_space=pltpu.VMEM)


def scalar_spec():
    return pl.BlockSpec(memory_space=pltpu.SMEM)


def owner_of(place, me, order):
    mask = 0
    for bit, step in enumerate(order):
        mask = mask + ((place >> bit) & 1) * step
    return jnp.bitwise_xor(me, mask)


def split3(value):
    high = value.astype(bf16)
    rest = value - high.astype(f32)
    middle = rest.astype(bf16)
    low = (rest - middle.astype(f32)).astype(bf16)
    return high, middle, low


PANELS = ((0, 48, 4), (192, 16, 4), (256, 16, 8), (384, 32, 4))


def pack_kernel(vec_width, me_ref, flat, vec, q_out, r_out, wide, line):
    wide[...] = flat[...].astype(f32)
    line[...] = jnp.zeros_like(line)
    line[0:1, 0:vec_width] = vec[...].astype(f32)
    shifted = pltpu.roll(line[...], (me_ref[0] * vec_width) % 128, 1)
    parts = []
    for start, rows, count in PANELS:
        for j in range(count):
            parts.append(wide[pl.ds(start + j, rows, stride=count), :].astype(bf16))
    q_out[0:192, :] = jnp.concatenate(parts[:4], axis=0)
    placed = jnp.concatenate([shifted[0:1, 0:128], shifted[0:1, 128:256], jnp.zeros((14, 128), f32)], axis=0)
    q_out[192:208, :] = placed.astype(bf16)
    r_out[...] = jnp.concatenate(parts[4:], axis=0)


def pack(me, flat, vec, vec_width):
    vmem = pl.BlockSpec(memory_space=pltpu.VMEM)
    return pl.pallas_call(
        functools.partial(pack_kernel, vec_width),
        in_specs=[scalar_spec(), vmem, vmem],
        out_shape=[
            jax.ShapeDtypeStruct((Q_ROWS, 128), bf16),
            jax.ShapeDtypeStruct((R_ROWS, 128), bf16),
        ],
        scratch_shapes=[pltpu.VMEM((512, 128), f32), pltpu.VMEM((8, 256), f32)],
        compiler_params=params("pack"),
        name="pack",
    )(me, flat, vec)


def project_kernel(masks, order, vec_width, me_ref, ends, tokens, *refs):
    pieces = refs[: len(masks)]
    qkv, keys_extra, query_extra, vec_out, weight, vec = refs[len(masks) :]
    step = pl.program_id(0)
    rows = tokens.shape[0]
    me = me_ref[0]

    @pl.when(step == 0)
    def _():
        vec[...] = jnp.zeros_like(vec)
        for mask, ref in zip(masks, pieces):
            for i in range(1 << len(order)):
                d = owner_of(i, jnp.bitwise_xor(me, mask), order)
                row = pl.multiple_of(d * QKV_ROWS, 16)
                for j in range(4):
                    at = i * Q_ROWS + QKV_ROWS * j
                    weight[pl.ds(row, QKV_ROWS), 128 * j : 128 * (j + 1)] = ref[at : at + QKV_ROWS, :]
                row = (d * vec_width) // 128
                at = i * Q_ROWS + 4 * QKV_ROWS
                vec[pl.ds(row, 2), :] = vec[pl.ds(row, 2), :] + ref[at : at + 16, :].astype(f32)[0:2, :]
        vec_out[...] = vec[...]

    x = tokens[...]
    scale = 1.0 / math.sqrt(HEAD_DIM)
    query_bias = jnp.concatenate([vec[j : j + 1, :] for j in range(4)], axis=1)
    value_bias = jnp.concatenate([vec[4 + j : 5 + j, :] for j in range(4)], axis=1)
    queries = ((dot(x, weight[0:512, :], NN) + query_bias) * scale).astype(bf16)
    key_heads = dot(x, weight[512:1024, :], NN).astype(bf16)
    values = (dot(x, weight[1024:1536, :], NN) + value_bias).astype(bf16)
    here = pl.ds(pl.multiple_of(step * rows, rows), rows)
    qkv[here, 0:512] = queries
    qkv[here, 512:1024] = key_heads
    qkv[here, 1024:1536] = values
    places = step * rows + lax.broadcasted_iota(jnp.int32, (rows, ends.shape[1]), 0)
    label = jnp.sum((ends[...] <= places).astype(f32), axis=1, keepdims=True)
    lane = lax.broadcasted_iota(jnp.int32, (rows, 128), 1)
    same = lane.astype(f32) == label
    keys_extra[here, :] = jnp.where(lane < 8, jnp.where(same, 1.0, 0.0), jnp.where(lane < 32, 1.0, 0.0)).astype(bf16)
    apart = jnp.where((lane < 8) & jnp.logical_not(same), FAR, 0.0)
    product = queries.astype(f32) * key_heads.astype(f32)
    extra = apart
    for h in range(HEADS):
        own = jnp.sum(product[:, 128 * h : 128 * (h + 1)], axis=1, keepdims=True)
        extra = jnp.where(lane == 8 + h, -own, extra)
    query_extra[here, :] = extra.astype(bf16)


def project(me, ends, tokens, pieces, masks, order, vec_width, rows=1024):
    count = tokens.shape[0]
    sets = ends.shape[1]
    return pl.pallas_call(
        functools.partial(project_kernel, masks, order, vec_width),
        grid=(count // rows,),
        in_specs=[
            scalar_spec(),
            whole((1, sets)),
            pl.BlockSpec((rows, 512), lambda i: (i, 0)),
        ]
        + [resident() for _ in pieces],
        out_specs=[resident() for _ in range(5)],
        out_shape=[
            jax.ShapeDtypeStruct((count, 1536), bf16),
            jax.ShapeDtypeStruct((count, 128), bf16),
            jax.ShapeDtypeStruct((count, 128), bf16),
            jax.ShapeDtypeStruct((48, 128), f32),
            jax.ShapeDtypeStruct((1536, 512), bf16),
        ],
        scratch_shapes=[pltpu.VMEM((48, 128), f32)],
        compiler_params=params("project"),
        cost_estimate=cost(2 * count * 512 * 1536, 12e6),
        name="project",
    )(me, ends, tokens, *pieces)


def own_lanes(lane, head):
    return (lane < 8) | (lane == 8 + head) | ((lane >= 16 + 4 * head) & (lane < 19 + 4 * head))


def attend_kernel(base, rows, qkv, query_extra, keys_extra, attended, offset_out, total, mixed, peak):
    local = pl.program_id(0)
    head = base + local
    start = pl.program_id(1) * rows
    here = pl.ds(pl.multiple_of(start, rows), rows)

    def columns(first):
        return pl.ds(pl.multiple_of(128 * (first + head), 128), 128)

    v = qkv[:, columns(2 * HEADS)]
    lane = lax.broadcasted_iota(jnp.int32, (rows, 128), 1)
    extra = jnp.where(own_lanes(lane, head), query_extra[here, :].astype(f32), 0.0).astype(bf16)
    left = jnp.concatenate([qkv[:, columns(HEADS)], keys_extra[...]], axis=1)
    right = jnp.concatenate([qkv[here, columns(0)], extra], axis=1)
    weights = jnp.exp(dot(left, right, NT))
    total[...] = jnp.sum(weights, axis=0, keepdims=True)
    mixed[...] = dot(v, weights.astype(bf16), TN)
    peak[...] = jnp.zeros_like(peak)
    good = (total[...] > 1e-20) & (total[...] < 1e30)

    @pl.when(jnp.sum(jnp.where(good, 0.0, 1.0)) > 0.0)
    def _():
        def part(j, _):
            place = pl.ds(pl.multiple_of(j * 128, 128), 128)
            some = pl.ds(pl.multiple_of(start + j * 128, 128), 128)
            lane = lax.broadcasted_iota(jnp.int32, (128, 128), 1)
            extra = jnp.where(own_lanes(lane, head), query_extra[some, :].astype(f32), 0.0).astype(bf16)
            again = dot(left, jnp.concatenate([qkv[some, columns(0)], extra], axis=1), NT)
            top = jnp.max(again, axis=0, keepdims=True)
            safe = jnp.exp(again - top)
            total[:, place] = jnp.sum(safe, axis=0, keepdims=True)
            mixed[:, place] = dot(v, safe.astype(bf16), TN)
            peak[:, place] = top
            return 0

        lax.fori_loop(0, rows // 128, part, 0)

    own = pl.ds(pl.multiple_of(128 * local, 128), 128)
    attended[here, own] = (mixed[...] * (1.0 / total[...])).T.astype(bf16)
    offset_out[local, :, here] = peak[...] + jnp.log(total[...])


def attend(qkv, query_extra, keys_extra, base, heads, rows=1024):
    count = qkv.shape[0]
    return pl.pallas_call(
        functools.partial(attend_kernel, base, rows),
        grid=(heads, count // rows),
        in_specs=[resident() for _ in range(3)],
        out_specs=[resident() for _ in range(2)],
        out_shape=[
            jax.ShapeDtypeStruct((count, 128 * heads), bf16),
            jax.ShapeDtypeStruct((heads, 1, count), f32),
        ],
        scratch_shapes=[pltpu.VMEM((1, rows), f32), pltpu.VMEM((128, rows), f32), pltpu.VMEM((1, rows), f32)],
        compiler_params=params("attend"),
        cost_estimate=cost(heads * 8 * count * count * 128, 6e6, heads * count * count),
        name="attend",
    )(qkv, query_extra, keys_extra)


def mean_row(value):
    return jnp.sum(value, axis=1, keepdims=True) * (1.0 / value.shape[1])


def norm_rows(summed):
    centered = summed - mean_row(summed)
    inverse = lax.rsqrt(mean_row(centered * centered) + NORM_EPS)
    return centered * inverse, inverse


def norm_back(grad, normed, inverse):
    return inverse * (grad - mean_row(grad) - normed * mean_row(grad * normed))


def fold8(value):
    return jnp.sum(value.reshape(value.shape[0] // 8, 8, value.shape[1]), axis=0)


def middle_kernel(
    masks,
    order_in,
    order_out,
    rows,
    sub,
    me_ref,
    tokens,
    attended_a,
    attended_b,
    offset_a,
    offset_b,
    query_extra,
    cotangent,
    vec,
    *refs,
):
    pieces = refs[: len(masks)]
    layer_output, grad_branch_out, grad_attended_out, grad_extra, query_extra_out, keep, send, vec_out = refs[
        len(masks) : -8
    ]
    attn_weight, in_weight, out_weight, grad_attn, grad_in, grad_out, sums, hidden_sum = refs[-8:]
    step = pl.program_id(0)
    me = me_ref[0]
    half = BLOCKS // 2

    @pl.when(step == 0)
    def _():
        for mask, ref in zip(masks, pieces):

            def place(i, _, mask=mask, ref=ref):
                d = owner_of(i, jnp.bitwise_xor(me, mask), order_in)
                start = i * R_ROWS
                a_row = pl.multiple_of(d * 16, 16)
                o_row = pl.multiple_of(d * 32, 16)
                for j in range(4):
                    attn_weight[pl.ds(a_row, 16), 128 * j : 128 * (j + 1)] = ref[
                        pl.ds(pl.multiple_of(start + 16 * j, 16), 16), :
                    ]
                for j in range(8):
                    in_weight[pl.ds(a_row, 16), 128 * j : 128 * (j + 1)] = ref[
                        pl.ds(pl.multiple_of(start + 64 + 16 * j, 16), 16), :
                    ]
                for j in range(4):
                    out_weight[pl.ds(o_row, 32), 128 * j : 128 * (j + 1)] = ref[
                        pl.ds(pl.multiple_of(start + 192 + 32 * j, 16), 32), :
                    ]
                return 0

            lax.fori_loop(0, 1 << len(order_in), place, 0, unroll=True)
        grad_attn[...] = jnp.zeros_like(grad_attn)
        grad_in[...] = jnp.zeros_like(grad_in)
        grad_out[...] = jnp.zeros_like(grad_out)
        sums[...] = jnp.zeros_like(sums)
        hidden_sum[...] = jnp.zeros_like(hidden_sum)

    def row_of(index):
        return jnp.concatenate([vec[4 * index + j : 4 * index + j + 1, :] for j in range(4)], axis=1)

    attn_bias, ffn_bias, gain_one, shift_one, gain_two, shift_two = [row_of(i) for i in range(2, 8)]
    hidden_bias = jnp.concatenate([vec[32 + j : 33 + j, :] for j in range(8)], axis=1)

    first_row = pl.multiple_of(step * rows, rows)
    here = pl.ds(first_row, rows)
    parts = [offset_a[h, :, here] for h in range(3)] + [offset_b[0, :, here], jnp.zeros((4, rows), f32)]
    offsets = jnp.concatenate(parts, axis=0).T
    lane = lax.broadcasted_iota(jnp.int32, (rows, 128), 1)
    extra = query_extra[here, :].astype(f32)
    for h in range(HEADS):
        for i, part in enumerate(split3(-offsets[:, h : h + 1])):
            extra = jnp.where(lane == 16 + 4 * h + i, part.astype(f32), extra)
    query_extra_out[here, :] = extra.astype(bf16)

    kept = [{} for _ in range(rows // sub)]

    def chain(s):
        out = slice(s * sub, (s + 1) * sub)
        sl = pl.ds(pl.multiple_of(step * rows + s * sub, sub), sub)
        att = jnp.concatenate([attended_a[sl, :], attended_b[sl, :]], axis=1)
        branch = dot(att, attn_weight[...], NN) + attn_bias
        yield
        normed_one, inverse_one = norm_rows(tokens[sl, :].astype(f32) + branch)
        hidden = normed_one * gain_one + shift_one
        hidden_low = hidden.astype(bf16)
        yield
        pre_act = dot(hidden_low, in_weight[...], NN) + hidden_bias
        yield
        cdf = 0.5 * (1.0 + lax.erf(pre_act * 0.7071067811865476))
        density = jnp.exp(-0.5 * pre_act * pre_act) * 0.3989422804014327
        activated = (pre_act * cdf).astype(bf16)
        slope = cdf + pre_act * density
        yield
        ffn_result = dot(activated, out_weight[...], NN) + ffn_bias
        yield
        normed_two, inverse_two = norm_rows(hidden + ffn_result)
        layer_output[out, :] = (normed_two * gain_two + shift_two).astype(bf16)
        grad_result = cotangent[sl, :].astype(f32)
        sums[4] += fold8(grad_result * normed_two)
        sums[5] += fold8(grad_result)
        grad_second = norm_back(grad_result * gain_two, normed_two, inverse_two)
        grad_ffn = grad_second.astype(bf16)
        sums[1] += fold8(grad_ffn.astype(f32))
        yield
        grad_activated = dot(grad_ffn, out_weight[...], NT)
        kept[s][0] = (activated, grad_ffn)
        yield
        grad_pre = (grad_activated * slope).astype(bf16)
        hidden_sum[...] += fold8(grad_pre.astype(f32))
        yield
        grad_hidden = grad_second + dot(grad_pre, in_weight[...], NT)
        kept[s][1] = (hidden_low, grad_pre)
        yield
        sums[2] += fold8(grad_hidden * normed_one)
        sums[3] += fold8(grad_hidden)
        grad_first = norm_back(grad_hidden * gain_one, normed_one, inverse_one)
        grad_branch = grad_first.astype(bf16)
        grad_branch_out[sl, :] = grad_branch
        sums[0] += fold8(grad_branch.astype(f32))
        yield
        grad_attended = dot(grad_branch, attn_weight[...], NT)
        kept[s][2] = (att, grad_branch)
        yield
        low = grad_attended.astype(bf16)
        grad_attended_out[sl, :] = low
        lane = lax.broadcasted_iota(jnp.int32, (sub, 128), 1)
        extra = jnp.zeros((sub, 128), f32)
        for h in range(HEADS):
            cols = slice(128 * h, 128 * (h + 1))
            low_cols = low[:, cols].astype(f32)
            centre = jnp.sum(low_cols * att[:, cols].astype(f32), axis=1, keepdims=True)
            for i, part in enumerate(split3(-centre)):
                extra = jnp.where(lane == 4 * h + i, part.astype(f32), extra)
        grad_extra[sl, :] = extra.astype(bf16)
        yield

    chains = [chain(s) for s in range(rows // sub)]
    started = 0
    live = []
    while started < len(chains) or live:
        if started < len(chains):
            live.append(chains[started])
            started += 1
        remaining = []
        for c in live:
            try:
                next(c)
                remaining.append(c)
            except StopIteration:
                pass
        live = remaining
        for i, ref in enumerate((grad_out, grad_in, grad_attn)):
            if all(i in k for k in kept):
                left = jnp.concatenate([k[i][0] for k in kept], axis=0)
                right = jnp.concatenate([k.pop(i)[1] for k in kept], axis=0)
                ref[...] += dot(left, right, TN)

    @pl.when(step == pl.num_programs(0) - 1)
    def _():
        for base, ref in ((0, keep), (half, send)):

            def place(i, _, base=base, ref=ref):
                d = owner_of(base + i, me, order_out)
                start = i * R_ROWS
                a_row = pl.multiple_of(d * 16, 16)
                o_row = pl.multiple_of(d * 32, 16)
                for j in range(4):
                    ref[pl.ds(pl.multiple_of(start + 16 * j, 16), 16), :] = grad_attn[
                        pl.ds(a_row, 16), 128 * j : 128 * (j + 1)
                    ].astype(bf16)
                for j in range(8):
                    ref[pl.ds(pl.multiple_of(start + 64 + 16 * j, 16), 16), :] = grad_in[
                        pl.ds(a_row, 16), 128 * j : 128 * (j + 1)
                    ].astype(bf16)
                for j in range(4):
                    ref[pl.ds(pl.multiple_of(start + 192 + 32 * j, 16), 32), :] = grad_out[
                        pl.ds(o_row, 32), 128 * j : 128 * (j + 1)
                    ].astype(bf16)
                return 0

            lax.fori_loop(0, half, place, 0, unroll=True)
        vec_out[...] = jnp.zeros_like(vec_out)
        for i in range(6):
            row = jnp.sum(sums[i], axis=0, keepdims=True)
            for j in range(4):
                vec_out[8 + 4 * i + j : 9 + 4 * i + j, :] = row[:, 128 * j : 128 * (j + 1)]
        row = jnp.sum(hidden_sum[...], axis=0, keepdims=True)
        for j in range(8):
            vec_out[32 + j : 33 + j, :] = row[:, 128 * j : 128 * (j + 1)]


def middle(me, tokens, attended, offset, query_extra, cotangent, vec, pieces, masks, order_in, order_out, rows=512, sub=256):
    count = tokens.shape[0]
    half_rows = BLOCKS // 2 * R_ROWS
    return pl.pallas_call(
        functools.partial(middle_kernel, masks, order_in, order_out, rows, sub),
        grid=(count // rows,),
        in_specs=[scalar_spec()] + [resident() for _ in range(8 + len(pieces))],
        out_specs=[pl.BlockSpec((rows, 512), lambda i: (i, 0))] + [resident() for _ in range(7)],
        out_shape=[
            jax.ShapeDtypeStruct((count, 512), bf16),
            jax.ShapeDtypeStruct((count, 512), bf16),
            jax.ShapeDtypeStruct((count, 512), bf16),
            jax.ShapeDtypeStruct((count, 128), bf16),
            jax.ShapeDtypeStruct((count, 128), bf16),
            jax.ShapeDtypeStruct((half_rows, 128), bf16),
            jax.ShapeDtypeStruct((half_rows, 128), bf16),
            jax.ShapeDtypeStruct((48, 128), f32),
        ],
        scratch_shapes=[
            pltpu.VMEM((512, 512), bf16),
            pltpu.VMEM((512, FF), bf16),
            pltpu.VMEM((FF, 512), bf16),
            pltpu.VMEM((512, 512), f32),
            pltpu.VMEM((512, FF), f32),
            pltpu.VMEM((FF, 512), f32),
            pltpu.VMEM((6, 8, 512), f32),
            pltpu.VMEM((8, FF), f32),
        ],
        compiler_params=params("middle"),
        cost_estimate=cost(6 * count * 1310720, 22e6, 3 * count * FF),
        name="middle",
    )(me, tokens, *attended, *offset, query_extra, cotangent, vec, *pieces)


def attend_back_kernel(
    base,
    heads,
    width,
    order,
    vec_width,
    me_ref,
    tokens,
    qkv,
    grad_all,
    query_extra,
    keys_extra,
    grad_extra,
    vec_in,
    grad_query,
    grad_keys,
    grad_values,
    keep,
    send,
    vec,
    acc,
    all_keys,
    all_values,
    grad_weight,
):
    local = pl.program_id(0)
    step = pl.program_id(1)
    steps = pl.num_programs(1)
    last = base + heads == HEADS

    @pl.when((local == 0) & (step == 0))
    def _():
        vec[...] = vec_in[...]

    head = base + local
    keys = pl.ds(pl.multiple_of(step * width, width), width)

    def columns(first):
        return pl.ds(pl.multiple_of(128 * (first + head), 128), 128)

    q = qkv[:, columns(0)]
    k = qkv[keys, columns(HEADS)]
    v = qkv[keys, columns(2 * HEADS)]
    grad = grad_all[:, columns(0)]
    lane = lax.broadcasted_iota(jnp.int32, (width, 128), 1)
    ones = jnp.where((lane >= 4 * head) & (lane < 4 * head + 3), 1.0, 0.0).astype(bf16)
    extra = jnp.where(own_lanes(lane, head), keys_extra[keys, :].astype(f32), 0.0).astype(bf16)
    scores = dot(jnp.concatenate([q, query_extra[...]], axis=1), jnp.concatenate([k, extra], axis=1), NT)
    centred = dot(jnp.concatenate([grad, grad_extra[...]], axis=1), jnp.concatenate([v, ones], axis=1), NT)
    probs = jnp.exp(scores)
    probs_low = probs.astype(bf16)
    grad_scores = (probs * centred).astype(bf16)
    gv = dot(grad, probs_low, TN).astype(bf16)
    gk = dot(q, grad_scores, TN).astype(bf16)
    own_rows = pl.ds(pl.multiple_of(local * 128, 128), 128)
    grad_values[own_rows, keys] = gv
    grad_keys[own_rows, keys] = gk
    all_values[step] = gv
    all_keys[step] = gk
    part = dot(grad_scores, k, NN)

    @pl.when(step == 0)
    def _():
        acc[...] = part

    @pl.when(step > 0)
    def _():
        acc[...] += part

    @pl.when(step == steps - 1)
    def _():
        me = me_ref[0]
        scale = 1.0 / math.sqrt(HEAD_DIM)
        x = tokens[...]
        gq_all = acc[...].astype(bf16)
        grad_query[:, pl.ds(pl.multiple_of(local * 128, 128), 128)] = gq_all
        gk_all = jnp.concatenate([all_keys[i] for i in range(all_keys.shape[0])], axis=1)
        gv_all = jnp.concatenate([all_values[i] for i in range(all_values.shape[0])], axis=1)
        sums = dot(jnp.concatenate([gq_all.T, gk_all, gv_all], axis=0), x, NN)
        grad_weight[0:512, :] = (sums[0:128].T * scale).astype(bf16)
        grad_weight[512:1024, :] = sums[128:256].T.astype(bf16)
        grad_weight[1024:1536, :] = sums[256:384].T.astype(bf16)
        row_ones = jnp.ones((8, x.shape[0]), bf16)
        vec[pl.ds(base + local, 1), :] = dot(row_ones, gq_all, NN)[0:1] * scale
        vec[pl.ds(4 + base + local, 1), :] = dot(row_ones, gv_all, NT)[0:1]
        half = BLOCKS // 2
        block = heads * QKV_ROWS + (16 if last else 0)
        for start, ref in ((0, keep), (half, send)):

            def place(i, _, start=start, ref=ref):
                d = owner_of(start + i, me, order)
                ref[pl.ds(pl.multiple_of(i * block + local * QKV_ROWS, 16), QKV_ROWS), :] = grad_weight[
                    pl.ds(pl.multiple_of(d * QKV_ROWS, 16), QKV_ROWS), :
                ]
                if last:
                    pair = vec[pl.ds((d * vec_width) // 128, 2), :]
                    pair = jnp.concatenate([pair, jnp.zeros((14, 128), f32)], axis=0)
                    ref[pl.ds(pl.multiple_of(i * block + heads * QKV_ROWS, 16), 16), :] = pair.astype(bf16)
                return 0

            lax.fori_loop(0, half, place, 0, unroll=True)


def attend_back(
    me, tokens, qkv, grad_attended, query_extra, keys_extra, grad_extra, vec, order, vec_width, base, heads, width=512
):
    count = qkv.shape[0]
    half_rows = BLOCKS // 2 * (heads * QKV_ROWS + (16 if base + heads == HEADS else 0))
    return pl.pallas_call(
        functools.partial(attend_back_kernel, base, heads, width, order, vec_width),
        grid=(heads, count // width),
        in_specs=[scalar_spec()] + [resident() for _ in range(7)],
        out_specs=[resident() for _ in range(6)],
        out_shape=[
            jax.ShapeDtypeStruct((count, 128 * heads), bf16),
            jax.ShapeDtypeStruct((128 * heads, count), bf16),
            jax.ShapeDtypeStruct((128 * heads, count), bf16),
            jax.ShapeDtypeStruct((half_rows, 128), bf16),
            jax.ShapeDtypeStruct((half_rows, 128), bf16),
            jax.ShapeDtypeStruct((48, 128), f32),
        ],
        scratch_shapes=[
            pltpu.VMEM((count, 128), f32),
            pltpu.VMEM((count // width, 128, width), bf16),
            pltpu.VMEM((count // width, 128, width), bf16),
            pltpu.VMEM((1536, 128), bf16),
        ],
        compiler_params=params("attend_back"),
        cost_estimate=cost(heads * 20 * count * count * 128, heads * 12e6, heads * count * count),
        name="attend_back",
    )(me, tokens, qkv, grad_attended, query_extra, keys_extra, grad_extra, vec)


def input_grad_kernel(groups, rows, *refs):
    grad_branch = refs[0]
    queries, keys, values = [refs[1 + i * groups : 1 + (i + 1) * groups] for i in range(3)]
    weight, out = refs[-2], refs[-1]
    scale = 1.0 / math.sqrt(HEAD_DIM)
    here = pl.ds(pl.multiple_of(pl.program_id(0) * rows, rows), rows)
    gq = jnp.concatenate([r[here, :] for r in queries], axis=1)
    gk = jnp.concatenate([r[:, here] for r in keys], axis=0)
    gv = jnp.concatenate([r[:, here] for r in values], axis=0)
    total = grad_branch[here, :].astype(f32) + scale * dot(gq, weight[0:512, :], NT)
    total = total + dot(gk, weight[512:1024, :], TT)
    out[...] = total + dot(gv, weight[1024:1536, :], TT)


def input_grad(grad_branch, queries, keys, values, weight, rows=1024):
    count = grad_branch.shape[0]
    by_row = pl.BlockSpec((rows, 512), lambda i: (i, 0))
    return pl.pallas_call(
        functools.partial(input_grad_kernel, len(queries), rows),
        grid=(count // rows,),
        in_specs=[resident() for _ in range(2 + 3 * len(queries))],
        out_specs=by_row,
        out_shape=jax.ShapeDtypeStruct((count, 512), f32),
        compiler_params=params("input_grad"),
        cost_estimate=cost(2 * count * 512 * 1536, 16e6),
        name="input_grad",
    )(grad_branch, *queries, *keys, *values, weight)


def unpack_kernel(vec_width, me_ref, *refs):
    q_parts, r_parts = refs[:4], refs[4:6]
    out, vec_out, line = refs[6:]
    q_sum, r_sum = q_parts[0][...], r_parts[0][...]
    for part in q_parts[1:]:
        q_sum = q_sum + part[...].astype(f32)
    for part in r_parts[1:]:
        r_sum = r_sum + part[...].astype(f32)
    at = 0
    source = q_sum
    for index, (start, rows, count) in enumerate(PANELS):
        if index == 1:
            source, at = r_sum, 0
        for j in range(count):
            out[pl.ds(start + j, rows, stride=count), :] = source[at : at + rows, :]
            at += rows
    pair = jnp.concatenate([q_sum[192:200, :], q_sum[193:201, :]], axis=1)
    line[...] = pltpu.roll(pair, 256 - (me_ref[0] * vec_width) % 128, 1)
    vec_out[...] = line[0:1, 0:vec_width]


def unpack(me, q_parts, r_parts, vec_width):
    vmem = pl.BlockSpec(memory_space=pltpu.VMEM)
    return pl.pallas_call(
        functools.partial(unpack_kernel, vec_width),
        in_specs=[scalar_spec()] + [vmem] * 6,
        out_shape=[jax.ShapeDtypeStruct((512, 128), f32), jax.ShapeDtypeStruct((1, vec_width), f32)],
        scratch_shapes=[pltpu.VMEM((8, 256), f32)],
        compiler_params=params("unpack"),
        name="unpack",
    )(me, *q_parts, *r_parts)


def swap(array, step, count):
    return lax.ppermute(array, AXES, [(i, i ^ step) for i in range(count)])


def swap_each(parts, steps, count):
    pairs = list(zip(parts, steps))
    return [swap(part, step, count) for part, step in pairs[::-1]][::-1]


def after(value, *others):
    return lax.optimization_barrier((value, *others))[0]


def quarters(groups):
    parts = []
    for keep, got in groups:
        keep, got = keep.reshape(4, 4, -1, 128), got.reshape(4, 4, -1, 128)
        parts.append([keep[i].astype(f32) + got[i].astype(f32) for i in range(4)])
    totals = [jnp.concatenate(same, axis=1) if len(same) > 1 else same[0] for same in zip(*parts)]
    return totals[0], [total.astype(bf16).reshape(-1, 128) for total in totals[1:]]


def halves(keep, gots):
    total = keep
    for got in gots:
        total = total + got.astype(f32).reshape(keep.shape)
    half = total.shape[0] // 2
    return total[:half], total[half:].astype(bf16).reshape(-1, 128)


def fourths(keep, gots):
    total = keep
    for got in gots:
        total = total + got.astype(f32).reshape(keep.shape)
    return [total[0]] + [total[i].astype(bf16) for i in range(1, 4)]


def fast_layout(dp, fsdp):
    return dp == 4 and fsdp == 8


def gather_line(block, steps, count):
    return jnp.concatenate([block] + [swap(block, step, count) for step in steps], axis=0)


def body(dp, fsdp, tokens, lengths, assignment, weights, vectors, cotangent):
    count = dp * fsdp
    fast = fast_layout(dp, fsdp)
    owner = lax.axis_index(AXES).astype(jnp.int32)
    owned = assignment == owner
    ends = jnp.cumsum(jnp.where(owned, lengths, 0), dtype=jnp.int32)
    ends = jnp.where(owned, ends, 1 << 30)[None, :]
    if fast:
        vec_width = vectors.shape[0]
        core, x_step, y_step, z_near, z_far = fsdp, 1, 2 * fsdp, 2, 4
        planes = [x_step, y_step, x_step + y_step]
        spread = [x_step + y_step, y_step, x_step]
        line = [z_near, z_far, z_near + z_far]
        order_in, order_rest = [z_near, z_far], [z_far, z_near]
        order_out = [z_near, z_far, x_step, y_step, core]
        order_rest_out = order_rest + order_out[2:]
        masks = [0] + spread
        masks = masks + [m + core for m in masks]
        me = owner[None]
        q_block, r_block = pack(me, pltpu.with_memory_space_constraint(weights.reshape(512, 128), pltpu.HBM), vectors.reshape(1, vec_width), vec_width)
        lines = [swap(q_block, step, count) for step in line[::-1]][::-1]
        q_far = jnp.concatenate([q_block, lines[0], lines[1], after(lines[2], ends)], axis=0)
        q_core = swap(q_far, core, count)
        q_pieces = [q_far] + [swap(q_far, step, count) for step in spread]
        r_far = gather_line(after(r_block, q_core), [z_far], count)
        r_far = gather_line(r_far, [z_near], count)
        q_pieces = q_pieces + [q_core] + [swap(piece, core, count) for piece in q_pieces[1:]]
        r_pieces = [swap(after(r_far, *q_pieces), step, count) for step in spread]
    else:
        vec_width = 160
        order_in, order_rest, order_out = [1, 2], [1, 2], [1, 2, 4, 8, 16]
        order_rest_out = order_out
        masks = [4 * i for i in range(8)]
        me = jnp.zeros((1,), jnp.int32)
        blocks = lax.all_gather(weights, AXES, axis=0, tiled=True).reshape(count, -1)
        flat = lax.all_gather(vectors, AXES, axis=0, tiled=True).reshape(40, 128)
        square = 512 * 512 // count
        cuts = [0, 3 * square, 4 * square, 6 * square, 8 * square]
        panels = []
        for index, (start, rows, width) in enumerate(PANELS):
            piece = blocks[:, cuts[index] : cuts[index + 1]].reshape(BLOCKS, rows, width, 128)
            panels.append(piece.transpose(0, 2, 1, 3).reshape(BLOCKS, rows * width, 128))
        spots = [(d * vec_width) // 128 for d in range(BLOCKS)]
        lanes = jnp.arange(256)
        vec_blocks = []
        for d in range(BLOCKS):
            pair = jnp.concatenate([flat, jnp.zeros((8, 128), bf16)], axis=0)[spots[d] : spots[d] + 2].reshape(256)
            offset = d * vec_width - 128 * spots[d]
            pair = jnp.where((lanes >= offset) & (lanes < offset + vec_width), pair, 0)
            vec_blocks.append(jnp.concatenate([pair.reshape(2, 128), jnp.zeros((14, 128), bf16)], axis=0))
        q_all = jnp.concatenate([panels[0], jnp.stack(vec_blocks)], axis=1)
        r_all = jnp.concatenate(panels[1:], axis=1)
        q_pieces = [q_all[4 * i : 4 * i + 4].reshape(-1, 128) for i in range(8)]
        r_pieces = [r_all[4 * i : 4 * i + 4].reshape(-1, 128) for i in range(8)]
    qkv, keys_extra, query_extra, vec, weight = project(
        me, ends, pltpu.with_memory_space_constraint(tokens, pltpu.HBM), q_pieces, masks, order_in, vec_width
    )
    attended_a, offset_a = attend(qkv, query_extra, keys_extra, 0, 3)
    if fast:
        r_pieces = [r_far] + [after(piece, attended_a) for piece in r_pieces]
        keys_extra = after(keys_extra, *r_pieces)
        r_pieces = r_pieces + [swap(piece, core, count) for piece in r_pieces]
    attended_b, offset_b = attend(qkv, query_extra, keys_extra, 3, 1)
    layer_output, grad_branch, grad_attended, grad_extra, query_extra, r_keep, r_send, vec_grad = middle(
        me, tokens, (attended_a, attended_b), (offset_a, offset_b), query_extra, cotangent, vec, r_pieces, masks, order_rest, order_rest_out
    )
    queries, keys, values, keeps, sends, gots = [], [], [], [], [], []
    if fast:
        r_got = swap(r_send, core, count)
    for base, heads in ((0, 1), (1, 2), (3, 1)):
        gq, gk, gv, keep, send, vec_grad = attend_back(
            me,
            tokens,
            qkv,
            grad_attended,
            query_extra,
            keys_extra,
            grad_extra,
            vec_grad,
            order_out,
            vec_width,
            base,
            heads,
        )
        queries.append(gq)
        keys.append(gk)
        values.append(gv)
        keeps.append(keep)
        sends.append(send)
        if not fast:
            continue
        gots.append(swap(send, core, count))
        if base == 0:
            r_keep, r_sends = quarters([(r_keep, after(r_got, gq))])
            vec_grad = after(vec_grad, *r_sends)
            r_gots = swap_each(r_sends, planes, count)
        elif base == 1:
            r_gots = [after(part, gq) for part in r_gots]
            r_keep, r_send = halves(r_keep, r_gots)
            vec_grad = after(vec_grad, r_send)
            r_got = swap(r_send, z_near, count)
    if fast:
        r_keep, r_send = halves(r_keep, [after(r_got, gq)])
        gots = [after(got, gq) for got in gots]
        q_keep, q_sends = quarters(list(zip(keeps, gots)))
        grad_branch = after(grad_branch, *q_sends)
        q_gots = swap_each(q_sends, planes, count)
    grad_tokens = input_grad(grad_branch, queries, keys, values, weight)
    if fast:
        r_parts = [r_keep.reshape(-1, 128), swap(after(r_send, grad_tokens), z_far, count)]
        q_gots = [after(part, grad_tokens) for part in q_gots]
        q_parts = fourths(q_keep, q_gots)
        q_parts = q_parts[:1] + swap_each(q_parts[1:], line, count)
        own_weights, own_vectors = unpack(me, q_parts, r_parts, vec_width)
        own_weights = own_weights.reshape(-1)
        own_vectors = own_vectors.reshape(-1)
    else:
        heads = [jnp.concatenate([k, g], axis=0).astype(f32).reshape(BLOCKS, -1, 128) for k, g in zip(keeps, sends)]
        q_all = jnp.concatenate(heads, axis=1)
        r_all = jnp.concatenate([r_keep, r_send], axis=0).astype(f32).reshape(BLOCKS, R_ROWS, 128)
        sources = (q_all[:, : 4 * QKV_ROWS], r_all[:, :64], r_all[:, 64:192], r_all[:, 192:])
        pieces = []
        for source, (start, rows, width) in zip(sources, PANELS):
            piece = source.reshape(BLOCKS, width, rows, 128).transpose(0, 2, 1, 3)
            pieces.append(piece.reshape(count, -1))
        own_weights = lax.psum_scatter(
            jnp.concatenate(pieces, axis=1).reshape(-1), AXES, scatter_dimension=0, tiled=True
        )
        pairs = q_all[:, 4 * QKV_ROWS : 4 * QKV_ROWS + 2].reshape(BLOCKS, 256)
        rows = [
            pairs[d, (d * vec_width) % 128 : (d * vec_width) % 128 + vec_width] for d in range(BLOCKS)
        ]
        own_vectors = lax.psum_scatter(jnp.concatenate(rows), AXES, scatter_dimension=0, tiled=True)
    return (layer_output, grad_tokens, own_weights, own_vectors)


def solution(mesh):
    dp, fsdp = mesh.shape["dp"], mesh.shape["fsdp"]
    in_specs = (
        P(AXES, None),
        P(),
        P(),
        P(AXES),
        P(AXES),
        P(AXES, None),
    )
    out_specs = (
        P(AXES, None),
        P(AXES, None),
        P(AXES),
        P(AXES),
    )
    return jax.shard_map(
        functools.partial(body, dp, fsdp), mesh=mesh, in_specs=in_specs, out_specs=out_specs, check_vma=False
    )
```

```python
import functools
import math

import jax
import jax.numpy as jnp
from jax import lax
from jax.experimental import pallas as pl
from jax.experimental.pallas import tpu as pltpu
from jax.sharding import PartitionSpec as P

HEADS = 4
HEAD_DIM = 128
FF = 1024
AXES = ("dp", "fsdp")
NORM_EPS = 1e-05
BLOCKS = 32
QKV_ROWS = 48
Q_ROWS = 4 * QKV_ROWS + 16
R_ROWS = 320
FAR = -1e30
f32 = jnp.float32
bf16 = jnp.bfloat16
NT = (((1,), (1,)), ((), ()))
NN = (((1,), (0,)), ((), ()))
TN = (((0,), (0,)), ((), ()))
TT = (((0,), (1,)), ((), ()))
VMEM_MIB = {"pack": 2, "fetch": 4, "project": 22, "attend": 18, "middle": 26, "attend_back": 28, "input_grad": 14, "unpack": 3}


def dot(a, b, dims):
    return lax.dot_general(a, b, dims, preferred_element_type=f32)


def params(name):
    return pltpu.CompilerParams(vmem_limit_bytes=VMEM_MIB[name] << 20)


def cost(flops, moved, special=0):
    return pl.CostEstimate(flops=int(flops), bytes_accessed=int(moved), transcendentals=int(special))


def whole(shape):
    return pl.BlockSpec(shape, lambda *_: (0,) * len(shape))


def resident():
    return pl.BlockSpec(memory_space=pltpu.VMEM)


def scalar_spec():
    return pl.BlockSpec(memory_space=pltpu.SMEM)


def owner_of(place, me, order):
    mask = 0
    for bit, step in enumerate(order):
        mask = mask + ((place >> bit) & 1) * step
    return jnp.bitwise_xor(me, mask)


def split3(value):
    high = value.astype(bf16)
    rest = value - high.astype(f32)
    middle = rest.astype(bf16)
    low = (rest - middle.astype(f32)).astype(bf16)
    return high, middle, low


PANELS = ((0, 48, 4), (192, 16, 4), (256, 16, 8), (384, 32, 4))


def pack_kernel(vec_width, me_ref, flat, vec, q_out, r_out, wide, line):
    wide[...] = flat[...].astype(f32)
    line[...] = jnp.zeros_like(line)
    line[0:1, 0:vec_width] = vec[...].astype(f32).reshape(1, vec_width)
    shifted = pltpu.roll(line[...], (me_ref[0] * vec_width) % 128, 1)
    parts = []
    for start, rows, count in PANELS:
        for j in range(count):
            parts.append(wide[pl.ds(start + j, rows, stride=count), :].astype(bf16))
    q_out[0:192, :] = jnp.concatenate(parts[:4], axis=0)
    placed = jnp.concatenate([shifted[0:1, 0:128], shifted[0:1, 128:256], jnp.zeros((14, 128), f32)], axis=0)
    q_out[192:208, :] = placed.astype(bf16)
    r_out[...] = jnp.concatenate(parts[4:], axis=0)


def pack(me, flat, vec, vec_width):
    vmem = pl.BlockSpec(memory_space=pltpu.VMEM)
    return pl.pallas_call(
        functools.partial(pack_kernel, vec_width),
        in_specs=[scalar_spec(), vmem, vmem],
        out_shape=[
            jax.ShapeDtypeStruct((Q_ROWS, 128), bf16),
            jax.ShapeDtypeStruct((R_ROWS, 128), bf16),
        ],
        scratch_shapes=[pltpu.VMEM((512, 128), f32), pltpu.VMEM((8, 256), f32)],
        compiler_params=params("pack"),
        name="pack",
    )(me, flat, vec)


def fetch_kernel(source, out, sem):
    copy = pltpu.make_async_copy(source, out, sem)
    copy.start()
    copy.wait()


def fetch(array):
    return pl.pallas_call(
        fetch_kernel,
        in_specs=[pl.BlockSpec(memory_space=pl.ANY)],
        out_specs=resident(),
        out_shape=jax.ShapeDtypeStruct(array.shape, array.dtype),
        scratch_shapes=[pltpu.SemaphoreType.DMA],
        compiler_params=params("fetch"),
        cost_estimate=cost(0, 2 * array.size * 2),
        name="fetch",
    )(array)


def project_kernel(rows, masks, order, vec_width, me_ref, ends, tokens, *refs):
    pieces = refs[: len(masks)]
    qkv, keys_extra, query_extra, vec_out, weight, vec = refs[len(masks) :]
    step = pl.program_id(0)
    me = me_ref[0]

    @pl.when(step == 0)
    def _():
        vec[...] = jnp.zeros_like(vec)
        for mask, ref in zip(masks, pieces):
            for i in range(1 << len(order)):
                d = owner_of(i, jnp.bitwise_xor(me, mask), order)
                row = pl.multiple_of(d * QKV_ROWS, 16)
                for j in range(4):
                    at = i * Q_ROWS + QKV_ROWS * j
                    weight[pl.ds(row, QKV_ROWS), 128 * j : 128 * (j + 1)] = ref[at : at + QKV_ROWS, :]
                row = (d * vec_width) // 128
                at = i * Q_ROWS + 4 * QKV_ROWS
                vec[pl.ds(row, 2), :] = vec[pl.ds(row, 2), :] + ref[at : at + 16, :].astype(f32)[0:2, :]
        vec_out[...] = vec[...]

    here = pl.ds(pl.multiple_of(step * rows, rows), rows)
    x = tokens[here, :]
    scale = 1.0 / math.sqrt(HEAD_DIM)
    query_bias = jnp.concatenate([vec[j : j + 1, :] for j in range(4)], axis=1)
    value_bias = jnp.concatenate([vec[4 + j : 5 + j, :] for j in range(4)], axis=1)
    queries = ((dot(x, weight[0:512, :], NN) + query_bias) * scale).astype(bf16)
    key_heads = dot(x, weight[512:1024, :], NN).astype(bf16)
    values = (dot(x, weight[1024:1536, :], NN) + value_bias).astype(bf16)
    qkv[here, 0:512] = queries
    qkv[here, 512:1024] = key_heads
    qkv[here, 1024:1536] = values
    places = step * rows + lax.broadcasted_iota(jnp.int32, (rows, ends.shape[1]), 0)
    label = jnp.sum((ends[...] <= places).astype(f32), axis=1, keepdims=True)
    lane = lax.broadcasted_iota(jnp.int32, (rows, 128), 1)
    same = lane.astype(f32) == label
    keys_extra[here, :] = jnp.where(lane < 8, jnp.where(same, 1.0, 0.0), jnp.where(lane < 32, 1.0, 0.0)).astype(bf16)
    apart = jnp.where((lane < 8) & jnp.logical_not(same), FAR, 0.0)
    product = queries.astype(f32) * key_heads.astype(f32)
    extra = apart
    for h in range(HEADS):
        own = jnp.sum(product[:, 128 * h : 128 * (h + 1)], axis=1, keepdims=True)
        extra = jnp.where(lane == 8 + h, -own, extra)
    query_extra[here, :] = extra.astype(bf16)


def project(me, ends, tokens, pieces, masks, order, vec_width, rows=1024):
    count = tokens.shape[0]
    sets = ends.shape[1]
    return pl.pallas_call(
        functools.partial(project_kernel, rows, masks, order, vec_width),
        grid=(count // rows,),
        in_specs=[
            scalar_spec(),
            whole((1, sets)),
            resident(),
        ]
        + [resident() for _ in pieces],
        out_specs=[resident() for _ in range(5)],
        out_shape=[
            jax.ShapeDtypeStruct((count, 1536), bf16),
            jax.ShapeDtypeStruct((count, 128), bf16),
            jax.ShapeDtypeStruct((count, 128), bf16),
            jax.ShapeDtypeStruct((48, 128), f32),
            jax.ShapeDtypeStruct((1536, 512), bf16),
        ],
        scratch_shapes=[pltpu.VMEM((48, 128), f32)],
        compiler_params=params("project"),
        cost_estimate=cost(2 * count * 512 * 1536, 12e6),
        name="project",
    )(me, ends, tokens, *pieces)


def own_lanes(lane, head):
    return (lane < 8) | (lane == 8 + head) | ((lane >= 16 + 4 * head) & (lane < 19 + 4 * head))


def attend_kernel(base, rows, qkv, query_extra, keys_extra, attended, offset_out, total, mixed, peak):
    local = pl.program_id(0)
    head = base + local
    start = pl.program_id(1) * rows
    here = pl.ds(pl.multiple_of(start, rows), rows)

    def columns(first):
        return pl.ds(pl.multiple_of(128 * (first + head), 128), 128)

    v = qkv[:, columns(2 * HEADS)]
    lane = lax.broadcasted_iota(jnp.int32, (rows, 128), 1)
    extra = jnp.where(own_lanes(lane, head), query_extra[here, :].astype(f32), 0.0).astype(bf16)
    left = jnp.concatenate([qkv[:, columns(HEADS)], keys_extra[...]], axis=1)
    right = jnp.concatenate([qkv[here, columns(0)], extra], axis=1)
    weights = jnp.exp(dot(left, right, NT))
    total[...] = jnp.sum(weights, axis=0, keepdims=True)
    mixed[...] = dot(v, weights.astype(bf16), TN)
    peak[...] = jnp.zeros_like(peak)
    good = (total[...] > 1e-20) & (total[...] < 1e30)

    @pl.when(jnp.sum(jnp.where(good, 0.0, 1.0)) > 0.0)
    def _():
        def part(j, _):
            place = pl.ds(pl.multiple_of(j * 128, 128), 128)
            some = pl.ds(pl.multiple_of(start + j * 128, 128), 128)
            lane = lax.broadcasted_iota(jnp.int32, (128, 128), 1)
            extra = jnp.where(own_lanes(lane, head), query_extra[some, :].astype(f32), 0.0).astype(bf16)
            again = dot(left, jnp.concatenate([qkv[some, columns(0)], extra], axis=1), NT)
            top = jnp.max(again, axis=0, keepdims=True)
            safe = jnp.exp(again - top)
            total[:, place] = jnp.sum(safe, axis=0, keepdims=True)
            mixed[:, place] = dot(v, safe.astype(bf16), TN)
            peak[:, place] = top
            return 0

        lax.fori_loop(0, rows // 128, part, 0)

    own = pl.ds(pl.multiple_of(128 * local, 128), 128)
    attended[here, own] = (mixed[...] * (1.0 / total[...])).T.astype(bf16)
    offset_out[local, :, here] = peak[...] + jnp.log(total[...])


def attend(qkv, query_extra, keys_extra, base, heads, rows=1024):
    count = qkv.shape[0]
    return pl.pallas_call(
        functools.partial(attend_kernel, base, rows),
        grid=(heads, count // rows),
        in_specs=[resident() for _ in range(3)],
        out_specs=[resident() for _ in range(2)],
        out_shape=[
            jax.ShapeDtypeStruct((count, 128 * heads), bf16),
            jax.ShapeDtypeStruct((heads, 1, count), f32),
        ],
        scratch_shapes=[pltpu.VMEM((1, rows), f32), pltpu.VMEM((128, rows), f32), pltpu.VMEM((1, rows), f32)],
        compiler_params=params("attend"),
        cost_estimate=cost(heads * 8 * count * count * 128, 6e6, heads * count * count),
        name="attend",
    )(qkv, query_extra, keys_extra)


def mean_row(value):
    return jnp.sum(value, axis=1, keepdims=True) * (1.0 / value.shape[1])


def norm_rows(summed):
    centered = summed - mean_row(summed)
    inverse = lax.rsqrt(mean_row(centered * centered) + NORM_EPS)
    return centered * inverse, inverse


def norm_back(grad, normed, inverse):
    return inverse * (grad - mean_row(grad) - normed * mean_row(grad * normed))


def fold8(value):
    return jnp.sum(value.reshape(value.shape[0] // 8, 8, value.shape[1]), axis=0)


def middle_kernel(
    masks,
    order_in,
    order_out,
    rows,
    sub,
    me_ref,
    tokens,
    attended_a,
    attended_b,
    offset_a,
    offset_b,
    query_extra,
    cotangent,
    vec,
    *refs,
):
    pieces = refs[: len(masks)]
    layer_output, grad_branch_out, grad_attended_out, grad_extra, query_extra_out, keep, send, vec_out = refs[
        len(masks) : -8
    ]
    attn_weight, in_weight, out_weight, grad_attn, grad_in, grad_out, sums, hidden_sum = refs[-8:]
    step = pl.program_id(0)
    me = me_ref[0]
    half = BLOCKS // 2

    @pl.when(step == 0)
    def _():
        for mask, ref in zip(masks, pieces):

            def place(i, _, mask=mask, ref=ref):
                d = owner_of(i, jnp.bitwise_xor(me, mask), order_in)
                start = i * R_ROWS
                a_row = pl.multiple_of(d * 16, 16)
                o_row = pl.multiple_of(d * 32, 16)
                for j in range(4):
                    attn_weight[pl.ds(a_row, 16), 128 * j : 128 * (j + 1)] = ref[
                        pl.ds(pl.multiple_of(start + 16 * j, 16), 16), :
                    ]
                for j in range(8):
                    in_weight[pl.ds(a_row, 16), 128 * j : 128 * (j + 1)] = ref[
                        pl.ds(pl.multiple_of(start + 64 + 16 * j, 16), 16), :
                    ]
                for j in range(4):
                    out_weight[pl.ds(o_row, 32), 128 * j : 128 * (j + 1)] = ref[
                        pl.ds(pl.multiple_of(start + 192 + 32 * j, 16), 32), :
                    ]
                return 0

            lax.fori_loop(0, 1 << len(order_in), place, 0, unroll=True)
        grad_attn[...] = jnp.zeros_like(grad_attn)
        grad_in[...] = jnp.zeros_like(grad_in)
        grad_out[...] = jnp.zeros_like(grad_out)
        sums[...] = jnp.zeros_like(sums)
        hidden_sum[...] = jnp.zeros_like(hidden_sum)

    def row_of(index):
        return jnp.concatenate([vec[4 * index + j : 4 * index + j + 1, :] for j in range(4)], axis=1)

    attn_bias, ffn_bias, gain_one, shift_one, gain_two, shift_two = [row_of(i) for i in range(2, 8)]
    hidden_bias = jnp.concatenate([vec[32 + j : 33 + j, :] for j in range(8)], axis=1)

    first_row = pl.multiple_of(step * rows, rows)
    here = pl.ds(first_row, rows)
    parts = [offset_a[h, :, here] for h in range(3)] + [offset_b[0, :, here], jnp.zeros((4, rows), f32)]
    offsets = jnp.concatenate(parts, axis=0).T
    lane = lax.broadcasted_iota(jnp.int32, (rows, 128), 1)
    extra = query_extra[here, :].astype(f32)
    for h in range(HEADS):
        for i, part in enumerate(split3(-offsets[:, h : h + 1])):
            extra = jnp.where(lane == 16 + 4 * h + i, part.astype(f32), extra)
    query_extra_out[here, :] = extra.astype(bf16)

    kept = [{} for _ in range(rows // sub)]

    def chain(s):
        out = slice(s * sub, (s + 1) * sub)
        sl = pl.ds(pl.multiple_of(step * rows + s * sub, sub), sub)
        att = jnp.concatenate([attended_a[sl, :], attended_b[sl, :]], axis=1)
        branch = dot(att, attn_weight[...], NN) + attn_bias
        yield
        normed_one, inverse_one = norm_rows(tokens[sl, :].astype(f32) + branch)
        hidden = normed_one * gain_one + shift_one
        hidden_low = hidden.astype(bf16)
        yield
        pre_act = dot(hidden_low, in_weight[...], NN) + hidden_bias
        yield
        cdf = 0.5 * (1.0 + lax.erf(pre_act * 0.7071067811865476))
        density = jnp.exp(-0.5 * pre_act * pre_act) * 0.3989422804014327
        activated = (pre_act * cdf).astype(bf16)
        slope = cdf + pre_act * density
        yield
        ffn_result = dot(activated, out_weight[...], NN) + ffn_bias
        yield
        normed_two, inverse_two = norm_rows(hidden + ffn_result)
        layer_output[out, :] = (normed_two * gain_two + shift_two).astype(bf16)
        grad_result = cotangent[sl, :].astype(f32)
        sums[4] += fold8(grad_result * normed_two)
        sums[5] += fold8(grad_result)
        grad_second = norm_back(grad_result * gain_two, normed_two, inverse_two)
        grad_ffn = grad_second.astype(bf16)
        sums[1] += fold8(grad_ffn.astype(f32))
        yield
        grad_activated = dot(grad_ffn, out_weight[...], NT)
        kept[s][0] = (activated, grad_ffn)
        yield
        grad_pre = (grad_activated * slope).astype(bf16)
        hidden_sum[...] += fold8(grad_pre.astype(f32))
        yield
        grad_hidden = grad_second + dot(grad_pre, in_weight[...], NT)
        kept[s][1] = (hidden_low, grad_pre)
        yield
        sums[2] += fold8(grad_hidden * normed_one)
        sums[3] += fold8(grad_hidden)
        grad_first = norm_back(grad_hidden * gain_one, normed_one, inverse_one)
        grad_branch = grad_first.astype(bf16)
        grad_branch_out[sl, :] = grad_branch
        sums[0] += fold8(grad_branch.astype(f32))
        yield
        grad_attended = dot(grad_branch, attn_weight[...], NT)
        kept[s][2] = (att, grad_branch)
        yield
        low = grad_attended.astype(bf16)
        grad_attended_out[sl, :] = low
        lane = lax.broadcasted_iota(jnp.int32, (sub, 128), 1)
        extra = jnp.zeros((sub, 128), f32)
        for h in range(HEADS):
            cols = slice(128 * h, 128 * (h + 1))
            low_cols = low[:, cols].astype(f32)
            centre = jnp.sum(low_cols * att[:, cols].astype(f32), axis=1, keepdims=True)
            for i, part in enumerate(split3(-centre)):
                extra = jnp.where(lane == 4 * h + i, part.astype(f32), extra)
        grad_extra[sl, :] = extra.astype(bf16)
        yield

    chains = [chain(s) for s in range(rows // sub)]
    started = 0
    live = []
    while started < len(chains) or live:
        if started < len(chains):
            live.append(chains[started])
            started += 1
        remaining = []
        for c in live:
            try:
                next(c)
                remaining.append(c)
            except StopIteration:
                pass
        live = remaining
        for i, ref in enumerate((grad_out, grad_in, grad_attn)):
            if all(i in k for k in kept):
                left = jnp.concatenate([k[i][0] for k in kept], axis=0)
                right = jnp.concatenate([k.pop(i)[1] for k in kept], axis=0)
                ref[...] += dot(left, right, TN)

    @pl.when(step == pl.num_programs(0) - 1)
    def _():
        for base, ref in ((0, keep), (half, send)):

            def place(i, _, base=base, ref=ref):
                d = owner_of(base + i, me, order_out)
                start = i * R_ROWS
                a_row = pl.multiple_of(d * 16, 16)
                o_row = pl.multiple_of(d * 32, 16)
                for j in range(4):
                    ref[pl.ds(pl.multiple_of(start + 16 * j, 16), 16), :] = grad_attn[
                        pl.ds(a_row, 16), 128 * j : 128 * (j + 1)
                    ].astype(bf16)
                for j in range(8):
                    ref[pl.ds(pl.multiple_of(start + 64 + 16 * j, 16), 16), :] = grad_in[
                        pl.ds(a_row, 16), 128 * j : 128 * (j + 1)
                    ].astype(bf16)
                for j in range(4):
                    ref[pl.ds(pl.multiple_of(start + 192 + 32 * j, 16), 32), :] = grad_out[
                        pl.ds(o_row, 32), 128 * j : 128 * (j + 1)
                    ].astype(bf16)
                return 0

            lax.fori_loop(0, half, place, 0, unroll=True)
        vec_out[...] = jnp.zeros_like(vec_out)
        for i in range(6):
            row = jnp.sum(sums[i], axis=0, keepdims=True)
            for j in range(4):
                vec_out[8 + 4 * i + j : 9 + 4 * i + j, :] = row[:, 128 * j : 128 * (j + 1)]
        row = jnp.sum(hidden_sum[...], axis=0, keepdims=True)
        for j in range(8):
            vec_out[32 + j : 33 + j, :] = row[:, 128 * j : 128 * (j + 1)]


def middle(me, tokens, attended, offset, query_extra, cotangent, vec, pieces, masks, order_in, order_out, rows=512, sub=256):
    count = tokens.shape[0]
    half_rows = BLOCKS // 2 * R_ROWS
    return pl.pallas_call(
        functools.partial(middle_kernel, masks, order_in, order_out, rows, sub),
        grid=(count // rows,),
        in_specs=[scalar_spec()] + [resident() for _ in range(8 + len(pieces))],
        out_specs=[pl.BlockSpec((rows, 512), lambda i: (i, 0))] + [resident() for _ in range(7)],
        out_shape=[
            jax.ShapeDtypeStruct((count, 512), bf16),
            jax.ShapeDtypeStruct((count, 512), bf16),
            jax.ShapeDtypeStruct((count, 512), bf16),
            jax.ShapeDtypeStruct((count, 128), bf16),
            jax.ShapeDtypeStruct((count, 128), bf16),
            jax.ShapeDtypeStruct((half_rows, 128), bf16),
            jax.ShapeDtypeStruct((half_rows, 128), bf16),
            jax.ShapeDtypeStruct((48, 128), f32),
        ],
        scratch_shapes=[
            pltpu.VMEM((512, 512), bf16),
            pltpu.VMEM((512, FF), bf16),
            pltpu.VMEM((FF, 512), bf16),
            pltpu.VMEM((512, 512), f32),
            pltpu.VMEM((512, FF), f32),
            pltpu.VMEM((FF, 512), f32),
            pltpu.VMEM((6, 8, 512), f32),
            pltpu.VMEM((8, FF), f32),
        ],
        compiler_params=params("middle"),
        cost_estimate=cost(6 * count * 1310720, 22e6, 3 * count * FF),
        name="middle",
    )(me, tokens, *attended, *offset, query_extra, cotangent, vec, *pieces)


def attend_back_kernel(
    base,
    heads,
    width,
    order,
    vec_width,
    me_ref,
    tokens,
    qkv,
    grad_all,
    query_extra,
    keys_extra,
    grad_extra,
    vec_in,
    grad_query,
    grad_keys,
    grad_values,
    keep,
    send,
    vec,
    acc,
    all_keys,
    all_values,
    grad_weight,
):
    local = pl.program_id(0)
    step = pl.program_id(1)
    steps = pl.num_programs(1)
    last = base + heads == HEADS

    @pl.when((local == 0) & (step == 0))
    def _():
        vec[...] = vec_in[...]

    head = base + local
    keys = pl.ds(pl.multiple_of(step * width, width), width)

    def columns(first):
        return pl.ds(pl.multiple_of(128 * (first + head), 128), 128)

    q = qkv[:, columns(0)]
    k = qkv[keys, columns(HEADS)]
    v = qkv[keys, columns(2 * HEADS)]
    grad = grad_all[:, columns(0)]
    lane = lax.broadcasted_iota(jnp.int32, (width, 128), 1)
    ones = jnp.where((lane >= 4 * head) & (lane < 4 * head + 3), 1.0, 0.0).astype(bf16)
    extra = jnp.where(own_lanes(lane, head), keys_extra[keys, :].astype(f32), 0.0).astype(bf16)
    scores = dot(jnp.concatenate([q, query_extra[...]], axis=1), jnp.concatenate([k, extra], axis=1), NT)
    centred = dot(jnp.concatenate([grad, grad_extra[...]], axis=1), jnp.concatenate([v, ones], axis=1), NT)
    probs = jnp.exp(scores)
    probs_low = probs.astype(bf16)
    grad_scores = (probs * centred).astype(bf16)
    gv = dot(grad, probs_low, TN).astype(bf16)
    gk = dot(q, grad_scores, TN).astype(bf16)
    own_rows = pl.ds(pl.multiple_of(local * 128, 128), 128)
    grad_values[own_rows, keys] = gv
    grad_keys[own_rows, keys] = gk
    all_values[step] = gv
    all_keys[step] = gk
    part = dot(grad_scores, k, NN)

    @pl.when(step == 0)
    def _():
        acc[...] = part

    @pl.when(step > 0)
    def _():
        acc[...] += part

    @pl.when(step == steps - 1)
    def _():
        me = me_ref[0]
        scale = 1.0 / math.sqrt(HEAD_DIM)
        x = tokens[...]
        gq_all = acc[...].astype(bf16)
        grad_query[:, pl.ds(pl.multiple_of(local * 128, 128), 128)] = gq_all
        gk_all = jnp.concatenate([all_keys[i] for i in range(all_keys.shape[0])], axis=1)
        gv_all = jnp.concatenate([all_values[i] for i in range(all_values.shape[0])], axis=1)
        sums = dot(jnp.concatenate([gq_all.T, gk_all, gv_all], axis=0), x, NN)
        grad_weight[0:512, :] = (sums[0:128].T * scale).astype(bf16)
        grad_weight[512:1024, :] = sums[128:256].T.astype(bf16)
        grad_weight[1024:1536, :] = sums[256:384].T.astype(bf16)
        row_ones = jnp.ones((8, x.shape[0]), bf16)
        vec[pl.ds(base + local, 1), :] = dot(row_ones, gq_all, NN)[0:1] * scale
        vec[pl.ds(4 + base + local, 1), :] = dot(row_ones, gv_all, NT)[0:1]
        half = BLOCKS // 2
        block = heads * QKV_ROWS + (16 if last else 0)
        for start, ref in ((0, keep), (half, send)):

            def place(i, _, start=start, ref=ref):
                d = owner_of(start + i, me, order)
                ref[pl.ds(pl.multiple_of(i * block + local * QKV_ROWS, 16), QKV_ROWS), :] = grad_weight[
                    pl.ds(pl.multiple_of(d * QKV_ROWS, 16), QKV_ROWS), :
                ]
                if last:
                    pair = vec[pl.ds((d * vec_width) // 128, 2), :]
                    pair = jnp.concatenate([pair, jnp.zeros((14, 128), f32)], axis=0)
                    ref[pl.ds(pl.multiple_of(i * block + heads * QKV_ROWS, 16), 16), :] = pair.astype(bf16)
                return 0

            lax.fori_loop(0, half, place, 0, unroll=True)


def attend_back(
    me, tokens, qkv, grad_attended, query_extra, keys_extra, grad_extra, vec, order, vec_width, base, heads, width=512
):
    count = qkv.shape[0]
    half_rows = BLOCKS // 2 * (heads * QKV_ROWS + (16 if base + heads == HEADS else 0))
    return pl.pallas_call(
        functools.partial(attend_back_kernel, base, heads, width, order, vec_width),
        grid=(heads, count // width),
        in_specs=[scalar_spec()] + [resident() for _ in range(7)],
        out_specs=[resident() for _ in range(6)],
        out_shape=[
            jax.ShapeDtypeStruct((count, 128 * heads), bf16),
            jax.ShapeDtypeStruct((128 * heads, count), bf16),
            jax.ShapeDtypeStruct((128 * heads, count), bf16),
            jax.ShapeDtypeStruct((half_rows, 128), bf16),
            jax.ShapeDtypeStruct((half_rows, 128), bf16),
            jax.ShapeDtypeStruct((48, 128), f32),
        ],
        scratch_shapes=[
            pltpu.VMEM((count, 128), f32),
            pltpu.VMEM((count // width, 128, width), bf16),
            pltpu.VMEM((count // width, 128, width), bf16),
            pltpu.VMEM((1536, 128), bf16),
        ],
        compiler_params=params("attend_back"),
        cost_estimate=cost(heads * 20 * count * count * 128, heads * 12e6, heads * count * count),
        name="attend_back",
    )(me, tokens, qkv, grad_attended, query_extra, keys_extra, grad_extra, vec)


def input_grad_kernel(groups, rows, *refs):
    grad_branch = refs[0]
    queries, keys, values = [refs[1 + i * groups : 1 + (i + 1) * groups] for i in range(3)]
    weight, out = refs[-2], refs[-1]
    scale = 1.0 / math.sqrt(HEAD_DIM)
    here = pl.ds(pl.multiple_of(pl.program_id(0) * rows, rows), rows)
    gq = jnp.concatenate([r[here, :] for r in queries], axis=1)
    gk = jnp.concatenate([r[:, here] for r in keys], axis=0)
    gv = jnp.concatenate([r[:, here] for r in values], axis=0)
    total = grad_branch[here, :].astype(f32) + scale * dot(gq, weight[0:512, :], NT)
    total = total + dot(gk, weight[512:1024, :], TT)
    out[...] = total + dot(gv, weight[1024:1536, :], TT)


def input_grad(grad_branch, queries, keys, values, weight, rows=1024):
    count = grad_branch.shape[0]
    by_row = pl.BlockSpec((rows, 512), lambda i: (i, 0))
    return pl.pallas_call(
        functools.partial(input_grad_kernel, len(queries), rows),
        grid=(count // rows,),
        in_specs=[resident() for _ in range(2 + 3 * len(queries))],
        out_specs=by_row,
        out_shape=jax.ShapeDtypeStruct((count, 512), f32),
        compiler_params=params("input_grad"),
        cost_estimate=cost(2 * count * 512 * 1536, 16e6),
        name="input_grad",
    )(grad_branch, *queries, *keys, *values, weight)


def unpack_kernel(vec_width, me_ref, *refs):
    q_parts, r_parts = refs[:4], refs[4:6]
    out, vec_out, line = refs[6:]
    q_sum, r_sum = q_parts[0][...], r_parts[0][...]
    for part in q_parts[1:]:
        q_sum = q_sum + part[...].astype(f32)
    for part in r_parts[1:]:
        r_sum = r_sum + part[...].astype(f32)
    at = 0
    source = q_sum
    for index, (start, rows, count) in enumerate(PANELS):
        if index == 1:
            source, at = r_sum, 0
        for j in range(count):
            out[pl.ds(start + j, rows, stride=count), :] = source[at : at + rows, :]
            at += rows
    pair = jnp.concatenate([q_sum[192:200, :], q_sum[193:201, :]], axis=1)
    line[...] = pltpu.roll(pair, 256 - (me_ref[0] * vec_width) % 128, 1)
    vec_out[...] = line[0:1, 0:vec_width]


def unpack(me, q_parts, r_parts, vec_width):
    vmem = pl.BlockSpec(memory_space=pltpu.VMEM)
    return pl.pallas_call(
        functools.partial(unpack_kernel, vec_width),
        in_specs=[scalar_spec()] + [vmem] * 6,
        out_shape=[jax.ShapeDtypeStruct((512, 128), f32), jax.ShapeDtypeStruct((1, vec_width), f32)],
        scratch_shapes=[pltpu.VMEM((8, 256), f32)],
        compiler_params=params("unpack"),
        name="unpack",
    )(me, *q_parts, *r_parts)


def swap(array, step, count):
    return lax.ppermute(array, AXES, [(i, i ^ step) for i in range(count)])


def swap_each(parts, steps, count):
    pairs = list(zip(parts, steps))
    return [swap(part, step, count) for part, step in pairs[::-1]][::-1]


def after(value, *others):
    return lax.optimization_barrier((value, *others))[0]


def quarters(groups):
    parts = []
    for keep, got in groups:
        keep, got = keep.reshape(4, 4, -1, 128), got.reshape(4, 4, -1, 128)
        parts.append([keep[i].astype(f32) + got[i].astype(f32) for i in range(4)])
    totals = [jnp.concatenate(same, axis=1) if len(same) > 1 else same[0] for same in zip(*parts)]
    return totals[0], [total.astype(bf16).reshape(-1, 128) for total in totals[1:]]


def halves(keep, gots):
    total = keep
    for got in gots:
        total = total + got.astype(f32).reshape(keep.shape)
    half = total.shape[0] // 2
    return total[:half], total[half:].astype(bf16).reshape(-1, 128)


def fourths(keep, gots):
    total = keep
    for got in gots:
        total = total + got.astype(f32).reshape(keep.shape)
    return [total[0]] + [total[i].astype(bf16) for i in range(1, 4)]


def fast_layout(dp, fsdp):
    return dp == 4 and fsdp == 8


def gather_line(block, steps, count):
    return jnp.concatenate([block] + [swap(block, step, count) for step in steps], axis=0)


def body(dp, fsdp, tokens, lengths, assignment, weights, vectors, cotangent):
    count = dp * fsdp
    fast = fast_layout(dp, fsdp)
    owner = lax.axis_index(AXES).astype(jnp.int32)
    owned = assignment == owner
    ends = jnp.cumsum(jnp.where(owned, lengths, 0), dtype=jnp.int32)
    ends = jnp.where(owned, ends, 1 << 30)[None, :]
    if fast:
        vec_width = vectors.shape[0]
        core, x_step, y_step, z_near, z_far = fsdp, 1, 2 * fsdp, 2, 4
        planes = [x_step, y_step, x_step + y_step]
        spread = [x_step + y_step, y_step, x_step]
        line = [z_near, z_far, z_near + z_far]
        order_in, order_rest = [z_near, z_far], [z_far, z_near]
        order_out = [z_near, z_far, x_step, y_step, core]
        order_rest_out = order_rest + order_out[2:]
        masks = [0] + spread
        masks = masks + [m + core for m in masks]
        me = owner[None]
        q_block, r_block = pack(me, pltpu.with_memory_space_constraint(weights.reshape(512, 128), pltpu.HBM), pltpu.with_memory_space_constraint(vectors, pltpu.HBM), vec_width)
        lines = [swap(q_block, step, count) for step in line[::-1]][::-1]
        q_far = jnp.concatenate([q_block, lines[0], lines[1], after(lines[2], ends)], axis=0)
        q_core = swap(q_far, core, count)
        q_pieces = [q_far] + [swap(q_far, step, count) for step in spread]
        r_far = gather_line(after(r_block, q_core), [z_far], count)
        r_far = gather_line(r_far, [z_near], count)
        tokens = fetch(after(pltpu.with_memory_space_constraint(tokens, pltpu.HBM), q_far))
        q_pieces[3] = after(q_pieces[3], tokens)
        q_pieces = q_pieces + [q_core] + [swap(piece, core, count) for piece in q_pieces[1:]]
        r_pieces = [swap(after(r_far, *q_pieces), step, count) for step in spread]
    else:
        vec_width = 160
        order_in, order_rest, order_out = [1, 2], [1, 2], [1, 2, 4, 8, 16]
        order_rest_out = order_out
        masks = [4 * i for i in range(8)]
        me = jnp.zeros((1,), jnp.int32)
        blocks = lax.all_gather(weights, AXES, axis=0, tiled=True).reshape(count, -1)
        flat = lax.all_gather(vectors, AXES, axis=0, tiled=True).reshape(40, 128)
        square = 512 * 512 // count
        cuts = [0, 3 * square, 4 * square, 6 * square, 8 * square]
        panels = []
        for index, (start, rows, width) in enumerate(PANELS):
            piece = blocks[:, cuts[index] : cuts[index + 1]].reshape(BLOCKS, rows, width, 128)
            panels.append(piece.transpose(0, 2, 1, 3).reshape(BLOCKS, rows * width, 128))
        spots = [(d * vec_width) // 128 for d in range(BLOCKS)]
        lanes = jnp.arange(256)
        vec_blocks = []
        for d in range(BLOCKS):
            pair = jnp.concatenate([flat, jnp.zeros((8, 128), bf16)], axis=0)[spots[d] : spots[d] + 2].reshape(256)
            offset = d * vec_width - 128 * spots[d]
            pair = jnp.where((lanes >= offset) & (lanes < offset + vec_width), pair, 0)
            vec_blocks.append(jnp.concatenate([pair.reshape(2, 128), jnp.zeros((14, 128), bf16)], axis=0))
        q_all = jnp.concatenate([panels[0], jnp.stack(vec_blocks)], axis=1)
        r_all = jnp.concatenate(panels[1:], axis=1)
        q_pieces = [q_all[4 * i : 4 * i + 4].reshape(-1, 128) for i in range(8)]
        r_pieces = [r_all[4 * i : 4 * i + 4].reshape(-1, 128) for i in range(8)]
    qkv, keys_extra, query_extra, vec, weight = project(
        me, ends, tokens, q_pieces, masks, order_in, vec_width
    )
    attended_a, offset_a = attend(qkv, query_extra, keys_extra, 0, 3)
    if fast:
        r_pieces = [r_far] + [after(piece, attended_a) for piece in r_pieces]
        keys_extra = after(keys_extra, *r_pieces)
        r_pieces = r_pieces + [swap(piece, core, count) for piece in r_pieces]
    attended_b, offset_b = attend(qkv, query_extra, keys_extra, 3, 1)
    layer_output, grad_branch, grad_attended, grad_extra, query_extra, r_keep, r_send, vec_grad = middle(
        me, tokens, (attended_a, attended_b), (offset_a, offset_b), query_extra, cotangent, vec, r_pieces, masks, order_rest, order_rest_out
    )
    queries, keys, values, keeps, sends, gots = [], [], [], [], [], []
    if fast:
        r_got = swap(r_send, core, count)
    for base, heads in ((0, 1), (1, 2), (3, 1)):
        gq, gk, gv, keep, send, vec_grad = attend_back(
            me,
            tokens,
            qkv,
            grad_attended,
            query_extra,
            keys_extra,
            grad_extra,
            vec_grad,
            order_out,
            vec_width,
            base,
            heads,
        )
        queries.append(gq)
        keys.append(gk)
        values.append(gv)
        keeps.append(keep)
        sends.append(send)
        if not fast:
            continue
        gots.append(swap(send, core, count))
        if base == 0:
            r_keep, r_sends = quarters([(r_keep, after(r_got, gq))])
            vec_grad = after(vec_grad, *r_sends)
            r_gots = swap_each(r_sends, planes, count)
        elif base == 1:
            r_gots = [after(part, gq) for part in r_gots]
            r_keep, r_send = halves(r_keep, r_gots)
            vec_grad = after(vec_grad, r_send)
            r_got = swap(r_send, z_near, count)
    if fast:
        r_keep, r_send = halves(r_keep, [after(r_got, gq)])
        gots = [after(got, gq) for got in gots]
        q_keep, q_sends = quarters(list(zip(keeps, gots)))
        grad_branch = after(grad_branch, *q_sends)
        q_gots = swap_each(q_sends, planes, count)
    grad_tokens = input_grad(grad_branch, queries, keys, values, weight)
    if fast:
        r_parts = [r_keep.reshape(-1, 128), swap(after(r_send, grad_tokens), z_far, count)]
        q_gots = [after(part, grad_tokens) for part in q_gots]
        q_parts = fourths(q_keep, q_gots)
        q_parts = q_parts[:1] + swap_each(q_parts[1:], line, count)
        own_weights, own_vectors = unpack(me, q_parts, r_parts, vec_width)
        own_weights = own_weights.reshape(-1)
        own_vectors = own_vectors.reshape(-1)
    else:
        heads = [jnp.concatenate([k, g], axis=0).astype(f32).reshape(BLOCKS, -1, 128) for k, g in zip(keeps, sends)]
        q_all = jnp.concatenate(heads, axis=1)
        r_all = jnp.concatenate([r_keep, r_send], axis=0).astype(f32).reshape(BLOCKS, R_ROWS, 128)
        sources = (q_all[:, : 4 * QKV_ROWS], r_all[:, :64], r_all[:, 64:192], r_all[:, 192:])
        pieces = []
        for source, (start, rows, width) in zip(sources, PANELS):
            piece = source.reshape(BLOCKS, width, rows, 128).transpose(0, 2, 1, 3)
            pieces.append(piece.reshape(count, -1))
        own_weights = lax.psum_scatter(
            jnp.concatenate(pieces, axis=1).reshape(-1), AXES, scatter_dimension=0, tiled=True
        )
        pairs = q_all[:, 4 * QKV_ROWS : 4 * QKV_ROWS + 2].reshape(BLOCKS, 256)
        rows = [
            pairs[d, (d * vec_width) % 128 : (d * vec_width) % 128 + vec_width] for d in range(BLOCKS)
        ]
        own_vectors = lax.psum_scatter(jnp.concatenate(rows), AXES, scatter_dimension=0, tiled=True)
    return (layer_output, grad_tokens, own_weights, own_vectors)


def solution(mesh):
    dp, fsdp = mesh.shape["dp"], mesh.shape["fsdp"]
    in_specs = (
        P(AXES, None),
        P(),
        P(),
        P(AXES),
        P(AXES),
        P(AXES, None),
    )
    out_specs = (
        P(AXES, None),
        P(AXES, None),
        P(AXES),
        P(AXES),
    )
    return jax.shard_map(
        functools.partial(body, dp, fsdp), mesh=mesh, in_specs=in_specs, out_specs=out_specs, check_vma=False
    )
```

```python
import functools
import math

import jax
import jax.numpy as jnp
from jax import lax
from jax.experimental import pallas as pl
from jax.experimental.pallas import tpu as pltpu
from jax.sharding import PartitionSpec as P

HEADS = 4
HEAD_DIM = 128
FF = 1024
AXES = ("dp", "fsdp")
NORM_EPS = 1e-05
BLOCKS = 32
QKV_ROWS = 48
Q_ROWS = 4 * QKV_ROWS + 16
R_ROWS = 320
FAR = -1e30
f32 = jnp.float32
bf16 = jnp.bfloat16
NT = (((1,), (1,)), ((), ()))
NN = (((1,), (0,)), ((), ()))
TN = (((0,), (0,)), ((), ()))
TT = (((0,), (1,)), ((), ()))
VMEM_MIB = {"pack": 2, "fetch": 4, "project": 22, "attend": 30, "middle": 26, "attend_back": 28, "input_grad": 14, "unpack": 3}


def dot(a, b, dims):
    return lax.dot_general(a, b, dims, preferred_element_type=f32)


def params(name):
    return pltpu.CompilerParams(vmem_limit_bytes=VMEM_MIB[name] << 20)


def cost(flops, moved, special=0):
    return pl.CostEstimate(flops=int(flops), bytes_accessed=int(moved), transcendentals=int(special))


def whole(shape):
    return pl.BlockSpec(shape, lambda *_: (0,) * len(shape))


def resident():
    return pl.BlockSpec(memory_space=pltpu.VMEM)


def scalar_spec():
    return pl.BlockSpec(memory_space=pltpu.SMEM)


def owner_of(place, me, order):
    mask = 0
    for bit, step in enumerate(order):
        mask = mask + ((place >> bit) & 1) * step
    return jnp.bitwise_xor(me, mask)


def split3(value):
    high = value.astype(bf16)
    rest = value - high.astype(f32)
    middle = rest.astype(bf16)
    low = (rest - middle.astype(f32)).astype(bf16)
    return high, middle, low


PANELS = ((0, 48, 4), (192, 16, 4), (256, 16, 8), (384, 32, 4))


def pack_kernel(vec_width, me_ref, flat, vec, q_out, r_out, wide, line):
    wide[...] = flat[...].astype(f32)
    line[...] = jnp.zeros_like(line)
    line[0:1, 0:vec_width] = vec[...].astype(f32).reshape(1, vec_width)
    shifted = pltpu.roll(line[...], (me_ref[0] * vec_width) % 128, 1)
    parts = []
    for start, rows, count in PANELS:
        for j in range(count):
            parts.append(wide[pl.ds(start + j, rows, stride=count), :].astype(bf16))
    q_out[0:192, :] = jnp.concatenate(parts[:4], axis=0)
    placed = jnp.concatenate([shifted[0:1, 0:128], shifted[0:1, 128:256], jnp.zeros((14, 128), f32)], axis=0)
    q_out[192:208, :] = placed.astype(bf16)
    r_out[...] = jnp.concatenate(parts[4:], axis=0)


def pack(me, flat, vec, vec_width):
    vmem = pl.BlockSpec(memory_space=pltpu.VMEM)
    return pl.pallas_call(
        functools.partial(pack_kernel, vec_width),
        in_specs=[scalar_spec(), vmem, vmem],
        out_shape=[
            jax.ShapeDtypeStruct((Q_ROWS, 128), bf16),
            jax.ShapeDtypeStruct((R_ROWS, 128), bf16),
        ],
        scratch_shapes=[pltpu.VMEM((512, 128), f32), pltpu.VMEM((8, 256), f32)],
        compiler_params=params("pack"),
        name="pack",
    )(me, flat, vec)


def fetch_kernel(source, out, sem):
    copy = pltpu.make_async_copy(source, out, sem)
    copy.start()
    copy.wait()


def fetch(array):
    return pl.pallas_call(
        fetch_kernel,
        in_specs=[pl.BlockSpec(memory_space=pl.ANY)],
        out_specs=resident(),
        out_shape=jax.ShapeDtypeStruct(array.shape, array.dtype),
        scratch_shapes=[pltpu.SemaphoreType.DMA],
        compiler_params=params("fetch"),
        cost_estimate=cost(0, 2 * array.size * 2),
        name="fetch",
    )(array)


def project_kernel(rows, masks, order, vec_width, me_ref, ends, tokens, *refs):
    pieces = refs[: len(masks)]
    qkv, keys_extra, query_extra, vec_out, weight, vec = refs[len(masks) :]
    step = pl.program_id(0)
    me = me_ref[0]

    @pl.when(step == 0)
    def _():
        vec[...] = jnp.zeros_like(vec)
        for mask, ref in zip(masks, pieces):
            for i in range(1 << len(order)):
                d = owner_of(i, jnp.bitwise_xor(me, mask), order)
                row = pl.multiple_of(d * QKV_ROWS, 16)
                for j in range(4):
                    at = i * Q_ROWS + QKV_ROWS * j
                    weight[pl.ds(row, QKV_ROWS), 128 * j : 128 * (j + 1)] = ref[at : at + QKV_ROWS, :]
                row = (d * vec_width) // 128
                at = i * Q_ROWS + 4 * QKV_ROWS
                vec[pl.ds(row, 2), :] = vec[pl.ds(row, 2), :] + ref[at : at + 16, :].astype(f32)[0:2, :]
        vec_out[...] = vec[...]

    here = pl.ds(pl.multiple_of(step * rows, rows), rows)
    x = tokens[here, :]
    scale = 1.0 / math.sqrt(HEAD_DIM)
    query_bias = jnp.concatenate([vec[j : j + 1, :] for j in range(4)], axis=1)
    value_bias = jnp.concatenate([vec[4 + j : 5 + j, :] for j in range(4)], axis=1)
    queries = ((dot(x, weight[0:512, :], NN) + query_bias) * scale).astype(bf16)
    key_heads = dot(x, weight[512:1024, :], NN).astype(bf16)
    values = (dot(x, weight[1024:1536, :], NN) + value_bias).astype(bf16)
    qkv[here, 0:512] = queries
    qkv[here, 512:1024] = key_heads
    qkv[here, 1024:1536] = values
    places = step * rows + lax.broadcasted_iota(jnp.int32, (rows, ends.shape[1]), 0)
    label = jnp.sum((ends[...] <= places).astype(f32), axis=1, keepdims=True)
    lane = lax.broadcasted_iota(jnp.int32, (rows, 128), 1)
    same = lane.astype(f32) == label
    keys_extra[here, :] = jnp.where(lane < 8, jnp.where(same, 1.0, 0.0), jnp.where(lane < 32, 1.0, 0.0)).astype(bf16)
    apart = jnp.where((lane < 8) & jnp.logical_not(same), FAR, 0.0)
    product = queries.astype(f32) * key_heads.astype(f32)
    extra = apart
    for h in range(HEADS):
        own = jnp.sum(product[:, 128 * h : 128 * (h + 1)], axis=1, keepdims=True)
        extra = jnp.where(lane == 8 + h, -own, extra)
    query_extra[here, :] = extra.astype(bf16)


def project(me, ends, tokens, pieces, masks, order, vec_width, rows=1024):
    count = tokens.shape[0]
    sets = ends.shape[1]
    return pl.pallas_call(
        functools.partial(project_kernel, rows, masks, order, vec_width),
        grid=(count // rows,),
        in_specs=[
            scalar_spec(),
            whole((1, sets)),
            resident(),
        ]
        + [resident() for _ in pieces],
        out_specs=[resident() for _ in range(5)],
        out_shape=[
            jax.ShapeDtypeStruct((count, 1536), bf16),
            jax.ShapeDtypeStruct((count, 128), bf16),
            jax.ShapeDtypeStruct((count, 128), bf16),
            jax.ShapeDtypeStruct((48, 128), f32),
            jax.ShapeDtypeStruct((1536, 512), bf16),
        ],
        scratch_shapes=[pltpu.VMEM((48, 128), f32)],
        compiler_params=params("project"),
        cost_estimate=cost(2 * count * 512 * 1536, 12e6),
        name="project",
    )(me, ends, tokens, *pieces)


def own_lanes(lane, head):
    return (lane < 8) | (lane == 8 + head) | ((lane >= 16 + 4 * head) & (lane < 19 + 4 * head))


def attend_kernel(base, rows, qkv, query_extra, keys_extra, attended, offset_out, total, mixed, peak):
    local = pl.program_id(0)
    head = base + local
    start = pl.program_id(1) * rows
    here = pl.ds(pl.multiple_of(start, rows), rows)

    def columns(first):
        return pl.ds(pl.multiple_of(128 * (first + head), 128), 128)

    v = qkv[:, columns(2 * HEADS)]
    lane = lax.broadcasted_iota(jnp.int32, (rows, 128), 1)
    extra = jnp.where(own_lanes(lane, head), query_extra[here, :].astype(f32), 0.0).astype(bf16)
    left = jnp.concatenate([qkv[:, columns(HEADS)], keys_extra[...]], axis=1)
    right = jnp.concatenate([qkv[here, columns(0)], extra], axis=1)
    weights = jnp.exp(dot(left, right, NT))
    total[...] = jnp.sum(weights, axis=0, keepdims=True)
    mixed[...] = dot(v, weights.astype(bf16), TN)
    peak[...] = jnp.zeros_like(peak)
    good = (total[...] > 1e-20) & (total[...] < 1e30)

    @pl.when(jnp.sum(jnp.where(good, 0.0, 1.0)) > 0.0)
    def _():
        def part(j, _):
            place = pl.ds(pl.multiple_of(j * 128, 128), 128)
            some = pl.ds(pl.multiple_of(start + j * 128, 128), 128)
            lane = lax.broadcasted_iota(jnp.int32, (128, 128), 1)
            extra = jnp.where(own_lanes(lane, head), query_extra[some, :].astype(f32), 0.0).astype(bf16)
            again = dot(left, jnp.concatenate([qkv[some, columns(0)], extra], axis=1), NT)
            top = jnp.max(again, axis=0, keepdims=True)
            safe = jnp.exp(again - top)
            total[:, place] = jnp.sum(safe, axis=0, keepdims=True)
            mixed[:, place] = dot(v, safe.astype(bf16), TN)
            peak[:, place] = top
            return 0

        lax.fori_loop(0, rows // 128, part, 0)

    own = pl.ds(pl.multiple_of(128 * local, 128), 128)
    attended[here, own] = (mixed[...] * (1.0 / total[...])).T.astype(bf16)
    offset_out[local, :, here] = peak[...] + jnp.log(total[...])


def attend(qkv, query_extra, keys_extra, base, heads, rows=2048):
    count = qkv.shape[0]
    return pl.pallas_call(
        functools.partial(attend_kernel, base, rows),
        grid=(heads, count // rows),
        in_specs=[resident() for _ in range(3)],
        out_specs=[resident() for _ in range(2)],
        out_shape=[
            jax.ShapeDtypeStruct((count, 128 * heads), bf16),
            jax.ShapeDtypeStruct((heads, 1, count), f32),
        ],
        scratch_shapes=[pltpu.VMEM((1, rows), f32), pltpu.VMEM((128, rows), f32), pltpu.VMEM((1, rows), f32)],
        compiler_params=params("attend"),
        cost_estimate=cost(heads * 8 * count * count * 128, 6e6, heads * count * count),
        name="attend",
    )(qkv, query_extra, keys_extra)


def mean_row(value):
    return jnp.sum(value, axis=1, keepdims=True) * (1.0 / value.shape[1])


def norm_rows(summed):
    centered = summed - mean_row(summed)
    inverse = lax.rsqrt(mean_row(centered * centered) + NORM_EPS)
    return centered * inverse, inverse


def norm_back(grad, normed, inverse):
    return inverse * (grad - mean_row(grad) - normed * mean_row(grad * normed))


def fold8(value):
    return jnp.sum(value.reshape(value.shape[0] // 8, 8, value.shape[1]), axis=0)


def middle_kernel(
    masks,
    order_in,
    order_out,
    rows,
    sub,
    me_ref,
    tokens,
    attended_a,
    attended_b,
    offset_a,
    offset_b,
    query_extra,
    cotangent,
    vec,
    *refs,
):
    pieces = refs[: len(masks)]
    layer_output, grad_branch_out, grad_attended_out, grad_extra, query_extra_out, keep, send, vec_out = refs[
        len(masks) : -8
    ]
    attn_weight, in_weight, out_weight, grad_attn, grad_in, grad_out, sums, hidden_sum = refs[-8:]
    step = pl.program_id(0)
    me = me_ref[0]
    half = BLOCKS // 2

    @pl.when(step == 0)
    def _():
        for mask, ref in zip(masks, pieces):

            def place(i, _, mask=mask, ref=ref):
                d = owner_of(i, jnp.bitwise_xor(me, mask), order_in)
                start = i * R_ROWS
                a_row = pl.multiple_of(d * 16, 16)
                o_row = pl.multiple_of(d * 32, 16)
                for j in range(4):
                    attn_weight[pl.ds(a_row, 16), 128 * j : 128 * (j + 1)] = ref[
                        pl.ds(pl.multiple_of(start + 16 * j, 16), 16), :
                    ]
                for j in range(8):
                    in_weight[pl.ds(a_row, 16), 128 * j : 128 * (j + 1)] = ref[
                        pl.ds(pl.multiple_of(start + 64 + 16 * j, 16), 16), :
                    ]
                for j in range(4):
                    out_weight[pl.ds(o_row, 32), 128 * j : 128 * (j + 1)] = ref[
                        pl.ds(pl.multiple_of(start + 192 + 32 * j, 16), 32), :
                    ]
                return 0

            lax.fori_loop(0, 1 << len(order_in), place, 0, unroll=True)
        grad_attn[...] = jnp.zeros_like(grad_attn)
        grad_in[...] = jnp.zeros_like(grad_in)
        grad_out[...] = jnp.zeros_like(grad_out)
        sums[...] = jnp.zeros_like(sums)
        hidden_sum[...] = jnp.zeros_like(hidden_sum)

    def row_of(index):
        return jnp.concatenate([vec[4 * index + j : 4 * index + j + 1, :] for j in range(4)], axis=1)

    attn_bias, ffn_bias, gain_one, shift_one, gain_two, shift_two = [row_of(i) for i in range(2, 8)]
    hidden_bias = jnp.concatenate([vec[32 + j : 33 + j, :] for j in range(8)], axis=1)

    first_row = pl.multiple_of(step * rows, rows)
    here = pl.ds(first_row, rows)
    parts = [offset_a[h, :, here] for h in range(3)] + [offset_b[0, :, here], jnp.zeros((4, rows), f32)]
    offsets = jnp.concatenate(parts, axis=0).T
    lane = lax.broadcasted_iota(jnp.int32, (rows, 128), 1)
    extra = query_extra[here, :].astype(f32)
    for h in range(HEADS):
        for i, part in enumerate(split3(-offsets[:, h : h + 1])):
            extra = jnp.where(lane == 16 + 4 * h + i, part.astype(f32), extra)
    query_extra_out[here, :] = extra.astype(bf16)

    kept = [{} for _ in range(rows // sub)]

    def chain(s):
        out = slice(s * sub, (s + 1) * sub)
        sl = pl.ds(pl.multiple_of(step * rows + s * sub, sub), sub)
        att = jnp.concatenate([attended_a[sl, :], attended_b[sl, :]], axis=1)
        branch = dot(att, attn_weight[...], NN) + attn_bias
        yield
        normed_one, inverse_one = norm_rows(tokens[sl, :].astype(f32) + branch)
        hidden = normed_one * gain_one + shift_one
        hidden_low = hidden.astype(bf16)
        yield
        pre_act = dot(hidden_low, in_weight[...], NN) + hidden_bias
        yield
        cdf = 0.5 * (1.0 + lax.erf(pre_act * 0.7071067811865476))
        density = jnp.exp(-0.5 * pre_act * pre_act) * 0.3989422804014327
        activated = (pre_act * cdf).astype(bf16)
        slope = cdf + pre_act * density
        yield
        ffn_result = dot(activated, out_weight[...], NN) + ffn_bias
        yield
        normed_two, inverse_two = norm_rows(hidden + ffn_result)
        layer_output[out, :] = (normed_two * gain_two + shift_two).astype(bf16)
        grad_result = cotangent[sl, :].astype(f32)
        sums[4] += fold8(grad_result * normed_two)
        sums[5] += fold8(grad_result)
        grad_second = norm_back(grad_result * gain_two, normed_two, inverse_two)
        grad_ffn = grad_second.astype(bf16)
        sums[1] += fold8(grad_ffn.astype(f32))
        yield
        grad_activated = dot(grad_ffn, out_weight[...], NT)
        kept[s][0] = (activated, grad_ffn)
        yield
        grad_pre = (grad_activated * slope).astype(bf16)
        hidden_sum[...] += fold8(grad_pre.astype(f32))
        yield
        grad_hidden = grad_second + dot(grad_pre, in_weight[...], NT)
        kept[s][1] = (hidden_low, grad_pre)
        yield
        sums[2] += fold8(grad_hidden * normed_one)
        sums[3] += fold8(grad_hidden)
        grad_first = norm_back(grad_hidden * gain_one, normed_one, inverse_one)
        grad_branch = grad_first.astype(bf16)
        grad_branch_out[sl, :] = grad_branch
        sums[0] += fold8(grad_branch.astype(f32))
        yield
        grad_attended = dot(grad_branch, attn_weight[...], NT)
        kept[s][2] = (att, grad_branch)
        yield
        low = grad_attended.astype(bf16)
        grad_attended_out[sl, :] = low
        lane = lax.broadcasted_iota(jnp.int32, (sub, 128), 1)
        extra = jnp.zeros((sub, 128), f32)
        for h in range(HEADS):
            cols = slice(128 * h, 128 * (h + 1))
            low_cols = low[:, cols].astype(f32)
            centre = jnp.sum(low_cols * att[:, cols].astype(f32), axis=1, keepdims=True)
            for i, part in enumerate(split3(-centre)):
                extra = jnp.where(lane == 4 * h + i, part.astype(f32), extra)
        grad_extra[sl, :] = extra.astype(bf16)
        yield

    chains = [chain(s) for s in range(rows // sub)]
    started = 0
    live = []
    while started < len(chains) or live:
        if started < len(chains):
            live.append(chains[started])
            started += 1
        remaining = []
        for c in live:
            try:
                next(c)
                remaining.append(c)
            except StopIteration:
                pass
        live = remaining
        for i, ref in enumerate((grad_out, grad_in, grad_attn)):
            if all(i in k for k in kept):
                left = jnp.concatenate([k[i][0] for k in kept], axis=0)
                right = jnp.concatenate([k.pop(i)[1] for k in kept], axis=0)
                ref[...] += dot(left, right, TN)

    @pl.when(step == pl.num_programs(0) - 1)
    def _():
        for base, ref in ((0, keep), (half, send)):

            def place(i, _, base=base, ref=ref):
                d = owner_of(base + i, me, order_out)
                start = i * R_ROWS
                a_row = pl.multiple_of(d * 16, 16)
                o_row = pl.multiple_of(d * 32, 16)
                for j in range(4):
                    ref[pl.ds(pl.multiple_of(start + 16 * j, 16), 16), :] = grad_attn[
                        pl.ds(a_row, 16), 128 * j : 128 * (j + 1)
                    ].astype(bf16)
                for j in range(8):
                    ref[pl.ds(pl.multiple_of(start + 64 + 16 * j, 16), 16), :] = grad_in[
                        pl.ds(a_row, 16), 128 * j : 128 * (j + 1)
                    ].astype(bf16)
                for j in range(4):
                    ref[pl.ds(pl.multiple_of(start + 192 + 32 * j, 16), 32), :] = grad_out[
                        pl.ds(o_row, 32), 128 * j : 128 * (j + 1)
                    ].astype(bf16)
                return 0

            lax.fori_loop(0, half, place, 0, unroll=True)
        vec_out[...] = jnp.zeros_like(vec_out)
        for i in range(6):
            row = jnp.sum(sums[i], axis=0, keepdims=True)
            for j in range(4):
                vec_out[8 + 4 * i + j : 9 + 4 * i + j, :] = row[:, 128 * j : 128 * (j + 1)]
        row = jnp.sum(hidden_sum[...], axis=0, keepdims=True)
        for j in range(8):
            vec_out[32 + j : 33 + j, :] = row[:, 128 * j : 128 * (j + 1)]


def middle(me, tokens, attended, offset, query_extra, cotangent, vec, pieces, masks, order_in, order_out, rows=512, sub=256):
    count = tokens.shape[0]
    half_rows = BLOCKS // 2 * R_ROWS
    return pl.pallas_call(
        functools.partial(middle_kernel, masks, order_in, order_out, rows, sub),
        grid=(count // rows,),
        in_specs=[scalar_spec()] + [resident() for _ in range(8 + len(pieces))],
        out_specs=[pl.BlockSpec((rows, 512), lambda i: (i, 0))] + [resident() for _ in range(7)],
        out_shape=[
            jax.ShapeDtypeStruct((count, 512), bf16),
            jax.ShapeDtypeStruct((count, 512), bf16),
            jax.ShapeDtypeStruct((count, 512), bf16),
            jax.ShapeDtypeStruct((count, 128), bf16),
            jax.ShapeDtypeStruct((count, 128), bf16),
            jax.ShapeDtypeStruct((half_rows, 128), bf16),
            jax.ShapeDtypeStruct((half_rows, 128), bf16),
            jax.ShapeDtypeStruct((48, 128), f32),
        ],
        scratch_shapes=[
            pltpu.VMEM((512, 512), bf16),
            pltpu.VMEM((512, FF), bf16),
            pltpu.VMEM((FF, 512), bf16),
            pltpu.VMEM((512, 512), f32),
            pltpu.VMEM((512, FF), f32),
            pltpu.VMEM((FF, 512), f32),
            pltpu.VMEM((6, 8, 512), f32),
            pltpu.VMEM((8, FF), f32),
        ],
        compiler_params=params("middle"),
        cost_estimate=cost(6 * count * 1310720, 22e6, 3 * count * FF),
        name="middle",
    )(me, tokens, *attended, *offset, query_extra, cotangent, vec, *pieces)


def attend_back_kernel(
    base,
    heads,
    width,
    order,
    vec_width,
    me_ref,
    tokens,
    qkv,
    grad_all,
    query_extra,
    keys_extra,
    grad_extra,
    vec_in,
    grad_query,
    grad_keys,
    grad_values,
    keep,
    send,
    vec,
    acc,
    all_keys,
    all_values,
    grad_weight,
):
    local = pl.program_id(0)
    step = pl.program_id(1)
    steps = pl.num_programs(1)
    last = base + heads == HEADS

    @pl.when((local == 0) & (step == 0))
    def _():
        vec[...] = vec_in[...]

    head = base + local
    keys = pl.ds(pl.multiple_of(step * width, width), width)

    def columns(first):
        return pl.ds(pl.multiple_of(128 * (first + head), 128), 128)

    q = qkv[:, columns(0)]
    k = qkv[keys, columns(HEADS)]
    v = qkv[keys, columns(2 * HEADS)]
    grad = grad_all[:, columns(0)]
    lane = lax.broadcasted_iota(jnp.int32, (width, 128), 1)
    ones = jnp.where((lane >= 4 * head) & (lane < 4 * head + 3), 1.0, 0.0).astype(bf16)
    extra = jnp.where(own_lanes(lane, head), keys_extra[keys, :].astype(f32), 0.0).astype(bf16)
    scores = dot(jnp.concatenate([q, query_extra[...]], axis=1), jnp.concatenate([k, extra], axis=1), NT)
    centred = dot(jnp.concatenate([grad, grad_extra[...]], axis=1), jnp.concatenate([v, ones], axis=1), NT)
    probs = jnp.exp(scores)
    probs_low = probs.astype(bf16)
    grad_scores = (probs * centred).astype(bf16)
    gv = dot(grad, probs_low, TN).astype(bf16)
    gk = dot(q, grad_scores, TN).astype(bf16)
    own_rows = pl.ds(pl.multiple_of(local * 128, 128), 128)
    grad_values[own_rows, keys] = gv
    grad_keys[own_rows, keys] = gk
    all_values[step] = gv
    all_keys[step] = gk
    part = dot(grad_scores, k, NN)

    @pl.when(step == 0)
    def _():
        acc[...] = part

    @pl.when(step > 0)
    def _():
        acc[...] += part

    @pl.when(step == steps - 1)
    def _():
        me = me_ref[0]
        scale = 1.0 / math.sqrt(HEAD_DIM)
        x = tokens[...]
        gq_all = acc[...].astype(bf16)
        grad_query[:, pl.ds(pl.multiple_of(local * 128, 128), 128)] = gq_all
        gk_all = jnp.concatenate([all_keys[i] for i in range(all_keys.shape[0])], axis=1)
        gv_all = jnp.concatenate([all_values[i] for i in range(all_values.shape[0])], axis=1)
        sums = dot(jnp.concatenate([gq_all.T, gk_all, gv_all], axis=0), x, NN)
        grad_weight[0:512, :] = (sums[0:128].T * scale).astype(bf16)
        grad_weight[512:1024, :] = sums[128:256].T.astype(bf16)
        grad_weight[1024:1536, :] = sums[256:384].T.astype(bf16)
        row_ones = jnp.ones((8, x.shape[0]), bf16)
        vec[pl.ds(base + local, 1), :] = dot(row_ones, gq_all, NN)[0:1] * scale
        vec[pl.ds(4 + base + local, 1), :] = dot(row_ones, gv_all, NT)[0:1]
        half = BLOCKS // 2
        block = heads * QKV_ROWS + (16 if last else 0)
        for start, ref in ((0, keep), (half, send)):

            def place(i, _, start=start, ref=ref):
                d = owner_of(start + i, me, order)
                ref[pl.ds(pl.multiple_of(i * block + local * QKV_ROWS, 16), QKV_ROWS), :] = grad_weight[
                    pl.ds(pl.multiple_of(d * QKV_ROWS, 16), QKV_ROWS), :
                ]
                if last:
                    pair = vec[pl.ds((d * vec_width) // 128, 2), :]
                    pair = jnp.concatenate([pair, jnp.zeros((14, 128), f32)], axis=0)
                    ref[pl.ds(pl.multiple_of(i * block + heads * QKV_ROWS, 16), 16), :] = pair.astype(bf16)
                return 0

            lax.fori_loop(0, half, place, 0, unroll=True)


def attend_back(
    me, tokens, qkv, grad_attended, query_extra, keys_extra, grad_extra, vec, order, vec_width, base, heads, width=512
):
    count = qkv.shape[0]
    half_rows = BLOCKS // 2 * (heads * QKV_ROWS + (16 if base + heads == HEADS else 0))
    return pl.pallas_call(
        functools.partial(attend_back_kernel, base, heads, width, order, vec_width),
        grid=(heads, count // width),
        in_specs=[scalar_spec()] + [resident() for _ in range(7)],
        out_specs=[resident() for _ in range(6)],
        out_shape=[
            jax.ShapeDtypeStruct((count, 128 * heads), bf16),
            jax.ShapeDtypeStruct((128 * heads, count), bf16),
            jax.ShapeDtypeStruct((128 * heads, count), bf16),
            jax.ShapeDtypeStruct((half_rows, 128), bf16),
            jax.ShapeDtypeStruct((half_rows, 128), bf16),
            jax.ShapeDtypeStruct((48, 128), f32),
        ],
        scratch_shapes=[
            pltpu.VMEM((count, 128), f32),
            pltpu.VMEM((count // width, 128, width), bf16),
            pltpu.VMEM((count // width, 128, width), bf16),
            pltpu.VMEM((1536, 128), bf16),
        ],
        compiler_params=params("attend_back"),
        cost_estimate=cost(heads * 20 * count * count * 128, heads * 12e6, heads * count * count),
        name="attend_back",
    )(me, tokens, qkv, grad_attended, query_extra, keys_extra, grad_extra, vec)


def input_grad_kernel(groups, rows, *refs):
    grad_branch = refs[0]
    queries, keys, values = [refs[1 + i * groups : 1 + (i + 1) * groups] for i in range(3)]
    weight, out = refs[-2], refs[-1]
    scale = 1.0 / math.sqrt(HEAD_DIM)
    here = pl.ds(pl.multiple_of(pl.program_id(0) * rows, rows), rows)
    gq = jnp.concatenate([r[here, :] for r in queries], axis=1)
    gk = jnp.concatenate([r[:, here] for r in keys], axis=0)
    gv = jnp.concatenate([r[:, here] for r in values], axis=0)
    total = grad_branch[here, :].astype(f32) + scale * dot(gq, weight[0:512, :], NT)
    total = total + dot(gk, weight[512:1024, :], TT)
    out[...] = total + dot(gv, weight[1024:1536, :], TT)


def input_grad(grad_branch, queries, keys, values, weight, rows=1024):
    count = grad_branch.shape[0]
    by_row = pl.BlockSpec((rows, 512), lambda i: (i, 0))
    return pl.pallas_call(
        functools.partial(input_grad_kernel, len(queries), rows),
        grid=(count // rows,),
        in_specs=[resident() for _ in range(2 + 3 * len(queries))],
        out_specs=by_row,
        out_shape=jax.ShapeDtypeStruct((count, 512), f32),
        compiler_params=params("input_grad"),
        cost_estimate=cost(2 * count * 512 * 1536, 16e6),
        name="input_grad",
    )(grad_branch, *queries, *keys, *values, weight)


def unpack_kernel(vec_width, me_ref, *refs):
    q_parts, r_parts = refs[:4], refs[4:6]
    out, vec_out, line = refs[6:]
    q_sum, r_sum = q_parts[0][...], r_parts[0][...]
    for part in q_parts[1:]:
        q_sum = q_sum + part[...].astype(f32)
    for part in r_parts[1:]:
        r_sum = r_sum + part[...].astype(f32)
    at = 0
    source = q_sum
    for index, (start, rows, count) in enumerate(PANELS):
        if index == 1:
            source, at = r_sum, 0
        for j in range(count):
            out[pl.ds(start + j, rows, stride=count), :] = source[at : at + rows, :]
            at += rows
    pair = jnp.concatenate([q_sum[192:200, :], q_sum[193:201, :]], axis=1)
    line[...] = pltpu.roll(pair, 256 - (me_ref[0] * vec_width) % 128, 1)
    vec_out[...] = line[0:1, 0:vec_width]


def unpack(me, q_parts, r_parts, vec_width):
    vmem = pl.BlockSpec(memory_space=pltpu.VMEM)
    return pl.pallas_call(
        functools.partial(unpack_kernel, vec_width),
        in_specs=[scalar_spec()] + [vmem] * 6,
        out_shape=[jax.ShapeDtypeStruct((512, 128), f32), jax.ShapeDtypeStruct((1, vec_width), f32)],
        scratch_shapes=[pltpu.VMEM((8, 256), f32)],
        compiler_params=params("unpack"),
        name="unpack",
    )(me, *q_parts, *r_parts)


def swap(array, step, count):
    return lax.ppermute(array, AXES, [(i, i ^ step) for i in range(count)])


def swap_each(parts, steps, count):
    pairs = list(zip(parts, steps))
    return [swap(part, step, count) for part, step in pairs[::-1]][::-1]


def after(value, *others):
    return lax.optimization_barrier((value, *others))[0]


def quarters(groups):
    parts = []
    for keep, got in groups:
        keep, got = keep.reshape(4, 4, -1, 128), got.reshape(4, 4, -1, 128)
        parts.append([keep[i].astype(f32) + got[i].astype(f32) for i in range(4)])
    totals = [jnp.concatenate(same, axis=1) if len(same) > 1 else same[0] for same in zip(*parts)]
    return totals[0], [total.astype(bf16).reshape(-1, 128) for total in totals[1:]]


def halves(keep, gots):
    total = keep
    for got in gots:
        total = total + got.astype(f32).reshape(keep.shape)
    half = total.shape[0] // 2
    return total[:half], total[half:].astype(bf16).reshape(-1, 128)


def fourths(keep, gots):
    total = keep
    for got in gots:
        total = total + got.astype(f32).reshape(keep.shape)
    return [total[0]] + [total[i].astype(bf16) for i in range(1, 4)]


def fast_layout(dp, fsdp):
    return dp == 4 and fsdp == 8


def gather_line(block, steps, count):
    return jnp.concatenate([block] + [swap(block, step, count) for step in steps], axis=0)


def body(dp, fsdp, tokens, lengths, assignment, weights, vectors, cotangent):
    count = dp * fsdp
    fast = fast_layout(dp, fsdp)
    owner = lax.axis_index(AXES).astype(jnp.int32)
    owned = assignment == owner
    ends = jnp.cumsum(jnp.where(owned, lengths, 0), dtype=jnp.int32)
    ends = jnp.where(owned, ends, 1 << 30)[None, :]
    if fast:
        vec_width = vectors.shape[0]
        core, x_step, y_step, z_near, z_far = fsdp, 1, 2 * fsdp, 2, 4
        planes = [x_step, y_step, x_step + y_step]
        spread = [x_step + y_step, y_step, x_step]
        line = [z_near, z_far, z_near + z_far]
        order_in, order_rest = [z_near, z_far], [z_far, z_near]
        order_out = [z_near, z_far, x_step, y_step, core]
        order_rest_out = order_rest + order_out[2:]
        masks = [0] + spread
        masks = masks + [m + core for m in masks]
        me = owner[None]
        q_block, r_block = pack(me, pltpu.with_memory_space_constraint(weights.reshape(512, 128), pltpu.HBM), pltpu.with_memory_space_constraint(vectors, pltpu.HBM), vec_width)
        lines = [swap(q_block, step, count) for step in line[::-1]][::-1]
        q_far = jnp.concatenate([q_block, lines[0], lines[1], after(lines[2], ends)], axis=0)
        q_core = swap(q_far, core, count)
        q_pieces = [q_far] + [swap(q_far, step, count) for step in spread]
        r_far = gather_line(after(r_block, q_core), [z_far], count)
        r_far = gather_line(r_far, [z_near], count)
        tokens = fetch(after(pltpu.with_memory_space_constraint(tokens, pltpu.HBM), q_far))
        q_pieces[3] = after(q_pieces[3], tokens)
        q_pieces[1] = after(q_pieces[1], r_far)
        q_pieces = q_pieces + [q_core] + [swap(piece, core, count) for piece in q_pieces[1:]]
        r_pieces = [swap(after(r_far, *q_pieces), step, count) for step in spread]
    else:
        vec_width = 160
        order_in, order_rest, order_out = [1, 2], [1, 2], [1, 2, 4, 8, 16]
        order_rest_out = order_out
        masks = [4 * i for i in range(8)]
        me = jnp.zeros((1,), jnp.int32)
        blocks = lax.all_gather(weights, AXES, axis=0, tiled=True).reshape(count, -1)
        flat = lax.all_gather(vectors, AXES, axis=0, tiled=True).reshape(40, 128)
        square = 512 * 512 // count
        cuts = [0, 3 * square, 4 * square, 6 * square, 8 * square]
        panels = []
        for index, (start, rows, width) in enumerate(PANELS):
            piece = blocks[:, cuts[index] : cuts[index + 1]].reshape(BLOCKS, rows, width, 128)
            panels.append(piece.transpose(0, 2, 1, 3).reshape(BLOCKS, rows * width, 128))
        spots = [(d * vec_width) // 128 for d in range(BLOCKS)]
        lanes = jnp.arange(256)
        vec_blocks = []
        for d in range(BLOCKS):
            pair = jnp.concatenate([flat, jnp.zeros((8, 128), bf16)], axis=0)[spots[d] : spots[d] + 2].reshape(256)
            offset = d * vec_width - 128 * spots[d]
            pair = jnp.where((lanes >= offset) & (lanes < offset + vec_width), pair, 0)
            vec_blocks.append(jnp.concatenate([pair.reshape(2, 128), jnp.zeros((14, 128), bf16)], axis=0))
        q_all = jnp.concatenate([panels[0], jnp.stack(vec_blocks)], axis=1)
        r_all = jnp.concatenate(panels[1:], axis=1)
        q_pieces = [q_all[4 * i : 4 * i + 4].reshape(-1, 128) for i in range(8)]
        r_pieces = [r_all[4 * i : 4 * i + 4].reshape(-1, 128) for i in range(8)]
    qkv, keys_extra, query_extra, vec, weight = project(
        me, ends, tokens, q_pieces, masks, order_in, vec_width
    )
    attended_a, offset_a = attend(qkv, query_extra, keys_extra, 0, 3)
    if fast:
        r_pieces = [r_far] + [after(piece, attended_a) for piece in r_pieces]
        keys_extra = after(keys_extra, *r_pieces)
        r_pieces = r_pieces + [swap(piece, core, count) for piece in r_pieces]
    attended_b, offset_b = attend(qkv, query_extra, keys_extra, 3, 1)
    layer_output, grad_branch, grad_attended, grad_extra, query_extra, r_keep, r_send, vec_grad = middle(
        me, tokens, (attended_a, attended_b), (offset_a, offset_b), query_extra, cotangent, vec, r_pieces, masks, order_rest, order_rest_out
    )
    queries, keys, values, keeps, sends, gots = [], [], [], [], [], []
    if fast:
        r_got = swap(r_send, core, count)
    for base, heads in ((0, 1), (1, 2), (3, 1)):
        gq, gk, gv, keep, send, vec_grad = attend_back(
            me,
            tokens,
            qkv,
            grad_attended,
            query_extra,
            keys_extra,
            grad_extra,
            vec_grad,
            order_out,
            vec_width,
            base,
            heads,
        )
        queries.append(gq)
        keys.append(gk)
        values.append(gv)
        keeps.append(keep)
        sends.append(send)
        if not fast:
            continue
        gots.append(swap(send, core, count))
        if base == 0:
            r_keep, r_sends = quarters([(r_keep, after(r_got, gq))])
            vec_grad = after(vec_grad, *r_sends)
            r_gots = swap_each(r_sends, planes, count)
        elif base == 1:
            r_gots = [after(part, gq) for part in r_gots]
            r_keep, r_send = halves(r_keep, r_gots)
            vec_grad = after(vec_grad, r_send)
            r_got = swap(r_send, z_near, count)
    if fast:
        r_keep, r_send = halves(r_keep, [after(r_got, gq)])
        gots = [after(got, gq) for got in gots]
        q_keep, q_sends = quarters(list(zip(keeps, gots)))
        grad_branch = after(grad_branch, *q_sends)
        q_gots = swap_each(q_sends, planes, count)
    grad_tokens = input_grad(grad_branch, queries, keys, values, weight)
    if fast:
        r_parts = [r_keep.reshape(-1, 128), swap(after(r_send, grad_tokens), z_far, count)]
        q_gots = [after(part, grad_tokens) for part in q_gots]
        q_parts = fourths(q_keep, q_gots)
        q_parts = q_parts[:1] + swap_each(q_parts[1:], line, count)
        own_weights, own_vectors = unpack(me, q_parts, r_parts, vec_width)
        own_weights = own_weights.reshape(-1)
        own_vectors = own_vectors.reshape(-1)
    else:
        heads = [jnp.concatenate([k, g], axis=0).astype(f32).reshape(BLOCKS, -1, 128) for k, g in zip(keeps, sends)]
        q_all = jnp.concatenate(heads, axis=1)
        r_all = jnp.concatenate([r_keep, r_send], axis=0).astype(f32).reshape(BLOCKS, R_ROWS, 128)
        sources = (q_all[:, : 4 * QKV_ROWS], r_all[:, :64], r_all[:, 64:192], r_all[:, 192:])
        pieces = []
        for source, (start, rows, width) in zip(sources, PANELS):
            piece = source.reshape(BLOCKS, width, rows, 128).transpose(0, 2, 1, 3)
            pieces.append(piece.reshape(count, -1))
        own_weights = lax.psum_scatter(
            jnp.concatenate(pieces, axis=1).reshape(-1), AXES, scatter_dimension=0, tiled=True
        )
        pairs = q_all[:, 4 * QKV_ROWS : 4 * QKV_ROWS + 2].reshape(BLOCKS, 256)
        rows = [
            pairs[d, (d * vec_width) % 128 : (d * vec_width) % 128 + vec_width] for d in range(BLOCKS)
        ]
        own_vectors = lax.psum_scatter(jnp.concatenate(rows), AXES, scatter_dimension=0, tiled=True)
    return (layer_output, grad_tokens, own_weights, own_vectors)


def solution(mesh):
    dp, fsdp = mesh.shape["dp"], mesh.shape["fsdp"]
    in_specs = (
        P(AXES, None),
        P(),
        P(),
        P(AXES),
        P(AXES),
        P(AXES, None),
    )
    out_specs = (
        P(AXES, None),
        P(AXES, None),
        P(AXES),
        P(AXES),
    )
    return jax.shard_map(
        functools.partial(body, dp, fsdp), mesh=mesh, in_specs=in_specs, out_specs=out_specs, check_vma=False
    )
```

```python
import functools
import math

import jax
import jax.numpy as jnp
from jax import lax
from jax.experimental import pallas as pl
from jax.experimental.pallas import tpu as pltpu
from jax.sharding import PartitionSpec as P

HEADS = 4
HEAD_DIM = 128
FF = 1024
AXES = ("dp", "fsdp")
NORM_EPS = 1e-05
BLOCKS = 32
QKV_ROWS = 48
Q_ROWS = 4 * QKV_ROWS + 16
R_ROWS = 320
FAR = -1e30
f32 = jnp.float32
bf16 = jnp.bfloat16
NT = (((1,), (1,)), ((), ()))
NN = (((1,), (0,)), ((), ()))
TN = (((0,), (0,)), ((), ()))
TT = (((0,), (1,)), ((), ()))
VMEM_MIB = {"pack": 2, "fetch": 4, "project": 22, "attend": 30, "middle": 26, "attend_back": 28, "input_grad": 14, "unpack": 3}


def dot(a, b, dims):
    return lax.dot_general(a, b, dims, preferred_element_type=f32)


def params(name):
    return pltpu.CompilerParams(vmem_limit_bytes=VMEM_MIB[name] << 20)


def cost(flops, moved, special=0):
    return pl.CostEstimate(flops=int(flops), bytes_accessed=int(moved), transcendentals=int(special))


def whole(shape):
    return pl.BlockSpec(shape, lambda *_: (0,) * len(shape))


def resident():
    return pl.BlockSpec(memory_space=pltpu.VMEM)


def scalar_spec():
    return pl.BlockSpec(memory_space=pltpu.SMEM)


def owner_of(place, me, order):
    mask = 0
    for bit, step in enumerate(order):
        mask = mask + ((place >> bit) & 1) * step
    return jnp.bitwise_xor(me, mask)


def split3(value):
    high = value.astype(bf16)
    rest = value - high.astype(f32)
    middle = rest.astype(bf16)
    low = (rest - middle.astype(f32)).astype(bf16)
    return high, middle, low


PANELS = ((0, 48, 4), (192, 16, 4), (256, 16, 8), (384, 32, 4))


def pack_kernel(vec_width, me_ref, flat, vec, q_out, r_out, wide, line):
    wide[...] = flat[...].astype(f32)
    line[...] = jnp.zeros_like(line)
    line[0:1, 0:vec_width] = vec[...].astype(f32).reshape(1, vec_width)
    shifted = pltpu.roll(line[...], (me_ref[0] * vec_width) % 128, 1)
    parts = []
    for start, rows, count in PANELS:
        for j in range(count):
            parts.append(wide[pl.ds(start + j, rows, stride=count), :].astype(bf16))
    q_out[0:192, :] = jnp.concatenate(parts[:4], axis=0)
    placed = jnp.concatenate([shifted[0:1, 0:128], shifted[0:1, 128:256], jnp.zeros((14, 128), f32)], axis=0)
    q_out[192:208, :] = placed.astype(bf16)
    r_out[...] = jnp.concatenate(parts[4:], axis=0)


def pack(me, flat, vec, vec_width):
    vmem = pl.BlockSpec(memory_space=pltpu.VMEM)
    return pl.pallas_call(
        functools.partial(pack_kernel, vec_width),
        in_specs=[scalar_spec(), vmem, vmem],
        out_shape=[
            jax.ShapeDtypeStruct((Q_ROWS, 128), bf16),
            jax.ShapeDtypeStruct((R_ROWS, 128), bf16),
        ],
        scratch_shapes=[pltpu.VMEM((512, 128), f32), pltpu.VMEM((8, 256), f32)],
        compiler_params=params("pack"),
        name="pack",
    )(me, flat, vec)


def fetch_kernel(source, ends, out, keys_extra, apart_out, sem):
    copy = pltpu.make_async_copy(source, out, sem)
    copy.start()
    count = out.shape[0]
    rows = 512

    def part(i, _):
        here = pl.ds(pl.multiple_of(i * rows, rows), rows)
        places = i * rows + lax.broadcasted_iota(jnp.int32, (rows, ends.shape[1]), 0)
        label = jnp.sum((ends[...] <= places).astype(f32), axis=1, keepdims=True)
        lane = lax.broadcasted_iota(jnp.int32, (rows, 128), 1)
        same = lane.astype(f32) == label
        ones = jnp.where(lane < 8, jnp.where(same, 1.0, 0.0), jnp.where(lane < 32, 1.0, 0.0))
        keys_extra[here, :] = ones.astype(bf16)
        apart_out[here, :] = jnp.where((lane < 8) & jnp.logical_not(same), FAR, 0.0).astype(bf16)
        return 0

    lax.fori_loop(0, count // rows, part, 0)
    copy.wait()


def fetch(array, ends):
    count = array.shape[0]
    return pl.pallas_call(
        fetch_kernel,
        in_specs=[pl.BlockSpec(memory_space=pl.ANY), resident()],
        out_specs=[resident() for _ in range(3)],
        out_shape=[
            jax.ShapeDtypeStruct(array.shape, array.dtype),
            jax.ShapeDtypeStruct((count, 128), bf16),
            jax.ShapeDtypeStruct((count, 128), bf16),
        ],
        scratch_shapes=[pltpu.SemaphoreType.DMA],
        compiler_params=params("fetch"),
        cost_estimate=cost(0, 6e6),
        name="fetch",
    )(array, ends)


def project_kernel(rows, masks, order, vec_width, me_ref, apart, tokens, *refs):
    pieces = refs[: len(masks)]
    qkv, query_extra, vec_out, weight, vec = refs[len(masks) :]
    step = pl.program_id(0)
    me = me_ref[0]

    @pl.when(step == 0)
    def _():
        vec[...] = jnp.zeros_like(vec)
        for mask, ref in zip(masks, pieces):
            for i in range(1 << len(order)):
                d = owner_of(i, jnp.bitwise_xor(me, mask), order)
                row = pl.multiple_of(d * QKV_ROWS, 16)
                for j in range(4):
                    at = i * Q_ROWS + QKV_ROWS * j
                    weight[pl.ds(row, QKV_ROWS), 128 * j : 128 * (j + 1)] = ref[at : at + QKV_ROWS, :]
                row = (d * vec_width) // 128
                at = i * Q_ROWS + 4 * QKV_ROWS
                vec[pl.ds(row, 2), :] = vec[pl.ds(row, 2), :] + ref[at : at + 16, :].astype(f32)[0:2, :]
        vec_out[...] = vec[...]

    here = pl.ds(pl.multiple_of(step * rows, rows), rows)
    x = tokens[here, :]
    scale = 1.0 / math.sqrt(HEAD_DIM)
    query_bias = jnp.concatenate([vec[j : j + 1, :] for j in range(4)], axis=1)
    value_bias = jnp.concatenate([vec[4 + j : 5 + j, :] for j in range(4)], axis=1)
    queries = ((dot(x, weight[0:512, :], NN) + query_bias) * scale).astype(bf16)
    key_heads = dot(x, weight[512:1024, :], NN).astype(bf16)
    values = (dot(x, weight[1024:1536, :], NN) + value_bias).astype(bf16)
    qkv[here, 0:512] = queries
    qkv[here, 512:1024] = key_heads
    qkv[here, 1024:1536] = values
    lane = lax.broadcasted_iota(jnp.int32, (rows, 128), 1)
    product = queries.astype(f32) * key_heads.astype(f32)
    extra = apart[here, :].astype(f32)
    for h in range(HEADS):
        own = jnp.sum(product[:, 128 * h : 128 * (h + 1)], axis=1, keepdims=True)
        extra = jnp.where(lane == 8 + h, -own, extra)
    query_extra[here, :] = extra.astype(bf16)


def project(me, apart, tokens, pieces, masks, order, vec_width, rows=1024):
    count = tokens.shape[0]
    return pl.pallas_call(
        functools.partial(project_kernel, rows, masks, order, vec_width),
        grid=(count // rows,),
        in_specs=[
            scalar_spec(),
            resident(),
            resident(),
        ]
        + [resident() for _ in pieces],
        out_specs=[resident() for _ in range(4)],
        out_shape=[
            jax.ShapeDtypeStruct((count, 1536), bf16),
            jax.ShapeDtypeStruct((count, 128), bf16),
            jax.ShapeDtypeStruct((48, 128), f32),
            jax.ShapeDtypeStruct((1536, 512), bf16),
        ],
        scratch_shapes=[pltpu.VMEM((48, 128), f32)],
        compiler_params=params("project"),
        cost_estimate=cost(2 * count * 512 * 1536, 12e6),
        name="project",
    )(me, apart, tokens, *pieces)


def own_lanes(lane, head):
    return (lane < 8) | (lane == 8 + head) | ((lane >= 16 + 4 * head) & (lane < 19 + 4 * head))


def attend_kernel(base, rows, qkv, query_extra, keys_extra, attended, offset_out, total, mixed, peak):
    local = pl.program_id(0)
    head = base + local
    start = pl.program_id(1) * rows
    here = pl.ds(pl.multiple_of(start, rows), rows)

    def columns(first):
        return pl.ds(pl.multiple_of(128 * (first + head), 128), 128)

    v = qkv[:, columns(2 * HEADS)]
    lane = lax.broadcasted_iota(jnp.int32, (rows, 128), 1)
    extra = jnp.where(own_lanes(lane, head), query_extra[here, :].astype(f32), 0.0).astype(bf16)
    left = jnp.concatenate([qkv[:, columns(HEADS)], keys_extra[...]], axis=1)
    right = jnp.concatenate([qkv[here, columns(0)], extra], axis=1)
    weights = jnp.exp(dot(left, right, NT))
    total[...] = jnp.sum(weights, axis=0, keepdims=True)
    mixed[...] = dot(v, weights.astype(bf16), TN)
    peak[...] = jnp.zeros_like(peak)
    good = (total[...] > 1e-20) & (total[...] < 1e30)

    @pl.when(jnp.sum(jnp.where(good, 0.0, 1.0)) > 0.0)
    def _():
        def part(j, _):
            place = pl.ds(pl.multiple_of(j * 128, 128), 128)
            some = pl.ds(pl.multiple_of(start + j * 128, 128), 128)
            lane = lax.broadcasted_iota(jnp.int32, (128, 128), 1)
            extra = jnp.where(own_lanes(lane, head), query_extra[some, :].astype(f32), 0.0).astype(bf16)
            again = dot(left, jnp.concatenate([qkv[some, columns(0)], extra], axis=1), NT)
            top = jnp.max(again, axis=0, keepdims=True)
            safe = jnp.exp(again - top)
            total[:, place] = jnp.sum(safe, axis=0, keepdims=True)
            mixed[:, place] = dot(v, safe.astype(bf16), TN)
            peak[:, place] = top
            return 0

        lax.fori_loop(0, rows // 128, part, 0)

    own = pl.ds(pl.multiple_of(128 * local, 128), 128)
    attended[here, own] = (mixed[...] * (1.0 / total[...])).T.astype(bf16)
    offset_out[local, :, here] = peak[...] + jnp.log(total[...])


def attend(qkv, query_extra, keys_extra, base, heads, rows=2048):
    count = qkv.shape[0]
    return pl.pallas_call(
        functools.partial(attend_kernel, base, rows),
        grid=(heads, count // rows),
        in_specs=[resident() for _ in range(3)],
        out_specs=[resident() for _ in range(2)],
        out_shape=[
            jax.ShapeDtypeStruct((count, 128 * heads), bf16),
            jax.ShapeDtypeStruct((heads, 1, count), f32),
        ],
        scratch_shapes=[pltpu.VMEM((1, rows), f32), pltpu.VMEM((128, rows), f32), pltpu.VMEM((1, rows), f32)],
        compiler_params=params("attend"),
        cost_estimate=cost(heads * 8 * count * count * 128, 6e6, heads * count * count),
        name="attend",
    )(qkv, query_extra, keys_extra)


def mean_row(value):
    return jnp.sum(value, axis=1, keepdims=True) * (1.0 / value.shape[1])


def norm_rows(summed):
    centered = summed - mean_row(summed)
    inverse = lax.rsqrt(mean_row(centered * centered) + NORM_EPS)
    return centered * inverse, inverse


def norm_back(grad, normed, inverse):
    return inverse * (grad - mean_row(grad) - normed * mean_row(grad * normed))


def fold8(value):
    return jnp.sum(value.reshape(value.shape[0] // 8, 8, value.shape[1]), axis=0)


def middle_kernel(
    masks,
    order_in,
    order_out,
    rows,
    sub,
    me_ref,
    tokens,
    attended_a,
    attended_b,
    offset_a,
    offset_b,
    query_extra,
    cotangent,
    vec,
    *refs,
):
    pieces = refs[: len(masks)]
    layer_output, grad_branch_out, grad_attended_out, grad_extra, query_extra_out, keep, send, vec_out = refs[
        len(masks) : -8
    ]
    attn_weight, in_weight, out_weight, grad_attn, grad_in, grad_out, sums, hidden_sum = refs[-8:]
    step = pl.program_id(0)
    me = me_ref[0]
    half = BLOCKS // 2

    @pl.when(step == 0)
    def _():
        for mask, ref in zip(masks, pieces):

            def place(i, _, mask=mask, ref=ref):
                d = owner_of(i, jnp.bitwise_xor(me, mask), order_in)
                start = i * R_ROWS
                a_row = pl.multiple_of(d * 16, 16)
                o_row = pl.multiple_of(d * 32, 16)
                for j in range(4):
                    attn_weight[pl.ds(a_row, 16), 128 * j : 128 * (j + 1)] = ref[
                        pl.ds(pl.multiple_of(start + 16 * j, 16), 16), :
                    ]
                for j in range(8):
                    in_weight[pl.ds(a_row, 16), 128 * j : 128 * (j + 1)] = ref[
                        pl.ds(pl.multiple_of(start + 64 + 16 * j, 16), 16), :
                    ]
                for j in range(4):
                    out_weight[pl.ds(o_row, 32), 128 * j : 128 * (j + 1)] = ref[
                        pl.ds(pl.multiple_of(start + 192 + 32 * j, 16), 32), :
                    ]
                return 0

            lax.fori_loop(0, 1 << len(order_in), place, 0, unroll=True)
        grad_attn[...] = jnp.zeros_like(grad_attn)
        grad_in[...] = jnp.zeros_like(grad_in)
        grad_out[...] = jnp.zeros_like(grad_out)
        sums[...] = jnp.zeros_like(sums)
        hidden_sum[...] = jnp.zeros_like(hidden_sum)

    def row_of(index):
        return jnp.concatenate([vec[4 * index + j : 4 * index + j + 1, :] for j in range(4)], axis=1)

    attn_bias, ffn_bias, gain_one, shift_one, gain_two, shift_two = [row_of(i) for i in range(2, 8)]
    hidden_bias = jnp.concatenate([vec[32 + j : 33 + j, :] for j in range(8)], axis=1)

    first_row = pl.multiple_of(step * rows, rows)
    here = pl.ds(first_row, rows)
    parts = [offset_a[h, :, here] for h in range(3)] + [offset_b[0, :, here], jnp.zeros((4, rows), f32)]
    offsets = jnp.concatenate(parts, axis=0).T
    lane = lax.broadcasted_iota(jnp.int32, (rows, 128), 1)
    extra = query_extra[here, :].astype(f32)
    for h in range(HEADS):
        for i, part in enumerate(split3(-offsets[:, h : h + 1])):
            extra = jnp.where(lane == 16 + 4 * h + i, part.astype(f32), extra)
    query_extra_out[here, :] = extra.astype(bf16)

    kept = [{} for _ in range(rows // sub)]

    def chain(s):
        out = slice(s * sub, (s + 1) * sub)
        sl = pl.ds(pl.multiple_of(step * rows + s * sub, sub), sub)
        att = jnp.concatenate([attended_a[sl, :], attended_b[sl, :]], axis=1)
        branch = dot(att, attn_weight[...], NN) + attn_bias
        yield
        normed_one, inverse_one = norm_rows(tokens[sl, :].astype(f32) + branch)
        hidden = normed_one * gain_one + shift_one
        hidden_low = hidden.astype(bf16)
        yield
        pre_act = dot(hidden_low, in_weight[...], NN) + hidden_bias
        yield
        cdf = 0.5 * (1.0 + lax.erf(pre_act * 0.7071067811865476))
        density = jnp.exp(-0.5 * pre_act * pre_act) * 0.3989422804014327
        activated = (pre_act * cdf).astype(bf16)
        slope = cdf + pre_act * density
        yield
        ffn_result = dot(activated, out_weight[...], NN) + ffn_bias
        yield
        normed_two, inverse_two = norm_rows(hidden + ffn_result)
        layer_output[out, :] = (normed_two * gain_two + shift_two).astype(bf16)
        grad_result = cotangent[sl, :].astype(f32)
        sums[4] += fold8(grad_result * normed_two)
        sums[5] += fold8(grad_result)
        grad_second = norm_back(grad_result * gain_two, normed_two, inverse_two)
        grad_ffn = grad_second.astype(bf16)
        sums[1] += fold8(grad_ffn.astype(f32))
        yield
        grad_activated = dot(grad_ffn, out_weight[...], NT)
        kept[s][0] = (activated, grad_ffn)
        yield
        grad_pre = (grad_activated * slope).astype(bf16)
        hidden_sum[...] += fold8(grad_pre.astype(f32))
        yield
        grad_hidden = grad_second + dot(grad_pre, in_weight[...], NT)
        kept[s][1] = (hidden_low, grad_pre)
        yield
        sums[2] += fold8(grad_hidden * normed_one)
        sums[3] += fold8(grad_hidden)
        grad_first = norm_back(grad_hidden * gain_one, normed_one, inverse_one)
        grad_branch = grad_first.astype(bf16)
        grad_branch_out[sl, :] = grad_branch
        sums[0] += fold8(grad_branch.astype(f32))
        yield
        grad_attended = dot(grad_branch, attn_weight[...], NT)
        kept[s][2] = (att, grad_branch)
        yield
        low = grad_attended.astype(bf16)
        grad_attended_out[sl, :] = low
        lane = lax.broadcasted_iota(jnp.int32, (sub, 128), 1)
        extra = jnp.zeros((sub, 128), f32)
        for h in range(HEADS):
            cols = slice(128 * h, 128 * (h + 1))
            low_cols = low[:, cols].astype(f32)
            centre = jnp.sum(low_cols * att[:, cols].astype(f32), axis=1, keepdims=True)
            for i, part in enumerate(split3(-centre)):
                extra = jnp.where(lane == 4 * h + i, part.astype(f32), extra)
        grad_extra[sl, :] = extra.astype(bf16)
        yield

    chains = [chain(s) for s in range(rows // sub)]
    started = 0
    live = []
    while started < len(chains) or live:
        if started < len(chains):
            live.append(chains[started])
            started += 1
        remaining = []
        for c in live:
            try:
                next(c)
                remaining.append(c)
            except StopIteration:
                pass
        live = remaining
        for i, ref in enumerate((grad_out, grad_in, grad_attn)):
            if all(i in k for k in kept):
                left = jnp.concatenate([k[i][0] for k in kept], axis=0)
                right = jnp.concatenate([k.pop(i)[1] for k in kept], axis=0)
                ref[...] += dot(left, right, TN)

    @pl.when(step == pl.num_programs(0) - 1)
    def _():
        for base, ref in ((0, keep), (half, send)):

            def place(i, _, base=base, ref=ref):
                d = owner_of(base + i, me, order_out)
                start = i * R_ROWS
                a_row = pl.multiple_of(d * 16, 16)
                o_row = pl.multiple_of(d * 32, 16)
                for j in range(4):
                    ref[pl.ds(pl.multiple_of(start + 16 * j, 16), 16), :] = grad_attn[
                        pl.ds(a_row, 16), 128 * j : 128 * (j + 1)
                    ].astype(bf16)
                for j in range(8):
                    ref[pl.ds(pl.multiple_of(start + 64 + 16 * j, 16), 16), :] = grad_in[
                        pl.ds(a_row, 16), 128 * j : 128 * (j + 1)
                    ].astype(bf16)
                for j in range(4):
                    ref[pl.ds(pl.multiple_of(start + 192 + 32 * j, 16), 32), :] = grad_out[
                        pl.ds(o_row, 32), 128 * j : 128 * (j + 1)
                    ].astype(bf16)
                return 0

            lax.fori_loop(0, half, place, 0, unroll=True)
        vec_out[...] = jnp.zeros_like(vec_out)
        for i in range(6):
            row = jnp.sum(sums[i], axis=0, keepdims=True)
            for j in range(4):
                vec_out[8 + 4 * i + j : 9 + 4 * i + j, :] = row[:, 128 * j : 128 * (j + 1)]
        row = jnp.sum(hidden_sum[...], axis=0, keepdims=True)
        for j in range(8):
            vec_out[32 + j : 33 + j, :] = row[:, 128 * j : 128 * (j + 1)]


def middle(me, tokens, attended, offset, query_extra, cotangent, vec, pieces, masks, order_in, order_out, rows=512, sub=256):
    count = tokens.shape[0]
    half_rows = BLOCKS // 2 * R_ROWS
    return pl.pallas_call(
        functools.partial(middle_kernel, masks, order_in, order_out, rows, sub),
        grid=(count // rows,),
        in_specs=[scalar_spec()] + [resident() for _ in range(8 + len(pieces))],
        out_specs=[pl.BlockSpec((rows, 512), lambda i: (i, 0))] + [resident() for _ in range(7)],
        out_shape=[
            jax.ShapeDtypeStruct((count, 512), bf16),
            jax.ShapeDtypeStruct((count, 512), bf16),
            jax.ShapeDtypeStruct((count, 512), bf16),
            jax.ShapeDtypeStruct((count, 128), bf16),
            jax.ShapeDtypeStruct((count, 128), bf16),
            jax.ShapeDtypeStruct((half_rows, 128), bf16),
            jax.ShapeDtypeStruct((half_rows, 128), bf16),
            jax.ShapeDtypeStruct((48, 128), f32),
        ],
        scratch_shapes=[
            pltpu.VMEM((512, 512), bf16),
            pltpu.VMEM((512, FF), bf16),
            pltpu.VMEM((FF, 512), bf16),
            pltpu.VMEM((512, 512), f32),
            pltpu.VMEM((512, FF), f32),
            pltpu.VMEM((FF, 512), f32),
            pltpu.VMEM((6, 8, 512), f32),
            pltpu.VMEM((8, FF), f32),
        ],
        compiler_params=params("middle"),
        cost_estimate=cost(6 * count * 1310720, 22e6, 3 * count * FF),
        name="middle",
    )(me, tokens, *attended, *offset, query_extra, cotangent, vec, *pieces)


def attend_back_kernel(
    base,
    heads,
    width,
    order,
    vec_width,
    me_ref,
    tokens,
    qkv,
    grad_all,
    query_extra,
    keys_extra,
    grad_extra,
    vec_in,
    grad_query,
    grad_keys,
    grad_values,
    keep,
    send,
    vec,
    acc,
    all_keys,
    all_values,
    grad_weight,
):
    local = pl.program_id(0)
    step = pl.program_id(1)
    steps = pl.num_programs(1)
    last = base + heads == HEADS

    @pl.when((local == 0) & (step == 0))
    def _():
        vec[...] = vec_in[...]

    head = base + local
    keys = pl.ds(pl.multiple_of(step * width, width), width)

    def columns(first):
        return pl.ds(pl.multiple_of(128 * (first + head), 128), 128)

    q = qkv[:, columns(0)]
    k = qkv[keys, columns(HEADS)]
    v = qkv[keys, columns(2 * HEADS)]
    grad = grad_all[:, columns(0)]
    lane = lax.broadcasted_iota(jnp.int32, (width, 128), 1)
    ones = jnp.where((lane >= 4 * head) & (lane < 4 * head + 3), 1.0, 0.0).astype(bf16)
    extra = jnp.where(own_lanes(lane, head), keys_extra[keys, :].astype(f32), 0.0).astype(bf16)
    scores = dot(jnp.concatenate([q, query_extra[...]], axis=1), jnp.concatenate([k, extra], axis=1), NT)
    centred = dot(jnp.concatenate([grad, grad_extra[...]], axis=1), jnp.concatenate([v, ones], axis=1), NT)
    probs = jnp.exp(scores)
    probs_low = probs.astype(bf16)
    grad_scores = (probs * centred).astype(bf16)
    gv = dot(grad, probs_low, TN).astype(bf16)
    gk = dot(q, grad_scores, TN).astype(bf16)
    own_rows = pl.ds(pl.multiple_of(local * 128, 128), 128)
    grad_values[own_rows, keys] = gv
    grad_keys[own_rows, keys] = gk
    all_values[step] = gv
    all_keys[step] = gk
    part = dot(grad_scores, k, NN)

    @pl.when(step == 0)
    def _():
        acc[...] = part

    @pl.when(step > 0)
    def _():
        acc[...] += part

    @pl.when(step == steps - 1)
    def _():
        me = me_ref[0]
        scale = 1.0 / math.sqrt(HEAD_DIM)
        x = tokens[...]
        gq_all = acc[...].astype(bf16)
        grad_query[:, pl.ds(pl.multiple_of(local * 128, 128), 128)] = gq_all
        gk_all = jnp.concatenate([all_keys[i] for i in range(all_keys.shape[0])], axis=1)
        gv_all = jnp.concatenate([all_values[i] for i in range(all_values.shape[0])], axis=1)
        sums = dot(jnp.concatenate([gq_all.T, gk_all, gv_all], axis=0), x, NN)
        grad_weight[0:512, :] = (sums[0:128].T * scale).astype(bf16)
        grad_weight[512:1024, :] = sums[128:256].T.astype(bf16)
        grad_weight[1024:1536, :] = sums[256:384].T.astype(bf16)
        row_ones = jnp.ones((8, x.shape[0]), bf16)
        vec[pl.ds(base + local, 1), :] = dot(row_ones, gq_all, NN)[0:1] * scale
        vec[pl.ds(4 + base + local, 1), :] = dot(row_ones, gv_all, NT)[0:1]
        half = BLOCKS // 2
        block = heads * QKV_ROWS + (16 if last else 0)
        for start, ref in ((0, keep), (half, send)):

            def place(i, _, start=start, ref=ref):
                d = owner_of(start + i, me, order)
                ref[pl.ds(pl.multiple_of(i * block + local * QKV_ROWS, 16), QKV_ROWS), :] = grad_weight[
                    pl.ds(pl.multiple_of(d * QKV_ROWS, 16), QKV_ROWS), :
                ]
                if last:
                    pair = vec[pl.ds((d * vec_width) // 128, 2), :]
                    pair = jnp.concatenate([pair, jnp.zeros((14, 128), f32)], axis=0)
                    ref[pl.ds(pl.multiple_of(i * block + heads * QKV_ROWS, 16), 16), :] = pair.astype(bf16)
                return 0

            lax.fori_loop(0, half, place, 0, unroll=True)


def attend_back(
    me, tokens, qkv, grad_attended, query_extra, keys_extra, grad_extra, vec, order, vec_width, base, heads, width=512
):
    count = qkv.shape[0]
    half_rows = BLOCKS // 2 * (heads * QKV_ROWS + (16 if base + heads == HEADS else 0))
    return pl.pallas_call(
        functools.partial(attend_back_kernel, base, heads, width, order, vec_width),
        grid=(heads, count // width),
        in_specs=[scalar_spec()] + [resident() for _ in range(7)],
        out_specs=[resident() for _ in range(6)],
        out_shape=[
            jax.ShapeDtypeStruct((count, 128 * heads), bf16),
            jax.ShapeDtypeStruct((128 * heads, count), bf16),
            jax.ShapeDtypeStruct((128 * heads, count), bf16),
            jax.ShapeDtypeStruct((half_rows, 128), bf16),
            jax.ShapeDtypeStruct((half_rows, 128), bf16),
            jax.ShapeDtypeStruct((48, 128), f32),
        ],
        scratch_shapes=[
            pltpu.VMEM((count, 128), f32),
            pltpu.VMEM((count // width, 128, width), bf16),
            pltpu.VMEM((count // width, 128, width), bf16),
            pltpu.VMEM((1536, 128), bf16),
        ],
        compiler_params=params("attend_back"),
        cost_estimate=cost(heads * 20 * count * count * 128, heads * 12e6, heads * count * count),
        name="attend_back",
    )(me, tokens, qkv, grad_attended, query_extra, keys_extra, grad_extra, vec)


def input_grad_kernel(groups, rows, *refs):
    grad_branch = refs[0]
    queries, keys, values = [refs[1 + i * groups : 1 + (i + 1) * groups] for i in range(3)]
    weight, out = refs[-2], refs[-1]
    scale = 1.0 / math.sqrt(HEAD_DIM)
    here = pl.ds(pl.multiple_of(pl.program_id(0) * rows, rows), rows)
    gq = jnp.concatenate([r[here, :] for r in queries], axis=1)
    gk = jnp.concatenate([r[:, here] for r in keys], axis=0)
    gv = jnp.concatenate([r[:, here] for r in values], axis=0)
    total = grad_branch[here, :].astype(f32) + scale * dot(gq, weight[0:512, :], NT)
    total = total + dot(gk, weight[512:1024, :], TT)
    out[...] = total + dot(gv, weight[1024:1536, :], TT)


def input_grad(grad_branch, queries, keys, values, weight, rows=1024):
    count = grad_branch.shape[0]
    by_row = pl.BlockSpec((rows, 512), lambda i: (i, 0))
    return pl.pallas_call(
        functools.partial(input_grad_kernel, len(queries), rows),
        grid=(count // rows,),
        in_specs=[resident() for _ in range(2 + 3 * len(queries))],
        out_specs=by_row,
        out_shape=jax.ShapeDtypeStruct((count, 512), f32),
        compiler_params=params("input_grad"),
        cost_estimate=cost(2 * count * 512 * 1536, 16e6),
        name="input_grad",
    )(grad_branch, *queries, *keys, *values, weight)


def unpack_kernel(vec_width, me_ref, *refs):
    q_parts, r_parts = refs[:4], refs[4:6]
    out, vec_out, line = refs[6:]
    q_sum, r_sum = q_parts[0][...], r_parts[0][...]
    for part in q_parts[1:]:
        q_sum = q_sum + part[...].astype(f32)
    for part in r_parts[1:]:
        r_sum = r_sum + part[...].astype(f32)
    at = 0
    source = q_sum
    for index, (start, rows, count) in enumerate(PANELS):
        if index == 1:
            source, at = r_sum, 0
        for j in range(count):
            out[pl.ds(start + j, rows, stride=count), :] = source[at : at + rows, :]
            at += rows
    pair = jnp.concatenate([q_sum[192:200, :], q_sum[193:201, :]], axis=1)
    line[...] = pltpu.roll(pair, 256 - (me_ref[0] * vec_width) % 128, 1)
    vec_out[...] = line[0:1, 0:vec_width]


def unpack(me, q_parts, r_parts, vec_width):
    vmem = pl.BlockSpec(memory_space=pltpu.VMEM)
    return pl.pallas_call(
        functools.partial(unpack_kernel, vec_width),
        in_specs=[scalar_spec()] + [vmem] * 6,
        out_shape=[jax.ShapeDtypeStruct((512, 128), f32), jax.ShapeDtypeStruct((1, vec_width), f32)],
        scratch_shapes=[pltpu.VMEM((8, 256), f32)],
        compiler_params=params("unpack"),
        name="unpack",
    )(me, *q_parts, *r_parts)


def swap(array, step, count):
    return lax.ppermute(array, AXES, [(i, i ^ step) for i in range(count)])


def swap_each(parts, steps, count):
    pairs = list(zip(parts, steps))
    return [swap(part, step, count) for part, step in pairs[::-1]][::-1]


def after(value, *others):
    return lax.optimization_barrier((value, *others))[0]


def quarters(groups):
    parts = []
    for keep, got in groups:
        keep, got = keep.reshape(4, 4, -1, 128), got.reshape(4, 4, -1, 128)
        parts.append([keep[i].astype(f32) + got[i].astype(f32) for i in range(4)])
    totals = [jnp.concatenate(same, axis=1) if len(same) > 1 else same[0] for same in zip(*parts)]
    return totals[0], [total.astype(bf16).reshape(-1, 128) for total in totals[1:]]


def halves(keep, gots):
    total = keep
    for got in gots:
        total = total + got.astype(f32).reshape(keep.shape)
    half = total.shape[0] // 2
    return total[:half], total[half:].astype(bf16).reshape(-1, 128)


def fourths(keep, gots):
    total = keep
    for got in gots:
        total = total + got.astype(f32).reshape(keep.shape)
    return [total[0]] + [total[i].astype(bf16) for i in range(1, 4)]


def fast_layout(dp, fsdp):
    return dp == 4 and fsdp == 8


def gather_line(block, steps, count):
    return jnp.concatenate([block] + [swap(block, step, count) for step in steps], axis=0)


def body(dp, fsdp, tokens, lengths, assignment, weights, vectors, cotangent):
    count = dp * fsdp
    fast = fast_layout(dp, fsdp)
    owner = lax.axis_index(AXES).astype(jnp.int32)
    owned = assignment == owner
    ends = jnp.cumsum(jnp.where(owned, lengths, 0), dtype=jnp.int32)
    ends = jnp.where(owned, ends, 1 << 30)[None, :]
    if fast:
        vec_width = vectors.shape[0]
        core, x_step, y_step, z_near, z_far = fsdp, 1, 2 * fsdp, 2, 4
        planes = [x_step, y_step, x_step + y_step]
        spread = [x_step + y_step, y_step, x_step]
        line = [z_near, z_far, z_near + z_far]
        order_in, order_rest = [z_near, z_far], [z_far, z_near]
        order_out = [z_near, z_far, x_step, y_step, core]
        order_rest_out = order_rest + order_out[2:]
        masks = [0] + spread
        masks = masks + [m + core for m in masks]
        me = owner[None]
        q_block, r_block = pack(me, pltpu.with_memory_space_constraint(weights.reshape(512, 128), pltpu.HBM), pltpu.with_memory_space_constraint(vectors, pltpu.HBM), vec_width)
        lines = [swap(q_block, step, count) for step in line[::-1]][::-1]
        q_far = jnp.concatenate([q_block, lines[0], lines[1], after(lines[2], ends)], axis=0)
        q_core = swap(q_far, core, count)
        q_pieces = [q_far] + [swap(q_far, step, count) for step in spread]
        r_far = gather_line(after(r_block, q_core), [z_far], count)
        r_far = gather_line(r_far, [z_near], count)
        tokens, keys_extra, apart = fetch(after(pltpu.with_memory_space_constraint(tokens, pltpu.HBM), q_far), ends)
        q_pieces[3] = after(q_pieces[3], tokens)
        q_pieces[1] = after(q_pieces[1], r_far)
        q_pieces = q_pieces + [q_core] + [swap(piece, core, count) for piece in q_pieces[1:]]
        r_pieces = [swap(after(r_far, *q_pieces), step, count) for step in spread]
    else:
        vec_width = 160
        order_in, order_rest, order_out = [1, 2], [1, 2], [1, 2, 4, 8, 16]
        tokens, keys_extra, apart = fetch(tokens, ends)
        order_rest_out = order_out
        masks = [4 * i for i in range(8)]
        me = jnp.zeros((1,), jnp.int32)
        blocks = lax.all_gather(weights, AXES, axis=0, tiled=True).reshape(count, -1)
        flat = lax.all_gather(vectors, AXES, axis=0, tiled=True).reshape(40, 128)
        square = 512 * 512 // count
        cuts = [0, 3 * square, 4 * square, 6 * square, 8 * square]
        panels = []
        for index, (start, rows, width) in enumerate(PANELS):
            piece = blocks[:, cuts[index] : cuts[index + 1]].reshape(BLOCKS, rows, width, 128)
            panels.append(piece.transpose(0, 2, 1, 3).reshape(BLOCKS, rows * width, 128))
        spots = [(d * vec_width) // 128 for d in range(BLOCKS)]
        lanes = jnp.arange(256)
        vec_blocks = []
        for d in range(BLOCKS):
            pair = jnp.concatenate([flat, jnp.zeros((8, 128), bf16)], axis=0)[spots[d] : spots[d] + 2].reshape(256)
            offset = d * vec_width - 128 * spots[d]
            pair = jnp.where((lanes >= offset) & (lanes < offset + vec_width), pair, 0)
            vec_blocks.append(jnp.concatenate([pair.reshape(2, 128), jnp.zeros((14, 128), bf16)], axis=0))
        q_all = jnp.concatenate([panels[0], jnp.stack(vec_blocks)], axis=1)
        r_all = jnp.concatenate(panels[1:], axis=1)
        q_pieces = [q_all[4 * i : 4 * i + 4].reshape(-1, 128) for i in range(8)]
        r_pieces = [r_all[4 * i : 4 * i + 4].reshape(-1, 128) for i in range(8)]
    qkv, query_extra, vec, weight = project(
        me, apart, tokens, q_pieces, masks, order_in, vec_width
    )
    attended_a, offset_a = attend(qkv, query_extra, keys_extra, 0, 3)
    if fast:
        r_pieces = [r_far] + [after(piece, attended_a) for piece in r_pieces]
        keys_extra = after(keys_extra, *r_pieces)
        r_pieces = r_pieces + [swap(piece, core, count) for piece in r_pieces]
    attended_b, offset_b = attend(qkv, query_extra, keys_extra, 3, 1)
    layer_output, grad_branch, grad_attended, grad_extra, query_extra, r_keep, r_send, vec_grad = middle(
        me, tokens, (attended_a, attended_b), (offset_a, offset_b), query_extra, cotangent, vec, r_pieces, masks, order_rest, order_rest_out
    )
    queries, keys, values, keeps, sends, gots = [], [], [], [], [], []
    if fast:
        r_got = swap(r_send, core, count)
    for base, heads in ((0, 1), (1, 2), (3, 1)):
        gq, gk, gv, keep, send, vec_grad = attend_back(
            me,
            tokens,
            qkv,
            grad_attended,
            query_extra,
            keys_extra,
            grad_extra,
            vec_grad,
            order_out,
            vec_width,
            base,
            heads,
        )
        queries.append(gq)
        keys.append(gk)
        values.append(gv)
        keeps.append(keep)
        sends.append(send)
        if not fast:
            continue
        gots.append(swap(send, core, count))
        if base == 0:
            r_keep, r_sends = quarters([(r_keep, after(r_got, gq))])
            vec_grad = after(vec_grad, *r_sends)
            r_gots = swap_each(r_sends, planes, count)
        elif base == 1:
            r_gots = [after(part, gq) for part in r_gots]
            r_keep, r_send = halves(r_keep, r_gots)
            vec_grad = after(vec_grad, r_send)
            r_got = swap(r_send, z_near, count)
    if fast:
        r_keep, r_send = halves(r_keep, [after(r_got, gq)])
        gots = [after(got, gq) for got in gots]
        q_keep, q_sends = quarters(list(zip(keeps, gots)))
        grad_branch = after(grad_branch, *q_sends)
        q_gots = swap_each(q_sends, planes, count)
    grad_tokens = input_grad(grad_branch, queries, keys, values, weight)
    if fast:
        r_parts = [r_keep.reshape(-1, 128), swap(after(r_send, grad_tokens), z_far, count)]
        q_gots = [after(part, grad_tokens) for part in q_gots]
        q_parts = fourths(q_keep, q_gots)
        q_parts = q_parts[:1] + swap_each(q_parts[1:], line, count)
        own_weights, own_vectors = unpack(me, q_parts, r_parts, vec_width)
        own_weights = own_weights.reshape(-1)
        own_vectors = own_vectors.reshape(-1)
    else:
        heads = [jnp.concatenate([k, g], axis=0).astype(f32).reshape(BLOCKS, -1, 128) for k, g in zip(keeps, sends)]
        q_all = jnp.concatenate(heads, axis=1)
        r_all = jnp.concatenate([r_keep, r_send], axis=0).astype(f32).reshape(BLOCKS, R_ROWS, 128)
        sources = (q_all[:, : 4 * QKV_ROWS], r_all[:, :64], r_all[:, 64:192], r_all[:, 192:])
        pieces = []
        for source, (start, rows, width) in zip(sources, PANELS):
            piece = source.reshape(BLOCKS, width, rows, 128).transpose(0, 2, 1, 3)
            pieces.append(piece.reshape(count, -1))
        own_weights = lax.psum_scatter(
            jnp.concatenate(pieces, axis=1).reshape(-1), AXES, scatter_dimension=0, tiled=True
        )
        pairs = q_all[:, 4 * QKV_ROWS : 4 * QKV_ROWS + 2].reshape(BLOCKS, 256)
        rows = [
            pairs[d, (d * vec_width) % 128 : (d * vec_width) % 128 + vec_width] for d in range(BLOCKS)
        ]
        own_vectors = lax.psum_scatter(jnp.concatenate(rows), AXES, scatter_dimension=0, tiled=True)
    return (layer_output, grad_tokens, own_weights, own_vectors)


def solution(mesh):
    dp, fsdp = mesh.shape["dp"], mesh.shape["fsdp"]
    in_specs = (
        P(AXES, None),
        P(),
        P(),
        P(AXES),
        P(AXES),
        P(AXES, None),
    )
    out_specs = (
        P(AXES, None),
        P(AXES, None),
        P(AXES),
        P(AXES),
    )
    return jax.shard_map(
        functools.partial(body, dp, fsdp), mesh=mesh, in_specs=in_specs, out_specs=out_specs, check_vma=False
    )
```
